128 devices in a mesh: lat: 8 (over z_hi, y), lon: 16 (over z_lo, x, core).
Axes of the slice: x: 4, y: 4, z: 4 (z_hi: 2, z_lo: 2; z = z_hi * 2 + z_lo), core: 2. Of those that a mesh axis runs over, the one named last changes fastest.
Arguments:
- stored_tiles: float32 [3456, 8, 8100], P(('lat', 'lon')), may hold values from -6 to 6
- stored_ids: int32 [3456], P(('lat', 'lon')), may hold values from -1 to 143, as said below
- wet_tiles: int32 [24, 48], P('lat', 'lon'), may hold values from 0 to 1, as said below
- control_map: int32 [24, 48], P('lat', 'lon'), may hold values from 0 to 127, as said below
- zonal_diffusivity: float32 [2160, 4320], P('lat', 'lon'), may hold values from 0.05 to 0.18
- meridional_diffusivity: float32 [2160, 4320], P('lat', 'lon'), may hold values from 0.05 to 0.18
- zonal_flow: float32 [2160, 4320], P('lat', 'lon'), may hold values from -0.1 to 0.1
- meridional_flow: float32 [2160, 4320], P('lat', 'lon'), may hold values from -0.1 to 0.1
- vertical_mixing: float32 [2160, 4320], P('lat', 'lon'), may hold values from 0.02 to 0.1
- forcing: float32 [2, 2160, 4320], P(None, 'lat', 'lon'), may hold values from -4 to 4
- final_adjoint: float32 [2, 4, 2160, 4320], P(None, None, 'lat', 'lon'), may hold values from -6 to 6
Outputs:
- final_state: float32 [2, 4, 2160, 4320], P(None, None, 'lat', 'lon')
- initial_adjoint: float32 [2, 4, 2160, 4320], P(None, None, 'lat', 'lon')
- control_adjoint: float32 [128, 2, 900], P(('lat', 'lon'))
The draws below stay inside these ranges and needn't reach their ends.
Inputs may be any that keep to these rules, and one draw needn't show every extreme that they name: `stored_ids`: entry -1 marks an empty slot; any other entry r * 48 + c names the wet tile in row r of the storing device's band of 3 tile rows and tile column c. Each wet tile of a band stands in exactly one slot of one device of that band. One device's slots name at most 2 tiles whose columns lie in one compute owner's 3 columns, and some device has exactly 2; in every band one device uses all 27 slots. `wet_tiles`: the wet tiles are exactly those named in stored_ids. `control_map`: the 3 x 3 tiles of one device name different control tiles.
All inputs are finite; a program needn't handle non-finite values.
Results may differ from the reference program's by a relative error of at most 0.000096.
Values sent between devices are 32-bit elements; how exact they have to be, the bound alone decides.
No kernel may reach another device: no remote copies, remote signals or barrier semaphores. Data moves between devices by JAX's collectives and lax.ppermute only.
A program may use at most 192 MiB of HBM per device.

```python
import math
import jax
import jax.numpy as jnp
import numpy as np

TILE = 90
TLAT = 3
TLON = 3
LEV = 4
STEPS = 3
COARSE = 3
SLOTS = 27
CELLS = 8100
NTY = 24
NTX = 48
NY = 2160
NX = 4320
NCTRL = 128
N_LAT = 8
N_LON = 16


def wet_layout(key):
    base_key = jax.random.fold_in(key, 11)
    key_wet, key_perm, key_order = jax.random.split(base_key, 3)
    wet_table = (jax.random.randint(key_wet, (NTY, NTX), 0, 100) < 80).astype(jnp.int32)
    count = N_LON
    band_tiles = TLAT * TLON * count
    extra_total = band_tiles - SLOTS - 3 * (count - 1)
    steps_np = np.arange(1, count)
    cumul = extra_total * steps_np * steps_np // ((count - 1) * (count - 1))
    before = np.concatenate([np.zeros(1, np.int64), cumul[:-1]])
    quotas = np.concatenate([np.array([SLOTS]), 3 + cumul - before]).astype(np.int64)
    starts = np.concatenate([np.zeros(1, np.int64), np.cumsum(quotas)[:-1]])
    rank_np = np.repeat(np.arange(count), quotas)
    order_np = np.arange(band_tiles)
    within_np = order_np - starts[rank_np]
    position = order_np // count
    owner = order_np % count
    local_row = jnp.asarray(position // TLON, jnp.int32)
    tile_col = jnp.asarray(owner * TLON + position % TLON, jnp.int32)
    bands = jnp.arange(N_LAT, dtype=jnp.int32)
    global_row = bands[:, None] * TLAT + local_row[None, :]
    col_all = jnp.broadcast_to(tile_col[None, :], (N_LAT, band_tiles))
    heavy = jnp.asarray(rank_np == 0)
    heavy_rows = jnp.where(heavy[None, :], global_row, NTY)
    wet_table = wet_table.at[heavy_rows, col_all].set(1, mode='drop')
    wet_table = wet_table.at[TLAT - 1, NTX - 1].set(1)
    perms = jax.vmap(lambda subkey: jax.random.permutation(subkey, count))(jax.random.split(key_perm, N_LAT)).astype(jnp.int32)
    storer = perms[:, jnp.asarray(rank_np, jnp.int32)]
    present = wet_table[global_row, col_all]
    tile_ids = jnp.where(present == 1, local_row[None, :] * NTX + tile_col[None, :], -1).astype(jnp.int32)
    band_grid = jnp.broadcast_to(bands[:, None], (N_LAT, band_tiles))
    within = jnp.broadcast_to(jnp.asarray(within_np, jnp.int32)[None, :], (N_LAT, band_tiles))
    slot_ids = jnp.full((N_LAT, count, SLOTS), -1, jnp.int32).at[band_grid, storer, within].set(tile_ids)
    orders = jax.vmap(lambda subkey: jax.random.permutation(subkey, SLOTS))(jax.random.split(key_order, N_LAT * count)).reshape(N_LAT, count, SLOTS)
    slot_ids = jnp.take_along_axis(slot_ids, orders, axis=2)
    return (wet_table.astype(jnp.int32), slot_ids.reshape(-1).astype(jnp.int32))


def draw_stored_ids(key, part):
    return wet_layout(key)[1]


def draw_wet_tiles(key, part):
    return wet_layout(key)[0]


def draw_control_map(key, part):
    base_key = jax.random.fold_in(key, 23)
    device_total = N_LAT * N_LON
    perms = jax.vmap(lambda subkey: jax.random.permutation(subkey, NCTRL))(jax.random.split(base_key, device_total)).astype(jnp.int32)
    picked = perms[:, :TLAT * TLON]
    device = jnp.arange(device_total, dtype=jnp.int32)
    offset = jnp.where(device == device_total - 1, NCTRL - 1 - picked[:, 0], jnp.where(device == 0, -picked[:, 1], 0))
    labels = (picked + offset[:, None]) % NCTRL
    return labels.reshape(N_LAT, N_LON, TLAT, TLON).transpose(0, 2, 1, 3).reshape(NTY, NTX).astype(jnp.int32)


def steps_of(rng, extent, cuts, least, largest):
    loudness, own = 1.0, jax.random.fold_in(rng, 6)
    for dim, shards_of in cuts:
        heights = jnp.exp(jax.random.uniform(jax.random.fold_in(own, dim), (shards_of,), jnp.float32, least / len(cuts), largest / len(cuts)))
        loudness = loudness * jnp.repeat(heights, extent[dim] // shards_of).reshape([-1 if axis == dim else 1 for axis in range(len(extent))])
    return loudness


def normal_values(key, shape, deviation, most, shards=(), held_as=jnp.bfloat16):
    factor_of = steps_of(key, shape, shards, -0.22, 0.18) if shards else 1.0
    entries = jax.random.normal(key, shape, jnp.float32) * deviation * factor_of
    return jnp.minimum(jnp.maximum(entries, -most), most).astype(held_as)


def setup_inputs(seed: int = 0) -> dict:
    arg_keys = jax.random.split(jax.random.key(seed), 12)
    stored_tiles = normal_values(arg_keys[0], (N_LAT * N_LON * SLOTS, 2 * LEV, CELLS), 1.0, 6.0, ((0, 128),), jnp.float32)
    stored_ids = draw_stored_ids(jax.random.fold_in(arg_keys[11], 71), 0)
    wet_tiles = draw_wet_tiles(jax.random.fold_in(arg_keys[11], 71), 0)
    control_map = draw_control_map(jax.random.fold_in(arg_keys[11], 71), 0)
    zonal_diffusivity = jnp.clip(jnp.exp(math.log(0.18) - 1.2809339 * jax.random.uniform(arg_keys[4], (NY, NX), jnp.float32) ** steps_of(arg_keys[4], (NY, NX), ((0, 8), (1, 16)), -0.2, 0.2)), 0.05, 0.18)
    meridional_diffusivity = jnp.clip(jnp.exp(math.log(0.18) - 1.2809339 * jax.random.uniform(arg_keys[5], (NY, NX), jnp.float32) ** steps_of(arg_keys[5], (NY, NX), ((0, 8), (1, 16)), -0.2, 0.2)), 0.05, 0.18)
    zonal_flow = jnp.clip(jax.random.uniform(arg_keys[6], (NY, NX), jnp.float32, -0.1, 0.1) * steps_of(arg_keys[6], (NY, NX), ((0, 8), (1, 16)), -0.4, 0.0), -0.1, 0.1)
    meridional_flow = jnp.clip(jax.random.uniform(arg_keys[7], (NY, NX), jnp.float32, -0.1, 0.1) * steps_of(arg_keys[7], (NY, NX), ((0, 8), (1, 16)), -0.4, 0.0), -0.1, 0.1)
    vertical_mixing = jnp.clip(jnp.exp(math.log(0.1) - 1.609438 * jax.random.uniform(arg_keys[8], (NY, NX), jnp.float32) ** steps_of(arg_keys[8], (NY, NX), ((0, 8), (1, 16)), -0.2, 0.2)), 0.02, 0.1)
    forcing = normal_values(arg_keys[9], (2, NY, NX), 0.3, 4.0, ((1, 8), (2, 16)), jnp.float32)
    final_adjoint = normal_values(arg_keys[10], (2, LEV, NY, NX), 0.5, 6.0, ((2, 8), (3, 16)), jnp.float32)
    return dict(stored_tiles=stored_tiles, stored_ids=stored_ids, wet_tiles=wet_tiles, control_map=control_map, zonal_diffusivity=zonal_diffusivity, meridional_diffusivity=meridional_diffusivity, zonal_flow=zonal_flow, meridional_flow=meridional_flow, vertical_mixing=vertical_mixing, forcing=forcing, final_adjoint=final_adjoint)


def shift_north(field):
    return jnp.concatenate([field[..., 1:, :], jnp.zeros_like(field[..., :1, :])], axis=-2)


def shift_south(field):
    return jnp.concatenate([jnp.zeros_like(field[..., :1, :]), field[..., :-1, :]], axis=-2)


def vertical(field, mixing):
    flux = mixing * (field[:, :-1] - field[:, 1:])
    edge = jnp.zeros_like(field[:, :1])
    return jnp.concatenate([edge, flux], axis=1) - jnp.concatenate([flux, edge], axis=1)


def reference(stored_tiles, stored_ids, wet_tiles, control_map, zonal_diffusivity, meridional_diffusivity, zonal_flow, meridional_flow, vertical_mixing, forcing, final_adjoint):
    wet_cells = jnp.repeat(jnp.repeat(wet_tiles.astype(jnp.float32), TILE, axis=0), TILE, axis=1)
    per_band = stored_ids.shape[0] // N_LAT
    band_index = (jnp.arange(stored_ids.shape[0], dtype=jnp.int32) // per_band).astype(jnp.int32)
    target = jnp.where(stored_ids >= 0, band_index * (TLAT * NTX) + stored_ids, NTY * NTX).astype(jnp.int32)
    tile_data = jnp.zeros((NTY * NTX, 2 * LEV, TILE * TILE), jnp.float32).at[target].set(stored_tiles, mode="drop")
    ocean_state = tile_data.reshape(NTY, NTX, 2, LEV, TILE, TILE).transpose(2, 3, 0, 4, 1, 5).reshape(2, LEV, NY, NX) * wet_cells
    east_open = wet_cells * jnp.roll(wet_cells, -1, axis=1)
    north_open = wet_cells * shift_north(wet_cells)
    east_diff = zonal_diffusivity * east_open
    east_adv = 0.5 * zonal_flow * east_open
    north_diff = meridional_diffusivity * north_open
    north_adv = 0.5 * meridional_flow * north_open
    mixing = vertical_mixing * wet_cells

    def forward_change(field):
        east_val = jnp.roll(field, -1, axis=-1)
        east_flux = east_diff * (field - east_val) + east_adv * (field + east_val)
        north_val = shift_north(field)
        north_flux = north_diff * (field - north_val) + north_adv * (field + north_val)
        return (jnp.roll(east_flux, 1, axis=-1) - east_flux) + (shift_south(north_flux) - north_flux) + vertical(field, mixing)

    def backward_change(field):
        east_step = jnp.roll(field, -1, axis=-1) - field
        north_step = shift_north(field) - field
        zonal_part = (east_diff + east_adv) * east_step + jnp.roll((east_adv - east_diff) * east_step, 1, axis=-1)
        merid_part = (north_diff + north_adv) * north_step + shift_south((north_adv - north_diff) * north_step)
        return zonal_part + merid_part + vertical(field, mixing)

    forcing_wet = forcing * wet_cells
    for _ in range(STEPS):
        ocean_state = ocean_state + forward_change(ocean_state)
        ocean_state = ocean_state.at[:, 0].add(forcing_wet)
    adjoint_field = final_adjoint
    surface = jnp.zeros((2, NY, NX), jnp.float32)
    for _ in range(STEPS):
        surface = surface + wet_cells * adjoint_field[:, 0]
        adjoint_field = adjoint_field + backward_change(adjoint_field)
    coarse_side = TILE // COARSE
    coarse_field = surface.reshape(2, NTY, coarse_side, COARSE, NTX, coarse_side, COARSE).mean(axis=(3, 6))
    blocks = coarse_field.transpose(1, 3, 0, 2, 4).reshape(NTY * NTX, 2, coarse_side * coarse_side)
    control = jax.ops.segment_sum(blocks, control_map.reshape(-1).astype(jnp.int32), num_segments=NCTRL)
    return ocean_state, wet_cells * adjoint_field, control
```

```python
import jax
import jax.numpy as jnp
from jax import lax
from jax.experimental import pallas as pl
from jax.experimental.pallas import tpu as pltpu
from jax.sharding import PartitionSpec as P

F32 = jnp.float32
I32 = jnp.int32
TILE = 90
SIDE = 3
COLUMNS = 48
HALO = 3
STEPS = 3
SLOTS = 27
PAIR = 2
LEV = 4
CELLS = TILE * TILE
N = TILE * SIDE
FLAT = 8192
TAIL = 8064
TAG = CELLS - TAIL
TOP = 16
ROWS = 296
LANES = 384
CHUNKS = 34
COARSE = 30
VMEM = pl.BlockSpec(memory_space=pltpu.VMEM)
SMEM = pl.BlockSpec(memory_space=pltpu.SMEM)
ANY = pl.BlockSpec(memory_space=pl.ANY)


def aligned(x):
    return pl.multiple_of(x, 8)


def pack_kernel(ids, stored, after, out, held, tail, empty, count, route, in_sem, out_sem, tail_sem, empty_sem):
    owners = out.shape[0]

    def fetch(s):
        return pltpu.make_async_copy(stored.at[s], held.at[s], in_sem.at[s])

    def send(s, owner, rank):
        return pltpu.make_async_copy(
            held.at[s, :, pl.ds(0, TAIL)], out.at[owner, rank, :, pl.ds(0, TAIL)], out_sem.at[s]
        )

    def send_tail(s, owner, rank):
        return pltpu.make_async_copy(
            tail.at[s], out.at[owner, rank, :, pl.ds(TAIL, 128)], tail_sem.at[s]
        )

    def send_empty(owner, rank):
        return pltpu.make_async_copy(
            empty, out.at[owner, rank, :, pl.ds(TAIL, 128)], empty_sem.at[owner, rank]
        )

    @pl.loop(0, SLOTS)
    def _(s):
        @pl.when(ids[s] >= 0)
        def _():
            fetch(s).start()

    @pl.loop(0, owners)
    def _(o):
        count[o] = 0

    empty[...] = jnp.full((8, 128), -1.0, F32)
    lane = lax.broadcasted_iota(I32, (8, 128), 1)

    @pl.loop(0, SLOTS)
    def _(s):
        tile = ids[s]

        @pl.when(tile >= 0)
        def _():
            row = tile // COLUMNS
            column = tile - row * COLUMNS
            owner = column // SIDE
            rank = count[owner]
            count[owner] = rank + 1
            route[s] = owner * PAIR + rank
            place = row * SIDE + column - owner * SIDE
            fetch(s).wait()
            last = jnp.concatenate([held[s, :, TAIL:CELLS], jnp.zeros((8, 128 - TAG), F32)], axis=1)
            tail[s] = jnp.where(lane < TAG, last, place.astype(F32))
            send(s, owner, rank).start()
            send_tail(s, owner, rank).start()

    for rank in range(PAIR):

        @pl.loop(0, owners)
        def _(o):
            @pl.when(count[o] <= rank)
            def _():
                send_empty(o, rank).start()

    @pl.loop(0, SLOTS)
    def _(s):
        @pl.when(ids[s] >= 0)
        def _():
            owner = route[s] // PAIR
            rank = route[s] - owner * PAIR
            send(s, owner, rank).wait()
            send_tail(s, owner, rank).wait()

    for rank in range(PAIR):

        @pl.loop(0, owners)
        def _(o):
            @pl.when(count[o] <= rank)
            def _():
                send_empty(o, rank).wait()


def pack_tiles(ids, stored, after, owners):
    return pl.pallas_call(
        pack_kernel,
        out_shape=jax.ShapeDtypeStruct((owners, PAIR, 8, FLAT), F32),
        in_specs=[SMEM, ANY, ANY],
        out_specs=ANY,
        scratch_shapes=[
            pltpu.VMEM((SLOTS, 8, CELLS), F32),
            pltpu.VMEM((SLOTS, 8, 128), F32),
            pltpu.VMEM((8, 128), F32),
            pltpu.SMEM((owners,), I32),
            pltpu.SMEM((SLOTS,), I32),
            pltpu.SemaphoreType.DMA((SLOTS,)),
            pltpu.SemaphoreType.DMA((SLOTS,)),
            pltpu.SemaphoreType.DMA((SLOTS,)),
            pltpu.SemaphoreType.DMA((owners, PAIR)),
        ],
        name="pack_tiles",
    )(ids, stored, after)


def strip_columns(load, count, first):
    lane = lax.broadcasted_iota(I32, (N + 2, 128), 1)
    strip = jnp.zeros((N + 2, 128), F32)
    for f in range(count):
        moved = pltpu.roll(load(f), (HALO * f - first) % 128, 1)
        strip = jnp.where((lane >= HALO * f) & (lane < HALO * f + HALO), moved, strip)
    return strip.T[0 : HALO * count]


def wet_field(wet, rows, row0):
    row = lax.broadcasted_iota(I32, (rows, LANES), 0) + row0
    lane = lax.broadcasted_iota(I32, (rows, LANES), 1)
    bands = []
    for r in range(SIDE):
        w = [wet[r, c].astype(F32) for c in range(SIDE)]
        bands.append(jnp.where(lane < TILE, w[0], jnp.where(lane < 2 * TILE, w[1], w[2])))
    return jnp.where(row < TILE, bands[0], jnp.where(row < 2 * TILE, bands[1], bands[2]))


def edges_kernel(wet, zd, zf, md, mf, vm, forcing, adjoint, west, east, south, north, held):
    views = [zd, zf, md, mf, vm]

    def plane(f):
        if f < 6:
            return views[f - 1]
        if f < 8:
            return forcing.at[f - 6]
        return adjoint.at[(f - 8) // LEV, (f - 8) % LEV]

    full = wet_field(wet, N + 2, 0)
    held[0] = full[:, 0:128]
    held[1] = full[:, 256:384]
    south[0:HALO, 0:N] = full[0:HALO, 0:N]
    north[0:HALO, 0:N] = full[N - HALO : N, 0:N]
    for f in range(1, 16):
        ref = plane(f)
        south[HALO * f : HALO * f + HALO, 0:N] = ref[0:HALO, :]
        north[HALO * f : HALO * f + HALO, 0:N] = ref[N - HALO : N, :]

    def low(f):
        if f == 0:
            return held[0]
        return jnp.concatenate([plane(f)[:, 0:128], jnp.zeros((2, 128), F32)], axis=0)

    def high(f):
        if f == 0:
            return held[1]
        part = jnp.concatenate([plane(f)[:, 256:N], jnp.zeros((N, LANES - N), F32)], axis=1)
        return jnp.concatenate([part, jnp.zeros((2, 128), F32)], axis=0)

    west[...] = strip_columns(low, 16, 0)
    east[...] = strip_columns(high, 16, N - HALO - 256)


def edge_strips(wet, zd, zf, md, mf, vm, forcing, adjoint):
    columns = jax.ShapeDtypeStruct((48, N + 2), F32)
    rows = jax.ShapeDtypeStruct((48, N + 2), F32)
    return pl.pallas_call(
        edges_kernel,
        out_shape=(columns, columns, rows, rows),
        in_specs=[SMEM] + [VMEM] * 7,
        out_specs=(VMEM,) * 4,
        scratch_shapes=[pltpu.VMEM((2, N + 2, 128), F32)],
        name="edge_strips",
    )(wet, zd, zf, md, mf, vm, forcing, adjoint)


def corners_kernel(south, north, west, east, to_south, to_north):
    for rows, out, first in ((south, to_south, 0), (north, to_north, N - HALO)):
        out[:, 0:N] = rows[:, 0:N]
        out[:, N : N + HALO] = west[:, first : first + HALO]
        out[:, N + HALO : N + 2 * HALO] = east[:, first : first + HALO]


def with_corners(south, north, west, east):
    shape = jax.ShapeDtypeStruct((south.shape[0], LANES), F32)
    return pl.pallas_call(
        corners_kernel,
        out_shape=(shape, shape),
        in_specs=[VMEM] * 4,
        out_specs=(VMEM,) * 2,
        name="row_strips",
    )(south, north, west, east)


def insert_halos(ext, base, count, west, east, south, north):
    blank = jnp.zeros((128 - HALO * count, N + 2), F32)
    from_west = jnp.concatenate([west[...], blank], axis=0).T
    from_east = jnp.concatenate([east[...], blank], axis=0).T
    blank = jnp.zeros((128 - HALO * count, 128), F32)
    low = jnp.concatenate([south[:, 256:384], blank], axis=0).T
    high = jnp.concatenate([north[:, 256:384], blank], axis=0).T
    for f in range(count):
        s = slice(HALO * f, HALO * f + HALO)
        field = ext.at[base + f]
        field[TOP : TOP + N + 2, LANES - HALO : LANES] = from_west[:, s]
        field[TOP : TOP + N + 2, N : N + HALO] = from_east[:, s]
        for first, rows, block in ((TOP - HALO, south, low), (TOP + N, north, high)):
            at = N - 256
            field[first : first + HALO, 0:N] = rows[s, 0:N]
            field[first : first + HALO, LANES - HALO : LANES] = block[at : at + HALO, s]
            field[first : first + HALO, N : N + HALO] = block[at + HALO : at + 2 * HALO, s]


def row_mask(k):
    return lax.broadcasted_iota(I32, (8, LANES), 0) == k


def to_south(current, following):
    return pltpu.roll(jnp.where(row_mask(0), following, current), 7, 0)


def to_north(current, previous):
    return pltpu.roll(jnp.where(row_mask(7), previous, current), 1, 0)


def stencil(src, b, coef):
    center, east, west, north, south, mix = coef
    result = []
    for t in range(2):
        level = [src[t * LEV + k, pl.ds(b, 8), :] for k in range(LEV)]
        flux = [mix * (level[k] - level[k + 1]) for k in range(LEV - 1)]
        for k in range(LEV):
            c = level[k]
            f = t * LEV + k
            up = to_south(c, src[f, pl.ds(aligned(b + 8), 8), :])
            down = to_north(c, src[f, pl.ds(aligned(b - 8), 8), :])
            new = center * c + east * pltpu.roll(c, LANES - 1, 1) + west * pltpu.roll(c, 1, 1)
            new = new + (north * up + south * down)
            if k > 0:
                new = new + flux[k - 1]
            if k < LEV - 1:
                new = new - flux[k]
            result.append((c, new))
    return result


def adjoint_kernel(
    wet, labels, zd, zf, md, mf, vm, forcing, adjoint, west, east, south, north,
    initial, forward_coef, control,
    ext, other, coef, surface, coarse, piece,
):
    views = [zd, zf, md, mf, vm]
    ext[0, TOP : TOP + N + 2, :] = wet_field(wet, N + 2, 0)
    for f in range(1, 16):
        if f < 6:
            value = views[f - 1]
        elif f < 8:
            value = forcing.at[f - 6]
        else:
            value = adjoint.at[(f - 8) // LEV, (f - 8) % LEV]
        ext[f, TOP : TOP + N, 0:N] = value[...]
    insert_halos(ext, 0, 16, west, east, south, north)

    def coefficients(r, carry):
        north_a, north_b = carry
        b = aligned(r * 8)
        w, z_d, z_f, m_d, m_f, v = [ext[f, pl.ds(b, 8), :] for f in range(6)]
        east_open = w * pltpu.roll(w, LANES - 1, 1)
        north_open = w * to_south(w, ext[0, pl.ds(aligned(b + 8), 8), :])
        de = z_d * east_open
        ue = 0.5 * z_f * east_open
        dn = m_d * north_open
        vn = 0.5 * m_f * north_open
        ea, eb, na, nb = de + ue, ue - de, dn + vn, vn - dn
        eb_west = pltpu.roll(eb, 1, 1)
        nb_south = to_north(nb, north_b)
        rows = pl.ds(b, 8)
        forward_coef[0, rows, :] = 1.0 + ((eb_west - ea) + (nb_south - na))
        forward_coef[1, rows, :] = -eb
        forward_coef[2, rows, :] = pltpu.roll(ea, 1, 1)
        forward_coef[3, rows, :] = -nb
        forward_coef[4, rows, :] = to_north(na, north_a)
        forward_coef[5, rows, :] = v * w
        forward_coef[6, rows, :] = ext[6, rows, :] * w
        forward_coef[7, rows, :] = ext[7, rows, :] * w
        coef[0, rows, :] = ea
        coef[1, rows, :] = -eb_west
        coef[2, rows, :] = na
        coef[3, rows, :] = -nb_south
        return na, nb

    zero = jnp.zeros((8, LANES), F32)
    lax.fori_loop(1, CHUNKS + 2, coefficients, (zero, zero))

    def load_coef(b):
        rows = pl.ds(b, 8)
        return [forward_coef[0, rows, :]] + [coef[i, rows, :] for i in range(4)] + [forward_coef[5, rows, :]]

    lam = ext.at[pl.ds(8, 8)]

    def step(src, dst, first):
        @pl.loop(1, CHUNKS + 2)
        def _(r):
            b = aligned(r * 8)
            for f, (old, new) in enumerate(stencil(src, b, load_coef(b))):
                dst[f, pl.ds(b, 8), :] = new
                if f % LEV == 0:
                    t = f // LEV
                    surface[t, pl.ds(b, 8), :] = old if first else surface[t, pl.ds(b, 8), :] + old

    step(lam, other, True)
    step(other, lam, False)

    def finish(i, rows):
        b = aligned(TOP + 8 * i)
        w = ext[0, pl.ds(b, 8), :]
        for f, (old, new) in enumerate(stencil(lam, b, load_coef(b))):
            t, k = f // LEV, f % LEV
            if rows == 8:
                initial[t, k, pl.ds(aligned(8 * i), 8), :] = (w * new)[:, 0:N]
            else:
                initial[t, k, 8 * i : 8 * i + rows, :] = (w * new)[0:rows, 0:N]
            if k == 0:
                surface[t, pl.ds(b, 8), :] = w * (surface[t, pl.ds(b, 8), :] + old)

    @pl.loop(0, N // 8)
    def _(i):
        finish(i, 8)

    finish(N // 8, N % 8)

    BF = jnp.bfloat16

    def parts(x):
        hi = x.astype(BF)
        rest = x - hi.astype(F32)
        mid = rest.astype(BF)
        return hi, mid, (rest - mid.astype(F32)).astype(BF)

    def band(shape, out_axis):
        i = lax.broadcasted_iota(I32, shape, out_axis) * 3
        j = lax.broadcasted_iota(I32, shape, 1 - out_axis)
        return ((j >= i) & (j < i + 3) & (j < N)).astype(F32).astype(BF)

    by_row = band((96, N + 2), 0)
    by_lane = band((LANES, 128), 1)
    shape = (N + 2, LANES)
    inside = (lax.broadcasted_iota(I32, shape, 0) < N) & (lax.broadcasted_iota(I32, shape, 1) < N)
    for t in range(2):
        cells = jnp.where(inside, surface[t, TOP : TOP + N + 2, :], 0.0)
        half = sum(jnp.dot(by_row, p, preferred_element_type=F32) for p in parts(cells))
        full = sum(jnp.dot(p, by_lane, preferred_element_type=F32) for p in parts(half))
        coarse[t] = full / 9.0
    control[...] = jnp.zeros(control.shape, F32)
    piece[...] = jnp.zeros((16, 128), F32)
    part = COARSE // 2
    for r in range(SIDE):
        for c in range(SIDE):
            for t in range(2):
                for h in range(2):
                    at = COARSE * r + part * h
                    lane = 64 * h + COARSE * t
                    piece[0:part, lane : lane + COARSE] = coarse[
                        t, at : at + part, COARSE * c : COARSE * c + COARSE
                    ]
            control[labels[r, c]] = piece[...]


def adjoint_window(wet, labels, zd, zf, md, mf, vm, forcing, adjoint, west, east, south, north, owners):
    return pl.pallas_call(
        adjoint_kernel,
        out_shape=(
            jax.ShapeDtypeStruct((2, LEV, N, N), F32),
            jax.ShapeDtypeStruct((8, ROWS, LANES), F32),
            jax.ShapeDtypeStruct((owners, 16, 128), F32),
        ),
        in_specs=[SMEM, SMEM] + [VMEM] * 11,
        out_specs=(VMEM,) * 3,
        scratch_shapes=[
            pltpu.VMEM((16, ROWS, LANES), F32),
            pltpu.VMEM((8, ROWS, LANES), F32),
            pltpu.VMEM((4, ROWS, LANES), F32),
            pltpu.VMEM((2, ROWS, LANES), F32),
            pltpu.VMEM((2, 96, 128), F32),
            pltpu.VMEM((16, 128), F32),
        ],
        name="adjoint_window",
    )(wet, labels, zd, zf, md, mf, vm, forcing, adjoint, west, east, south, north)


def unpack_kernel(arrived, state, west, east, south, north, tags, slot_of, tiles, lined, tag_sem, tile_sem):
    sources = arrived.shape[0]
    copy = pltpu.make_async_copy(
        arrived.at[:, :, pl.ds(0, 1), pl.ds(TAIL, 128)], tags, tag_sem
    )
    copy.start()
    places = SIDE * SIDE

    @pl.loop(0, places)
    def _(p):
        slot_of[p] = -1

    copy.wait()

    @pl.loop(0, sources * PAIR)
    def _(i):
        source = i // PAIR
        place = tags[source, i - source * PAIR, 0, TAG].astype(I32)

        @pl.when(place >= 0)
        def _():
            slot_of[place] = i

    def fetch(p):
        slot = slot_of[p]
        source = slot // PAIR
        return pltpu.make_async_copy(arrived.at[source, slot - source * PAIR], tiles.at[p], tile_sem.at[p])

    @pl.loop(0, places)
    def _(p):
        @pl.when(slot_of[p] >= 0)
        def _():
            fetch(p).start()

        @pl.when(slot_of[p] < 0)
        def _():
            tiles[p] = jnp.zeros((8, FLAT), F32)

    @pl.loop(0, SIDE)
    def _(r):
        for c in range(SIDE):

            @pl.when(slot_of[r * SIDE + c] >= 0)
            def _():
                fetch(r * SIDE + c).wait()

        for y in range(TILE):
            for c in range(SIDE):
                lined[r * TILE + y, :, TILE * c : TILE * c + TILE] = tiles[
                    r * SIDE + c, :, TILE * y : TILE * y + TILE
                ]

    @pl.loop(0, CHUNKS)
    def _(g):
        state[:, pl.ds(aligned(TOP + 8 * g), 8), :] = jnp.swapaxes(lined[pl.ds(8 * g, 8)], 0, 1)

    west[...] = strip_columns(lambda f: state[f, TOP : TOP + N + 2, 0:128], 8, 0)
    east[...] = strip_columns(lambda f: state[f, TOP : TOP + N + 2, 256:384], 8, N - HALO - 256)
    for f in range(8):
        south[HALO * f : HALO * f + HALO, 0:N] = state[f, TOP : TOP + HALO, 0:N]
        north[HALO * f : HALO * f + HALO, 0:N] = state[f, TOP + N - HALO : TOP + N, 0:N]


def unpack_tiles(arrived):
    strip = jax.ShapeDtypeStruct((24, N + 2), F32)
    return pl.pallas_call(
        unpack_kernel,
        out_shape=(jax.ShapeDtypeStruct((8, ROWS, LANES), F32),) + (strip,) * 4,
        in_specs=[ANY],
        out_specs=(VMEM,) * 5,
        scratch_shapes=[
            pltpu.SMEM((arrived.shape[0], PAIR, 1, 128), F32),
            pltpu.SMEM((SIDE * SIDE,), I32),
            pltpu.VMEM((SIDE * SIDE, 8, FLAT), F32),
            pltpu.VMEM((8 * CHUNKS, 8, LANES), F32),
            pltpu.SemaphoreType.DMA,
            pltpu.SemaphoreType.DMA((SIDE * SIDE,)),
        ],
        name="unpack_tiles",
    )(arrived)


def forward_kernel(state, coef, west, east, south, north, final, first, second, sem):
    copy = pltpu.make_async_copy(state, first, sem)
    copy.start()
    copy.wait()
    insert_halos(first, 0, 8, west, east, south, north)

    def advanced(src, b):
        rows = pl.ds(b, 8)
        result = []
        for f, (_, new) in enumerate(stencil(src, b, [coef[i, rows, :] for i in range(6)])):
            if f % LEV == 0:
                new = new + coef[6 + f // LEV, rows, :]
            result.append(new)
        return result

    def step(src, dst):
        @pl.loop(1, CHUNKS + 2)
        def _(r):
            b = aligned(r * 8)
            for f, new in enumerate(advanced(src, b)):
                dst[f, pl.ds(b, 8), :] = new

    step(first, second)
    step(second, first)

    @pl.loop(0, N // 8)
    def _(i):
        for f, new in enumerate(advanced(first, aligned(TOP + 8 * i))):
            final[f // LEV, f % LEV, pl.ds(aligned(8 * i), 8), :] = new[:, 0:N]

    i = N // 8
    for f, new in enumerate(advanced(first, TOP + 8 * i)):
        final[f // LEV, f % LEV, 8 * i : N, :] = new[0 : N % 8, 0:N]


def forward_window(state, coef, west, east, south, north):
    return pl.pallas_call(
        forward_kernel,
        out_shape=jax.ShapeDtypeStruct((2, LEV, N, N), F32),
        in_specs=[ANY] + [VMEM] * 5,
        out_specs=VMEM,
        scratch_shapes=[
            pltpu.VMEM((8, ROWS, LANES), F32),
            pltpu.VMEM((8, ROWS, LANES), F32),
            pltpu.SemaphoreType.DMA,
        ],
        name="forward_window",
    )(state, coef, west, east, south, north)


def neighbours(low, high, axis, periodic):
    count = lax.axis_size(axis)
    up = [(i, i + 1) for i in range(count - 1)] + ([(count - 1, 0)] if periodic else [])
    down = [(b, a) for a, b in up]
    return lax.ppermute(high, axis, up), lax.ppermute(low, axis, down)


def per_device(
    stored_tiles, stored_ids, wet_tiles, control_map, zonal_diffusivity, meridional_diffusivity,
    zonal_flow, meridional_flow, vertical_mixing, forcing, final_adjoint,
):
    owners = lax.axis_size("lon")
    devices = lax.axis_size(("lat", "lon"))
    fields = (
        zonal_diffusivity, zonal_flow, meridional_diffusivity, meridional_flow, vertical_mixing,
        forcing, final_adjoint,
    )
    low, high, bottom, top = edge_strips(wet_tiles, *fields)
    west, east = neighbours(low, high, "lon", True)
    outgoing = pack_tiles(stored_ids, stored_tiles, low, owners)
    outgoing, west, east = lax.optimization_barrier((outgoing, west, east))
    arrived = lax.all_to_all(outgoing, "lon", split_axis=0, concat_axis=0, tiled=True)
    south, north = neighbours(*with_corners(bottom, top, west, east), "lat", False)
    initial, coef, pieces = adjoint_window(
        wet_tiles, control_map, *fields, west, east, south, north, devices
    )
    gathered = lax.all_to_all(pieces, ("lat", "lon"), split_axis=0, concat_axis=0, tiled=True)
    total = jnp.sum(gathered, axis=0)[: COARSE // 2]
    total = jnp.stack([total[:, :60], total[:, 64:124]]).reshape(2, COARSE // 2, 2, COARSE)
    control = total.transpose(2, 0, 1, 3).reshape(1, 2, COARSE * COARSE)

    state, low, high, bottom, top = unpack_tiles(arrived)
    west, east = neighbours(low, high, "lon", True)
    south, north = neighbours(*with_corners(bottom, top, west, east), "lat", False)
    final = forward_window(state, coef, west, east, south, north)
    return final, initial, control


def solution(mesh):
    grid = P("lat", "lon")
    return jax.shard_map(
        per_device,
        mesh=mesh,
        in_specs=(
            P(("lat", "lon"), None, None), P(("lat", "lon")), grid, grid, grid, grid, grid, grid, grid,
            P(None, "lat", "lon"), P(None, None, "lat", "lon"),
        ),
        out_specs=(
            P(None, None, "lat", "lon"), P(None, None, "lat", "lon"), P(("lat", "lon"), None, None),
        ),
        check_vma=False,
    )
```

```python
import jax
import jax.numpy as jnp
from jax import lax
from jax.experimental import pallas as pl
from jax.experimental.pallas import tpu as pltpu
from jax.sharding import PartitionSpec as P


F32 = jnp.float32
I32 = jnp.int32
TILE = 90
SIDE = 3
COLUMNS = 48
HALO = 3
SLOTS = 27
PAIR = 2
LEV = 4
CELLS = TILE * TILE
N = TILE * SIDE
FLAT = 8192
TAIL = 8064
TAG = CELLS - TAIL
TOP = 16
ROWS = 296
LANES = 384
CHUNKS = 34
COARSE = 30
VMEM = pl.BlockSpec(memory_space=pltpu.VMEM)
SMEM = pl.BlockSpec(memory_space=pltpu.SMEM)
ANY = pl.BlockSpec(memory_space=pl.ANY)


def aligned(x):
    return pl.multiple_of(x, 8)


def pack_kernel(ids, stored, after, out, held, tail, empty, count, route, in_sem, out_sem, tail_sem, empty_sem):
    owners = out.shape[0]

    def fetch(s):
        return pltpu.make_async_copy(stored.at[s], held.at[s], in_sem.at[s])

    def send(s, owner, rank):
        return pltpu.make_async_copy(
            held.at[s, :, pl.ds(0, TAIL)], out.at[owner, rank, :, pl.ds(0, TAIL)], out_sem.at[s]
        )

    def send_tail(s, owner, rank):
        return pltpu.make_async_copy(
            tail.at[s], out.at[owner, rank, :, pl.ds(TAIL, 128)], tail_sem.at[s]
        )

    def send_empty(owner, rank):
        return pltpu.make_async_copy(
            empty, out.at[owner, rank, :, pl.ds(TAIL, 128)], empty_sem.at[owner, rank]
        )

    @pl.loop(0, SLOTS)
    def _(s):
        @pl.when(ids[s] >= 0)
        def _():
            fetch(s).start()

    @pl.loop(0, owners)
    def _(o):
        count[o] = 0

    empty[...] = jnp.full((8, 128), -1.0, F32)
    lane = lax.broadcasted_iota(I32, (8, 128), 1)

    @pl.loop(0, SLOTS)
    def _(s):
        tile = ids[s]

        @pl.when(tile >= 0)
        def _():
            row = tile // COLUMNS
            column = tile - row * COLUMNS
            owner = column // SIDE
            rank = count[owner]
            count[owner] = rank + 1
            route[s] = owner * PAIR + rank
            place = row * SIDE + column - owner * SIDE
            fetch(s).wait()
            last = jnp.concatenate([held[s, :, TAIL:CELLS], jnp.zeros((8, 128 - TAG), F32)], axis=1)
            tail[s] = jnp.where(lane < TAG, last, place.astype(F32))
            send(s, owner, rank).start()
            send_tail(s, owner, rank).start()

    for rank in range(PAIR):

        @pl.loop(0, owners)
        def _(o):
            @pl.when(count[o] <= rank)
            def _():
                send_empty(o, rank).start()

    @pl.loop(0, SLOTS)
    def _(s):
        @pl.when(ids[s] >= 0)
        def _():
            owner = route[s] // PAIR
            rank = route[s] - owner * PAIR
            send(s, owner, rank).wait()
            send_tail(s, owner, rank).wait()

    for rank in range(PAIR):

        @pl.loop(0, owners)
        def _(o):
            @pl.when(count[o] <= rank)
            def _():
                send_empty(o, rank).wait()


def pack_tiles(ids, stored, after, owners):
    return pl.pallas_call(
        pack_kernel,
        out_shape=jax.ShapeDtypeStruct((owners, PAIR, 8, FLAT), F32),
        in_specs=[SMEM, ANY, ANY],
        out_specs=ANY,
        scratch_shapes=[
            pltpu.VMEM((SLOTS, 8, CELLS), F32),
            pltpu.VMEM((SLOTS, 8, 128), F32),
            pltpu.VMEM((8, 128), F32),
            pltpu.SMEM((owners,), I32),
            pltpu.SMEM((SLOTS,), I32),
            pltpu.SemaphoreType.DMA((SLOTS,)),
            pltpu.SemaphoreType.DMA((SLOTS,)),
            pltpu.SemaphoreType.DMA((SLOTS,)),
            pltpu.SemaphoreType.DMA((owners, PAIR)),
        ],
        name="pack_tiles",
    )(ids, stored, after)


def strip_columns(load, count, first):
    lane = lax.broadcasted_iota(I32, (N + 2, 128), 1)
    strip = jnp.zeros((N + 2, 128), F32)
    for f in range(count):
        moved = pltpu.roll(load(f), (HALO * f - first) % 128, 1)
        strip = jnp.where((lane >= HALO * f) & (lane < HALO * f + HALO), moved, strip)
    return strip.T[0 : HALO * count]


def wet_field(wet, rows, row0):
    row = lax.broadcasted_iota(I32, (rows, LANES), 0) + row0
    lane = lax.broadcasted_iota(I32, (rows, LANES), 1)
    bands = []
    for r in range(SIDE):
        w = [wet[r, c].astype(F32) for c in range(SIDE)]
        bands.append(jnp.where(lane < TILE, w[0], jnp.where(lane < 2 * TILE, w[1], w[2])))
    return jnp.where(row < TILE, bands[0], jnp.where(row < 2 * TILE, bands[1], bands[2]))


def edges_kernel(wet, zd, zf, md, mf, vm, forcing, adjoint, west, east, south, north, held):
    views = [zd, zf, md, mf, vm]
    full = wet_field(wet, N + 2, 0)
    held[0, 0] = full[:, 0:128]
    held[1, 0] = full[:, 256:384]
    south[0:HALO, 0:N] = full[0:HALO, 0:N]
    north[0:HALO, 0:N] = full[N - HALO : N, 0:N]
    for f in range(1, 6):
        ref = views[f - 1]
        south[HALO * f : HALO * f + HALO, 0:N] = ref[0:HALO, :]
        north[HALO * f : HALO * f + HALO, 0:N] = ref[N - HALO : N, :]
        held[0, f, 0:N, :] = ref[:, 0:128]
        held[1, f, 0:N, 0 : N - 256] = ref[:, 256:N]
    for out, first in ((south, 0), (north, N - HALO)):
        for y in range(HALO):
            row = forcing[first + y]
            for f in range(2):
                out[HALO * (6 + f) + y, 0:N] = row[f]
            for t in range(2):
                row = adjoint[t, first + y]
                for k in range(LEV):
                    out[HALO * (8 + LEV * t + k) + y, 0:N] = row[k]

    def lines(at, start):
        for side, width in ((0, 128), (1, N - 256)):
            lanes = slice(256 * side, 256 * side + width)
            for base, ref, depth in ((6, forcing, 2), (8, adjoint.at[0], LEV), (8 + LEV, adjoint.at[1], LEV)):
                block = jnp.swapaxes(ref[pl.ds(start, 8), :, lanes], 0, 1)
                for k in range(depth):
                    held[side, base + k, at, 0:width] = block[k]

    @pl.loop(0, N // 8)
    def _(g):
        lines(pl.ds(aligned(8 * g), 8), 8 * g)

    lines(slice(N - 8, N), N - 8)

    def low(f):
        return held[0, f]

    def high(f):
        return held[1, f]

    west[...] = strip_columns(low, 16, 0)
    east[...] = strip_columns(high, 16, N - HALO - 256)


def edge_strips(wet, zd, zf, md, mf, vm, forcing, adjoint):
    columns = jax.ShapeDtypeStruct((48, N + 2), F32)
    rows = jax.ShapeDtypeStruct((48, N + 2), F32)
    return pl.pallas_call(
        edges_kernel,
        out_shape=(columns, columns, rows, rows),
        in_specs=[SMEM] + [VMEM] * 7,
        out_specs=(VMEM,) * 4,
        scratch_shapes=[pltpu.VMEM((2, 16, N + 2, 128), F32)],
        name="edge_strips",
    )(wet, zd, zf, md, mf, vm, forcing, adjoint)


def corners_kernel(south, north, west, east, to_south, to_north):
    for rows, out, first in ((south, to_south, 0), (north, to_north, N - HALO)):
        out[:, 0:N] = rows[:, 0:N]
        out[:, N : N + HALO] = west[:, first : first + HALO]
        out[:, N + HALO : N + 2 * HALO] = east[:, first : first + HALO]


def with_corners(south, north, west, east):
    shape = jax.ShapeDtypeStruct((south.shape[0], LANES), F32)
    return pl.pallas_call(
        corners_kernel,
        out_shape=(shape, shape),
        in_specs=[VMEM] * 4,
        out_specs=(VMEM,) * 2,
        name="row_strips",
    )(south, north, west, east)


def insert_halos(ext, base, count, west, east, south, north):
    blank = jnp.zeros((128 - HALO * count, N + 2), F32)
    from_west = jnp.concatenate([west[...], blank], axis=0).T
    from_east = jnp.concatenate([east[...], blank], axis=0).T
    blank = jnp.zeros((128 - HALO * count, 128), F32)
    low = jnp.concatenate([south[:, 256:384], blank], axis=0).T
    high = jnp.concatenate([north[:, 256:384], blank], axis=0).T
    for f in range(count):
        s = slice(HALO * f, HALO * f + HALO)
        field = ext.at[base + f]
        field[TOP : TOP + N + 2, LANES - HALO : LANES] = from_west[:, s]
        field[TOP : TOP + N + 2, N : N + HALO] = from_east[:, s]
        for first, rows, block in ((TOP - HALO, south, low), (TOP + N, north, high)):
            at = N - 256
            field[first : first + HALO, 0:N] = rows[s, 0:N]
            field[first : first + HALO, LANES - HALO : LANES] = block[at : at + HALO, s]
            field[first : first + HALO, N : N + HALO] = block[at + HALO : at + 2 * HALO, s]


def row_mask(k):
    return lax.broadcasted_iota(I32, (8, LANES), 0) == k


def to_south(current, following):
    return pltpu.roll(jnp.where(row_mask(0), following, current), 7, 0)


def to_north(current, previous):
    return pltpu.roll(jnp.where(row_mask(7), previous, current), 1, 0)


def stencil(src, b, coef):
    center, east, west, north, south, mix = coef
    result = []
    for t in range(2):
        level = [src[t * LEV + k, pl.ds(b, 8), :] for k in range(LEV)]
        flux = [mix * (level[k] - level[k + 1]) for k in range(LEV - 1)]
        for k in range(LEV):
            c = level[k]
            f = t * LEV + k
            up = to_south(c, src[f, pl.ds(aligned(b + 8), 8), :])
            down = to_north(c, src[f, pl.ds(aligned(b - 8), 8), :])
            new = center * c + east * pltpu.roll(c, LANES - 1, 1) + west * pltpu.roll(c, 1, 1)
            new = new + (north * up + south * down)
            if k > 0:
                new = new + flux[k - 1]
            if k < LEV - 1:
                new = new - flux[k]
            result.append((c, new))
    return result


def store_levels(out, values, i, rows):
    for t in range(2):
        block = jnp.swapaxes(jnp.stack(values[LEV * t : LEV * t + LEV]), 0, 1)
        out[t, pl.ds(8 * i, rows)] = block[0:rows, :, 0:N]


def adjoint_kernel(
    wet, labels, zd, zf, md, mf, vm, forcing, adjoint, west, east, south, north,
    initial, forward_coef, keep, give,
    ext, other, coef, surface, coarse, piece,
):
    views = [zd, zf, md, mf, vm]
    ext[0, TOP : TOP + N + 2, :] = wet_field(wet, N + 2, 0)
    for f in range(1, 6):
        ext[f, TOP : TOP + N, 0:N] = views[f - 1][...]

    def lines(at, start):
        for base, ref, depth in ((6, forcing, 2), (8, adjoint.at[0], LEV), (8 + LEV, adjoint.at[1], LEV)):
            block = jnp.swapaxes(ref[pl.ds(start, 8)], 0, 1)
            for k in range(depth):
                ext[base + k, at, 0:N] = block[k]

    @pl.loop(0, N // 8)
    def _(g):
        lines(pl.ds(aligned(TOP + 8 * g), 8), 8 * g)

    lines(slice(TOP + N - 8, TOP + N), N - 8)
    insert_halos(ext, 0, 16, west, east, south, north)

    def coefficients(r, carry):
        north_a, north_b = carry
        b = aligned(r * 8)
        w, z_d, z_f, m_d, m_f, v = [ext[f, pl.ds(b, 8), :] for f in range(6)]
        east_open = w * pltpu.roll(w, LANES - 1, 1)
        north_open = w * to_south(w, ext[0, pl.ds(aligned(b + 8), 8), :])
        de = z_d * east_open
        ue = 0.5 * z_f * east_open
        dn = m_d * north_open
        vn = 0.5 * m_f * north_open
        ea, eb, na, nb = de + ue, ue - de, dn + vn, vn - dn
        eb_west = pltpu.roll(eb, 1, 1)
        nb_south = to_north(nb, north_b)
        rows = pl.ds(b, 8)
        forward_coef[0, rows, :] = 1.0 + ((eb_west - ea) + (nb_south - na))
        forward_coef[1, rows, :] = -eb
        forward_coef[2, rows, :] = pltpu.roll(ea, 1, 1)
        forward_coef[3, rows, :] = -nb
        forward_coef[4, rows, :] = to_north(na, north_a)
        forward_coef[5, rows, :] = v * w
        forward_coef[6, rows, :] = ext[6, rows, :] * w
        forward_coef[7, rows, :] = ext[7, rows, :] * w
        coef[0, rows, :] = ea
        coef[1, rows, :] = -eb_west
        coef[2, rows, :] = na
        coef[3, rows, :] = -nb_south
        return na, nb

    zero = jnp.zeros((8, LANES), F32)
    lax.fori_loop(1, CHUNKS + 2, coefficients, (zero, zero))

    def load_coef(b):
        rows = pl.ds(b, 8)
        return [forward_coef[0, rows, :]] + [coef[i, rows, :] for i in range(4)] + [forward_coef[5, rows, :]]

    lam = ext.at[pl.ds(8, 8)]

    def step(src, dst, first):
        @pl.loop(1, CHUNKS + 2)
        def _(r):
            b = aligned(r * 8)
            for f, (old, new) in enumerate(stencil(src, b, load_coef(b))):
                dst[f, pl.ds(b, 8), :] = new
                if f % LEV == 0:
                    t = f // LEV
                    surface[t, pl.ds(b, 8), :] = old if first else surface[t, pl.ds(b, 8), :] + old

    step(lam, other, True)
    step(other, lam, False)

    def finish(i, rows):
        b = aligned(TOP + 8 * i)
        w = ext[0, pl.ds(b, 8), :]
        values = stencil(lam, b, load_coef(b))
        store_levels(initial, [w * new for _, new in values], i, rows)
        for t in range(2):
            surface[t, pl.ds(b, 8), :] = w * (surface[t, pl.ds(b, 8), :] + values[LEV * t][0])

    @pl.loop(0, N // 8)
    def _(i):
        finish(i, 8)

    finish(N // 8, N % 8)

    BF = jnp.bfloat16

    def parts(x):
        hi = x.astype(BF)
        rest = x - hi.astype(F32)
        mid = rest.astype(BF)
        return hi, mid, (rest - mid.astype(F32)).astype(BF)

    def band(shape, out_axis):
        i = lax.broadcasted_iota(I32, shape, out_axis) * 3
        j = lax.broadcasted_iota(I32, shape, 1 - out_axis)
        return ((j >= i) & (j < i + 3) & (j < N)).astype(F32).astype(BF)

    by_row = band((96, N + 2), 0)
    by_lane = band((LANES, 128), 1)
    shape = (N + 2, LANES)
    inside = (lax.broadcasted_iota(I32, shape, 0) < N) & (lax.broadcasted_iota(I32, shape, 1) < N)
    for t in range(2):
        cells = jnp.where(inside, surface[t, TOP : TOP + N + 2, :], 0.0)
        half = sum(jnp.dot(by_row, p, preferred_element_type=F32) for p in parts(cells))
        full = sum(jnp.dot(p, by_lane, preferred_element_type=F32) for p in parts(half))
        coarse[t] = full / 9.0
    owners = keep.shape[0] // 4
    here = lax.axis_index("lat")
    keep[...] = jnp.zeros(keep.shape, F32)
    give[...] = jnp.zeros(give.shape, F32)
    piece[...] = jnp.zeros((16, 128), F32)
    part = COARSE // 2
    for r in range(SIDE):
        for c in range(SIDE):
            for t in range(2):
                for h in range(2):
                    at = COARSE * r + part * h
                    lane = 64 * h + COARSE * t
                    piece[0:part, lane : lane + COARSE] = coarse[
                        t, at : at + part, COARSE * c : COARSE * c + COARSE
                    ]
            label = labels[r, c]
            row = label // owners
            away = row ^ here
            at = ((away & 1) * 2 + (away >> 2)) * owners + label - row * owners

            @pl.when((away & 2) == 0)
            def _():
                keep[at] = piece[...]

            @pl.when((away & 2) != 0)
            def _():
                give[at] = piece[...]


def adjoint_window(wet, labels, zd, zf, md, mf, vm, forcing, adjoint, west, east, south, north, owners):
    return pl.pallas_call(
        adjoint_kernel,
        out_shape=(
            jax.ShapeDtypeStruct((2, N, LEV, N), F32),
            jax.ShapeDtypeStruct((8, ROWS, LANES), F32),
            jax.ShapeDtypeStruct((4 * owners, 16, 128), F32),
            jax.ShapeDtypeStruct((4 * owners, 16, 128), F32),
        ),
        in_specs=[SMEM, SMEM] + [VMEM] * 11,
        out_specs=(VMEM,) * 4,
        scratch_shapes=[
            pltpu.VMEM((16, ROWS, LANES), F32),
            pltpu.VMEM((8, ROWS, LANES), F32),
            pltpu.VMEM((4, ROWS, LANES), F32),
            pltpu.VMEM((2, ROWS, LANES), F32),
            pltpu.VMEM((2, 96, 128), F32),
            pltpu.VMEM((16, 128), F32),
        ],
        name="adjoint_window",
    )(wet, labels, zd, zf, md, mf, vm, forcing, adjoint, west, east, south, north)


def unpack_kernel(arrived, state, west, east, south, north, tags, slot_of, tiles, lined, tag_sem, tile_sem):
    sources = arrived.shape[0]
    copy = pltpu.make_async_copy(
        arrived.at[:, :, pl.ds(0, 1), pl.ds(TAIL, 128)], tags, tag_sem
    )
    copy.start()
    places = SIDE * SIDE

    @pl.loop(0, places)
    def _(p):
        slot_of[p] = -1

    copy.wait()

    @pl.loop(0, sources * PAIR)
    def _(i):
        source = i // PAIR
        place = tags[source, i - source * PAIR, 0, TAG].astype(I32)

        @pl.when(place >= 0)
        def _():
            slot_of[place] = i

    def fetch(p):
        slot = slot_of[p]
        source = slot // PAIR
        return pltpu.make_async_copy(arrived.at[source, slot - source * PAIR], tiles.at[p], tile_sem.at[p])

    @pl.loop(0, places)
    def _(p):
        @pl.when(slot_of[p] >= 0)
        def _():
            fetch(p).start()

        @pl.when(slot_of[p] < 0)
        def _():
            tiles[p] = jnp.zeros((8, FLAT), F32)

    @pl.loop(0, SIDE)
    def _(r):
        for c in range(SIDE):

            @pl.when(slot_of[r * SIDE + c] >= 0)
            def _():
                fetch(r * SIDE + c).wait()

        for y in range(TILE):
            for c in range(SIDE):
                lined[r * TILE + y, :, TILE * c : TILE * c + TILE] = tiles[
                    r * SIDE + c, :, TILE * y : TILE * y + TILE
                ]

    @pl.loop(0, CHUNKS)
    def _(g):
        state[:, pl.ds(aligned(TOP + 8 * g), 8), :] = jnp.swapaxes(lined[pl.ds(8 * g, 8)], 0, 1)

    west[...] = strip_columns(lambda f: state[f, TOP : TOP + N + 2, 0:128], 8, 0)
    east[...] = strip_columns(lambda f: state[f, TOP : TOP + N + 2, 256:384], 8, N - HALO - 256)
    for f in range(8):
        south[HALO * f : HALO * f + HALO, 0:N] = state[f, TOP : TOP + HALO, 0:N]
        north[HALO * f : HALO * f + HALO, 0:N] = state[f, TOP + N - HALO : TOP + N, 0:N]


def unpack_tiles(arrived):
    strip = jax.ShapeDtypeStruct((24, N + 2), F32)
    return pl.pallas_call(
        unpack_kernel,
        out_shape=(jax.ShapeDtypeStruct((8, ROWS, LANES), F32),) + (strip,) * 4,
        in_specs=[ANY],
        out_specs=(VMEM,) * 5,
        scratch_shapes=[
            pltpu.SMEM((arrived.shape[0], PAIR, 1, 128), F32),
            pltpu.SMEM((SIDE * SIDE,), I32),
            pltpu.VMEM((SIDE * SIDE, 8, FLAT), F32),
            pltpu.VMEM((8 * CHUNKS, 8, LANES), F32),
            pltpu.SemaphoreType.DMA,
            pltpu.SemaphoreType.DMA((SIDE * SIDE,)),
        ],
        name="unpack_tiles",
    )(arrived)


def forward_kernel(state, coef, west, east, south, north, final, first, second, sem):
    copy = pltpu.make_async_copy(state, first, sem)
    copy.start()
    copy.wait()
    insert_halos(first, 0, 8, west, east, south, north)

    def advanced(src, b):
        rows = pl.ds(b, 8)
        result = []
        for f, (_, new) in enumerate(stencil(src, b, [coef[i, rows, :] for i in range(6)])):
            if f % LEV == 0:
                new = new + coef[6 + f // LEV, rows, :]
            result.append(new)
        return result

    def step(src, dst):
        @pl.loop(1, CHUNKS + 2)
        def _(r):
            b = aligned(r * 8)
            for f, new in enumerate(advanced(src, b)):
                dst[f, pl.ds(b, 8), :] = new

    step(first, second)
    step(second, first)

    @pl.loop(0, N // 8)
    def _(i):
        store_levels(final, advanced(first, aligned(TOP + 8 * i)), i, 8)

    store_levels(final, advanced(first, TOP + N // 8 * 8), N // 8, N % 8)


def forward_window(state, coef, west, east, south, north):
    return pl.pallas_call(
        forward_kernel,
        out_shape=jax.ShapeDtypeStruct((2, N, LEV, N), F32),
        in_specs=[ANY] + [VMEM] * 5,
        out_specs=VMEM,
        scratch_shapes=[
            pltpu.VMEM((8, ROWS, LANES), F32),
            pltpu.VMEM((8, ROWS, LANES), F32),
            pltpu.SemaphoreType.DMA,
        ],
        name="forward_window",
    )(state, coef, west, east, south, north)


def neighbours(low, high, axis, periodic):
    count = lax.axis_size(axis)
    up = [(i, i + 1) for i in range(count - 1)] + ([(count - 1, 0)] if periodic else [])
    down = [(b, a) for a, b in up]
    return lax.ppermute(high, axis, up), lax.ppermute(low, axis, down)


def per_device(
    stored_tiles, stored_ids, wet_tiles, control_map, zonal_diffusivity, meridional_diffusivity,
    zonal_flow, meridional_flow, vertical_mixing, forcing, final_adjoint,
):
    owners = lax.axis_size("lon")
    fields = (
        zonal_diffusivity, zonal_flow, meridional_diffusivity, meridional_flow, vertical_mixing,
        forcing.transpose(1, 0, 2), final_adjoint.transpose(0, 2, 1, 3),
    )
    low, high, bottom, top = edge_strips(wet_tiles, *fields)
    west, east = neighbours(low, high, "lon", True)
    outgoing = pack_tiles(stored_ids, stored_tiles, low, owners)
    outgoing, west, east = lax.optimization_barrier((outgoing, west, east))
    arrived = lax.all_to_all(outgoing, "lon", split_axis=0, concat_axis=0, tiled=True)
    south, north = neighbours(*with_corners(bottom, top, west, east), "lat", False)
    initial, coef, keep, give = adjoint_window(
        wet_tiles, control_map, *fields, west, east, south, north, owners
    )
    for bit in (2, 1, 4):
        keep = keep + lax.ppermute(give, "lat", [(i, i ^ bit) for i in range(lax.axis_size("lat"))])
        half = keep.shape[0] // 2
        if bit != 4:
            keep, give = keep[:half], keep[half:]
    gathered = lax.all_to_all(keep, "lon", split_axis=0, concat_axis=0, tiled=True)
    total = jnp.sum(gathered, axis=0)[: COARSE // 2]
    total = jnp.stack([total[:, :60], total[:, 64:124]]).reshape(2, COARSE // 2, 2, COARSE)
    control = total.transpose(2, 0, 1, 3).reshape(1, 2, COARSE * COARSE)

    state, low, high, bottom, top = unpack_tiles(arrived)
    west, east = neighbours(low, high, "lon", True)
    south, north = neighbours(*with_corners(bottom, top, west, east), "lat", False)
    final = forward_window(state, coef, west, east, south, north)
    return final.transpose(0, 2, 1, 3), initial.transpose(0, 2, 1, 3), control


def solution(mesh):
    grid = P("lat", "lon")
    return jax.shard_map(
        per_device,
        mesh=mesh,
        in_specs=(
            P(("lat", "lon"), None, None), P(("lat", "lon")), grid, grid, grid, grid, grid, grid, grid,
            P(None, "lat", "lon"), P(None, None, "lat", "lon"),
        ),
        out_specs=(
            P(None, None, "lat", "lon"), P(None, None, "lat", "lon"), P(("lat", "lon"), None, None),
        ),
        check_vma=False,
    )
```

```python
import jax
import jax.numpy as jnp
from jax import lax
from jax.experimental import pallas as pl
from jax.experimental.pallas import tpu as pltpu
from jax.sharding import PartitionSpec as P


F32 = jnp.float32
I32 = jnp.int32
TILE = 90
SIDE = 3
COLUMNS = 48
HALO = 3
SLOTS = 27
PAIR = 2
LEV = 4
CELLS = TILE * TILE
N = TILE * SIDE
FLAT = 8192
TAIL = 8064
TAG = CELLS - TAIL
TOP = 16
ROWS = 304
LANES = 384
BLOCKS = ((0, 128), (1, 128), (2, N - 256))
CHUNKS = 34
COARSE = 30
VMEM = pl.BlockSpec(memory_space=pltpu.VMEM)
SMEM = pl.BlockSpec(memory_space=pltpu.SMEM)
ANY = pl.BlockSpec(memory_space=pl.ANY)


def aligned(x):
    return pl.multiple_of(x, 8)


def pack_kernel(ids, stored, after, out, held, tail, empty, count, route, in_sem, out_sem, tail_sem, empty_sem):
    owners = out.shape[0]

    def fetch(s):
        return pltpu.make_async_copy(stored.at[s], held.at[s], in_sem.at[s])

    def send(s, owner, rank):
        return pltpu.make_async_copy(
            held.at[s, :, pl.ds(0, TAIL)], out.at[owner, rank, :, pl.ds(0, TAIL)], out_sem.at[s]
        )

    def send_tail(s, owner, rank):
        return pltpu.make_async_copy(
            tail.at[s], out.at[owner, rank, :, pl.ds(TAIL, 128)], tail_sem.at[s]
        )

    def send_empty(owner, rank):
        return pltpu.make_async_copy(
            empty, out.at[owner, rank, :, pl.ds(TAIL, 128)], empty_sem.at[owner, rank]
        )

    @pl.loop(0, SLOTS)
    def _(s):
        @pl.when(ids[s] >= 0)
        def _():
            fetch(s).start()

    @pl.loop(0, owners)
    def _(o):
        count[o] = 0

    empty[...] = jnp.full((8, 128), -1.0, F32)
    lane = lax.broadcasted_iota(I32, (8, 128), 1)

    @pl.loop(0, SLOTS)
    def _(s):
        tile = ids[s]

        @pl.when(tile >= 0)
        def _():
            row = tile // COLUMNS
            column = tile - row * COLUMNS
            owner = column // SIDE
            rank = count[owner]
            count[owner] = rank + 1
            route[s] = owner * PAIR + rank
            place = row * SIDE + column - owner * SIDE
            fetch(s).wait()
            last = jnp.concatenate([held[s, :, TAIL:CELLS], jnp.zeros((8, 128 - TAG), F32)], axis=1)
            tail[s] = jnp.where(lane < TAG, last, place.astype(F32))
            send(s, owner, rank).start()
            send_tail(s, owner, rank).start()

    for rank in range(PAIR):

        @pl.loop(0, owners)
        def _(o):
            @pl.when(count[o] <= rank)
            def _():
                send_empty(o, rank).start()

    @pl.loop(0, SLOTS)
    def _(s):
        @pl.when(ids[s] >= 0)
        def _():
            owner = route[s] // PAIR
            rank = route[s] - owner * PAIR
            send(s, owner, rank).wait()
            send_tail(s, owner, rank).wait()

    for rank in range(PAIR):

        @pl.loop(0, owners)
        def _(o):
            @pl.when(count[o] <= rank)
            def _():
                send_empty(o, rank).wait()


def pack_tiles(ids, stored, after, owners):
    return pl.pallas_call(
        pack_kernel,
        out_shape=jax.ShapeDtypeStruct((owners, PAIR, 8, FLAT), F32),
        in_specs=[SMEM, ANY, ANY],
        out_specs=ANY,
        scratch_shapes=[
            pltpu.VMEM((SLOTS, 8, CELLS), F32),
            pltpu.VMEM((SLOTS, 8, 128), F32),
            pltpu.VMEM((8, 128), F32),
            pltpu.SMEM((owners,), I32),
            pltpu.SMEM((SLOTS,), I32),
            pltpu.SemaphoreType.DMA((SLOTS,)),
            pltpu.SemaphoreType.DMA((SLOTS,)),
            pltpu.SemaphoreType.DMA((SLOTS,)),
            pltpu.SemaphoreType.DMA((owners, PAIR)),
        ],
        name="pack_tiles",
    )(ids, stored, after)


def strip_columns(load, count, first):
    lane = lax.broadcasted_iota(I32, (N + 2, 128), 1)
    strip = jnp.zeros((N + 2, 128), F32)
    for f in range(count):
        moved = pltpu.roll(load(f), (HALO * f - first) % 128, 1)
        strip = jnp.where((lane >= HALO * f) & (lane < HALO * f + HALO), moved, strip)
    return strip.T[0 : HALO * count]


def wet_field(wet, rows, row0):
    row = lax.broadcasted_iota(I32, (rows, LANES), 0) + row0
    lane = lax.broadcasted_iota(I32, (rows, LANES), 1)
    bands = []
    for r in range(SIDE):
        w = [wet[r, c].astype(F32) for c in range(SIDE)]
        bands.append(jnp.where(lane < TILE, w[0], jnp.where(lane < 2 * TILE, w[1], w[2])))
    return jnp.where(row < TILE, bands[0], jnp.where(row < 2 * TILE, bands[1], bands[2]))


def edges_kernel(wet, zd, zf, md, mf, vm, forcing, adjoint, west, east, south, north, held):
    views = [zd, zf, md, mf, vm]
    full = wet_field(wet, N + 2, 0)
    held[0, 0] = full[:, 0:128]
    held[1, 0] = full[:, 256:384]
    south[0:HALO, 0:N] = full[0:HALO, 0:N]
    north[0:HALO, 0:N] = full[N - HALO : N, 0:N]
    for f in range(1, 6):
        ref = views[f - 1]
        south[HALO * f : HALO * f + HALO, 0:N] = ref[0:HALO, :]
        north[HALO * f : HALO * f + HALO, 0:N] = ref[N - HALO : N, :]
        held[0, f, 0:N, :] = ref[:, 0:128]
        held[1, f, 0:N, 0 : N - 256] = ref[:, 256:N]
    for out, first in ((south, 0), (north, N - HALO)):
        for y in range(HALO):
            row = forcing[first + y]
            for f in range(2):
                out[HALO * (6 + f) + y, 0:N] = row[f]
            for t in range(2):
                row = adjoint[t, first + y]
                for k in range(LEV):
                    out[HALO * (8 + LEV * t + k) + y, 0:N] = row[k]

    def lines(at, start):
        for side, width in ((0, 128), (1, N - 256)):
            lanes = slice(256 * side, 256 * side + width)
            for base, ref, depth in ((6, forcing, 2), (8, adjoint.at[0], LEV), (8 + LEV, adjoint.at[1], LEV)):
                block = jnp.swapaxes(ref[pl.ds(start, 8), :, lanes], 0, 1)
                for k in range(depth):
                    held[side, base + k, at, 0:width] = block[k]

    @pl.loop(0, N // 8)
    def _(g):
        lines(pl.ds(aligned(8 * g), 8), 8 * g)

    lines(slice(N - 8, N), N - 8)

    def low(f):
        return held[0, f]

    def high(f):
        return held[1, f]

    west[...] = strip_columns(low, 16, 0)
    east[...] = strip_columns(high, 16, N - HALO - 256)


def edge_strips(wet, zd, zf, md, mf, vm, forcing, adjoint):
    columns = jax.ShapeDtypeStruct((48, N + 2), F32)
    rows = jax.ShapeDtypeStruct((48, N + 2), F32)
    return pl.pallas_call(
        edges_kernel,
        out_shape=(columns, columns, rows, rows),
        in_specs=[SMEM] + [VMEM] * 7,
        out_specs=(VMEM,) * 4,
        scratch_shapes=[pltpu.VMEM((2, 16, N + 2, 128), F32)],
        name="edge_strips",
    )(wet, zd, zf, md, mf, vm, forcing, adjoint)


def corners_kernel(south, north, west, east, to_south, to_north):
    for rows, out, first in ((south, to_south, 0), (north, to_north, N - HALO)):
        out[:, 0:N] = rows[:, 0:N]
        out[:, N : N + HALO] = west[:, first : first + HALO]
        out[:, N + HALO : N + 2 * HALO] = east[:, first : first + HALO]


def with_corners(south, north, west, east):
    shape = jax.ShapeDtypeStruct((south.shape[0], LANES), F32)
    return pl.pallas_call(
        corners_kernel,
        out_shape=(shape, shape),
        in_specs=[VMEM] * 4,
        out_specs=(VMEM,) * 2,
        name="row_strips",
    )(south, north, west, east)


def insert_halos(ext, base, count, west, east, south, north):
    blank = jnp.zeros((128 - HALO * count, N + 2), F32)
    from_west = jnp.concatenate([west[...], blank], axis=0).T
    from_east = jnp.concatenate([east[...], blank], axis=0).T
    blank = jnp.zeros((128 - HALO * count, 128), F32)
    low = jnp.concatenate([south[:, 256:384], blank], axis=0).T
    high = jnp.concatenate([north[:, 256:384], blank], axis=0).T
    at = N - 256
    for f in range(count):
        s = slice(HALO * f, HALO * f + HALO)
        field = ext.at[base + f]
        field[2, TOP : TOP + N + 2, 128 - HALO : 128] = from_west[:, s]
        field[2, TOP : TOP + N + 2, at : at + HALO] = from_east[:, s]
        for first, rows, block in ((TOP - HALO, south, low), (TOP + N, north, high)):
            for j, width in BLOCKS:
                field[j, first : first + HALO, 0:width] = rows[s, 128 * j : 128 * j + width]
            field[2, first : first + HALO, 128 - HALO : 128] = block[at : at + HALO, s]
            field[2, first : first + HALO, at : at + HALO] = block[at + HALO : at + 2 * HALO, s]


def from_east(block):
    lane = lax.broadcasted_iota(I32, (8, 128), 1)
    return lambda j: pltpu.roll(jnp.where(lane == 0, block((j + 1) % 3), block(j)), 127, 1)


def from_west(block):
    lane = lax.broadcasted_iota(I32, (8, 128), 1)
    return lambda j: pltpu.roll(jnp.where(lane == 127, block((j + 2) % 3), block(j)), 1, 1)


def stencil(src, b, coef, take):
    rows = pl.ds(b, 8)
    for j in range(3):
        center, east, west, north, south, mix = coef(j)
        for t in range(2):
            fields = [src.at[t * LEV + k] for k in range(LEV)]
            level = [field[j, rows, :] for field in fields]
            flux = [mix * (level[k] - level[k + 1]) for k in range(LEV - 1)]
            result = []
            for k in range(LEV):
                block = lambda i, field=fields[k]: field[i, rows, :]
                new = center * level[k] + east * from_east(block)(j) + west * from_west(block)(j)
                up = fields[k][j, pl.ds(b + 1, 8), :]
                down = fields[k][j, pl.ds(b - 1, 8), :]
                new = new + (north * up + south * down)
                if k > 0:
                    new = new + flux[k - 1]
                if k < LEV - 1:
                    new = new - flux[k]
                result.append(new)
            take(t, j, level, result)


def store_levels(out, t, j, values, i, rows):
    width = BLOCKS[j][1]
    block = jnp.swapaxes(jnp.stack(values), 0, 1)
    out[t, pl.ds(8 * i, rows), :, 128 * j : 128 * j + width] = block[0:rows, :, 0:width]


def adjoint_kernel(
    wet, labels, zd, zf, md, mf, vm, forcing, adjoint, west, east, south, north,
    initial, forward_coef, keep, give,
    ext, other, coef, surface, coarse, piece,
):
    views = [zd, zf, md, mf, vm]
    full = wet_field(wet, N + 2, 0)
    for j, width in BLOCKS:
        ext[0, j, TOP : TOP + N + 2, :] = full[:, 128 * j : 128 * j + 128]
        for f in range(1, 6):
            ext[f, j, TOP : TOP + N, 0:width] = views[f - 1][:, 128 * j : 128 * j + width]

    def lines(at, start):
        for base, ref, depth in ((6, forcing, 2), (8, adjoint.at[0], LEV), (8 + LEV, adjoint.at[1], LEV)):
            block = jnp.swapaxes(ref[pl.ds(start, 8)], 0, 1)
            for k in range(depth):
                for j, width in BLOCKS:
                    ext[base + k, j, at, 0:width] = block[k, :, 128 * j : 128 * j + width]

    @pl.loop(0, N // 8)
    def _(g):
        lines(pl.ds(aligned(TOP + 8 * g), 8), 8 * g)

    lines(slice(TOP + N - 8, TOP + N), N - 8)
    insert_halos(ext, 0, 16, west, east, south, north)

    @pl.loop(1, CHUNKS + 2)
    def _(r):
        b = aligned(r * 8)
        rows = pl.ds(b, 8)
        faces = []
        wets = [ext[0, j, rows, :] for j in range(3)]
        for j in range(3):
            w, z_d, z_f, m_d, m_f, v = [ext[f, j, rows, :] for f in range(6)]
            east_open = w * from_east(wets.__getitem__)(j)
            north_open = w * ext[0, j, pl.ds(b + 1, 8), :]
            de = z_d * east_open
            ue = 0.5 * z_f * east_open
            dn = m_d * north_open
            vn = 0.5 * m_f * north_open
            faces.append((de + ue, ue - de))
            coef[0, j, rows, :] = de + ue
            coef[2, j, rows, :] = dn + vn
            forward_coef[1, j, rows, :] = de - ue
            forward_coef[3, j, rows, :] = dn - vn
            forward_coef[5, j, rows, :] = v * w
            forward_coef[6, j, rows, :] = ext[6, j, rows, :] * w
            forward_coef[7, j, rows, :] = ext[7, j, rows, :] * w
        for j in range(3):
            ea_west = from_west(lambda i: faces[i][0])(j)
            eb_west = from_west(lambda i: faces[i][1])(j)
            na_south = coef[2, j, pl.ds(b - 1, 8), :]
            minus_nb_south = forward_coef[3, j, pl.ds(b - 1, 8), :]
            forward_coef[0, j, rows, :] = 1.0 + (
                (eb_west - faces[j][0]) - (minus_nb_south + coef[2, j, rows, :])
            )
            forward_coef[2, j, rows, :] = ea_west
            forward_coef[4, j, rows, :] = na_south
            coef[1, j, rows, :] = -eb_west
            coef[3, j, rows, :] = minus_nb_south

    def load_coef(b):
        rows = pl.ds(b, 8)
        return lambda j: (
            [forward_coef[0, j, rows, :]]
            + [coef[i, j, rows, :] for i in range(4)]
            + [forward_coef[5, j, rows, :]]
        )

    lam = ext.at[pl.ds(8, 8)]

    def step(src, dst, first):
        @pl.loop(0, CHUNKS // 2 + 1)
        def _(r):
            for u in range(2):
                b = aligned(r * 16 + 8 * u + 8)
                rows = pl.ds(b, 8)

                def take(t, j, old, new):
                    for k in range(LEV):
                        dst[t * LEV + k, j, rows, :] = new[k]
                    surface[t, j, rows, :] = old[0] if first else surface[t, j, rows, :] + old[0]

                stencil(src, b, load_coef(b), take)

    step(lam, other, True)
    step(other, lam, False)

    def finish(i, count):
        b = aligned(TOP + 8 * i)
        rows = pl.ds(b, 8)

        def take(t, j, old, new):
            w = ext[0, j, rows, :]
            store_levels(initial, t, j, [w * value for value in new], i, count)
            surface[t, j, rows, :] = w * (surface[t, j, rows, :] + old[0])

        stencil(lam, b, load_coef(b), take)

    @pl.loop(0, N // 16)
    def _(i):
        finish(2 * i, 8)
        finish(2 * i + 1, 8)

    finish(N // 8 - 1, 8)
    finish(N // 8, N % 8)

    BF = jnp.bfloat16

    def parts(x):
        hi = x.astype(BF)
        rest = x - hi.astype(F32)
        mid = rest.astype(BF)
        return hi, mid, (rest - mid.astype(F32)).astype(BF)

    def band(shape, out_axis):
        i = lax.broadcasted_iota(I32, shape, out_axis) * 3
        j = lax.broadcasted_iota(I32, shape, 1 - out_axis)
        return ((j >= i) & (j < i + 3) & (j < N)).astype(F32).astype(BF)

    by_row = band((96, N + 2), 0)
    by_lane = band((LANES, 128), 1)
    shape = (N + 2, 128)
    for t in range(2):
        full = jnp.zeros((96, 128), F32)
        for j, width in BLOCKS:
            inside = (lax.broadcasted_iota(I32, shape, 0) < N) & (
                lax.broadcasted_iota(I32, shape, 1) < width
            )
            cells = jnp.where(inside, surface[t, j, TOP : TOP + N + 2, :], 0.0)
            half = sum(jnp.dot(by_row, p, preferred_element_type=F32) for p in parts(cells))
            for p in parts(half):
                full += jnp.dot(p, by_lane[128 * j : 128 * j + 128], preferred_element_type=F32)
        coarse[t] = full / 9.0
    owners = keep.shape[0] // 4
    here = lax.axis_index("lat")
    keep[...] = jnp.zeros(keep.shape, F32)
    give[...] = jnp.zeros(give.shape, F32)
    piece[...] = jnp.zeros((16, 128), F32)
    part = COARSE // 2
    for r in range(SIDE):
        for c in range(SIDE):
            for t in range(2):
                for h in range(2):
                    at = COARSE * r + part * h
                    lane = 64 * h + COARSE * t
                    piece[0:part, lane : lane + COARSE] = coarse[
                        t, at : at + part, COARSE * c : COARSE * c + COARSE
                    ]
            label = labels[r, c]
            row = label // owners
            away = row ^ here
            at = ((away & 1) * 2 + (away >> 2)) * owners + label - row * owners

            @pl.when((away & 2) == 0)
            def _():
                keep[at] = piece[...]

            @pl.when((away & 2) != 0)
            def _():
                give[at] = piece[...]


def adjoint_window(wet, labels, zd, zf, md, mf, vm, forcing, adjoint, west, east, south, north, owners):
    return pl.pallas_call(
        adjoint_kernel,
        out_shape=(
            jax.ShapeDtypeStruct((2, N, LEV, N), F32),
            jax.ShapeDtypeStruct((8, 3, ROWS, 128), F32),
            jax.ShapeDtypeStruct((4 * owners, 16, 128), F32),
            jax.ShapeDtypeStruct((4 * owners, 16, 128), F32),
        ),
        in_specs=[SMEM, SMEM] + [VMEM] * 11,
        out_specs=(VMEM,) * 4,
        scratch_shapes=[
            pltpu.VMEM((16, 3, ROWS, 128), F32),
            pltpu.VMEM((8, 3, ROWS, 128), F32),
            pltpu.VMEM((4, 3, ROWS, 128), F32),
            pltpu.VMEM((2, 3, ROWS, 128), F32),
            pltpu.VMEM((2, 96, 128), F32),
            pltpu.VMEM((16, 128), F32),
        ],
        name="adjoint_window",
    )(wet, labels, zd, zf, md, mf, vm, forcing, adjoint, west, east, south, north)


def unpack_kernel(arrived, state, west, east, south, north, tags, slot_of, tiles, lined, tag_sem, tile_sem):
    sources = arrived.shape[0]
    copy = pltpu.make_async_copy(
        arrived.at[:, :, pl.ds(0, 1), pl.ds(TAIL, 128)], tags, tag_sem
    )
    copy.start()
    places = SIDE * SIDE

    @pl.loop(0, places)
    def _(p):
        slot_of[p] = -1

    copy.wait()

    @pl.loop(0, sources * PAIR)
    def _(i):
        source = i // PAIR
        place = tags[source, i - source * PAIR, 0, TAG].astype(I32)

        @pl.when(place >= 0)
        def _():
            slot_of[place] = i

    def fetch(p):
        slot = slot_of[p]
        source = slot // PAIR
        return pltpu.make_async_copy(arrived.at[source, slot - source * PAIR], tiles.at[p], tile_sem.at[p])

    @pl.loop(0, places)
    def _(p):
        @pl.when(slot_of[p] >= 0)
        def _():
            fetch(p).start()

        @pl.when(slot_of[p] < 0)
        def _():
            tiles[p] = jnp.zeros((8, FLAT), F32)

    @pl.loop(0, SIDE)
    def _(r):
        for c in range(SIDE):

            @pl.when(slot_of[r * SIDE + c] >= 0)
            def _():
                fetch(r * SIDE + c).wait()

        for y in range(TILE):
            for c in range(SIDE):
                lined[r * TILE + y, :, TILE * c : TILE * c + TILE] = tiles[
                    r * SIDE + c, :, TILE * y : TILE * y + TILE
                ]

    @pl.loop(0, CHUNKS)
    def _(g):
        block = jnp.swapaxes(lined[pl.ds(8 * g, 8)], 0, 1)
        for j in range(3):
            state[:, j, pl.ds(aligned(TOP + 8 * g), 8), :] = block[:, :, 128 * j : 128 * j + 128]

    west[...] = strip_columns(lambda f: state[f, 0, TOP : TOP + N + 2, :], 8, 0)
    east[...] = strip_columns(lambda f: state[f, 2, TOP : TOP + N + 2, :], 8, N - HALO - 256)
    for f in range(8):
        for j, width in BLOCKS:
            lanes = slice(128 * j, 128 * j + width)
            rows = slice(HALO * f, HALO * f + HALO)
            south[rows, lanes] = state[f, j, TOP : TOP + HALO, 0:width]
            north[rows, lanes] = state[f, j, TOP + N - HALO : TOP + N, 0:width]


def unpack_tiles(arrived):
    strip = jax.ShapeDtypeStruct((24, N + 2), F32)
    return pl.pallas_call(
        unpack_kernel,
        out_shape=(jax.ShapeDtypeStruct((8, 3, ROWS, 128), F32),) + (strip,) * 4,
        in_specs=[ANY],
        out_specs=(VMEM,) * 5,
        scratch_shapes=[
            pltpu.SMEM((arrived.shape[0], PAIR, 1, 128), F32),
            pltpu.SMEM((SIDE * SIDE,), I32),
            pltpu.VMEM((SIDE * SIDE, 8, FLAT), F32),
            pltpu.VMEM((8 * CHUNKS, 8, LANES), F32),
            pltpu.SemaphoreType.DMA,
            pltpu.SemaphoreType.DMA((SIDE * SIDE,)),
        ],
        name="unpack_tiles",
    )(arrived)


def forward_kernel(state, coef, west, east, south, north, final, first, second, sem):
    copy = pltpu.make_async_copy(state, first, sem)
    copy.start()
    copy.wait()
    insert_halos(first, 0, 8, west, east, south, north)

    def load_coef(b):
        rows = pl.ds(b, 8)
        return lambda j: [coef[i, j, rows, :] for i in range(6)]

    def step(src, dst):
        @pl.loop(0, CHUNKS // 2 + 1)
        def _(r):
            for u in range(2):
                b = aligned(r * 16 + 8 * u + 8)
                rows = pl.ds(b, 8)

                def take(t, j, old, new):
                    dst[t * LEV, j, rows, :] = new[0] + coef[6 + t, j, rows, :]
                    for k in range(1, LEV):
                        dst[t * LEV + k, j, rows, :] = new[k]

                stencil(src, b, load_coef(b), take)

    step(first, second)
    step(second, first)

    def finish(i, count):
        b = aligned(TOP + 8 * i)

        def take(t, j, old, new):
            top = new[0] + coef[6 + t, j, pl.ds(b, 8), :]
            store_levels(final, t, j, [top] + new[1:], i, count)

        stencil(first, b, load_coef(b), take)

    @pl.loop(0, N // 16)
    def _(i):
        finish(2 * i, 8)
        finish(2 * i + 1, 8)

    finish(N // 8 - 1, 8)
    finish(N // 8, N % 8)


def forward_window(state, coef, west, east, south, north):
    return pl.pallas_call(
        forward_kernel,
        out_shape=jax.ShapeDtypeStruct((2, N, LEV, N), F32),
        in_specs=[ANY] + [VMEM] * 5,
        out_specs=VMEM,
        scratch_shapes=[
            pltpu.VMEM((8, 3, ROWS, 128), F32),
            pltpu.VMEM((8, 3, ROWS, 128), F32),
            pltpu.SemaphoreType.DMA,
        ],
        name="forward_window",
    )(state, coef, west, east, south, north)


def neighbours(low, high, axis, periodic):
    count = lax.axis_size(axis)
    up = [(i, i + 1) for i in range(count - 1)] + ([(count - 1, 0)] if periodic else [])
    down = [(b, a) for a, b in up]
    return lax.ppermute(high, axis, up), lax.ppermute(low, axis, down)


def per_device(
    stored_tiles, stored_ids, wet_tiles, control_map, zonal_diffusivity, meridional_diffusivity,
    zonal_flow, meridional_flow, vertical_mixing, forcing, final_adjoint,
):
    owners = lax.axis_size("lon")
    fields = (
        zonal_diffusivity, zonal_flow, meridional_diffusivity, meridional_flow, vertical_mixing,
        forcing.transpose(1, 0, 2), final_adjoint.transpose(0, 2, 1, 3),
    )
    low, high, bottom, top = edge_strips(wet_tiles, *fields)
    west, east = neighbours(low, high, "lon", True)
    outgoing = pack_tiles(stored_ids, stored_tiles, low, owners)
    outgoing, west, east = lax.optimization_barrier((outgoing, west, east))
    arrived = lax.all_to_all(outgoing, "lon", split_axis=0, concat_axis=0, tiled=True)
    south, north = neighbours(*with_corners(bottom, top, west, east), "lat", False)
    initial, coef, keep, give = adjoint_window(
        wet_tiles, control_map, *fields, west, east, south, north, owners
    )
    for bit in (2, 1, 4):
        keep = keep + lax.ppermute(give, "lat", [(i, i ^ bit) for i in range(lax.axis_size("lat"))])
        half = keep.shape[0] // 2
        if bit != 4:
            keep, give = keep[:half], keep[half:]
    gathered = lax.all_to_all(keep, "lon", split_axis=0, concat_axis=0, tiled=True)
    total = jnp.sum(gathered, axis=0)[: COARSE // 2]
    total = jnp.stack([total[:, :60], total[:, 64:124]]).reshape(2, COARSE // 2, 2, COARSE)
    control = total.transpose(2, 0, 1, 3).reshape(1, 2, COARSE * COARSE)

    state, low, high, bottom, top = unpack_tiles(arrived)
    west, east = neighbours(low, high, "lon", True)
    south, north = neighbours(*with_corners(bottom, top, west, east), "lat", False)
    final = forward_window(state, coef, west, east, south, north)
    return final.transpose(0, 2, 1, 3), initial.transpose(0, 2, 1, 3), control


def solution(mesh):
    grid = P("lat", "lon")
    return jax.shard_map(
        per_device,
        mesh=mesh,
        in_specs=(
            P(("lat", "lon"), None, None), P(("lat", "lon")), grid, grid, grid, grid, grid, grid, grid,
            P(None, "lat", "lon"), P(None, None, "lat", "lon"),
        ),
        out_specs=(
            P(None, None, "lat", "lon"), P(None, None, "lat", "lon"), P(("lat", "lon"), None, None),
        ),
        check_vma=False,
    )
```

```python
import functools

import jax
import jax.numpy as jnp
from jax import lax
from jax.experimental import pallas as pl
from jax.experimental.pallas import tpu as pltpu
from jax.sharding import PartitionSpec as P


F32 = jnp.float32
I32 = jnp.int32
TILE = 90
SIDE = 3
COLUMNS = 48
HALO = 3
SLOTS = 27
PAIR = 2
LEV = 4
CELLS = TILE * TILE
N = TILE * SIDE
FLAT = 8192
TAIL = 8064
TAG = CELLS - TAIL
TOP = 16
ROWS = 304
LANES = 384
BLOCKS = ((0, 128), (1, 128), (2, N - 256))
CHUNKS = 34
COARSE = 30
VMEM = pl.BlockSpec(memory_space=pltpu.VMEM)
SMEM = pl.BlockSpec(memory_space=pltpu.SMEM)
ANY = pl.BlockSpec(memory_space=pl.ANY)


def aligned(x):
    return pl.multiple_of(x, 8)


def pack_kernel(ids, stored, after, out, held, tail, empty, count, route, in_sem, out_sem, tail_sem, empty_sem):
    owners = out.shape[0]

    def fetch(s):
        return pltpu.make_async_copy(stored.at[s], held.at[s], in_sem.at[s])

    def send(s, owner, rank):
        return pltpu.make_async_copy(
            held.at[s, :, pl.ds(0, TAIL)], out.at[owner, rank, :, pl.ds(0, TAIL)], out_sem.at[s]
        )

    def send_tail(s, owner, rank):
        return pltpu.make_async_copy(
            tail.at[s], out.at[owner, rank, :, pl.ds(TAIL, 128)], tail_sem.at[s]
        )

    def send_empty(owner, rank):
        return pltpu.make_async_copy(
            empty, out.at[owner, rank, :, pl.ds(TAIL, 128)], empty_sem.at[owner, rank]
        )

    @pl.loop(0, SLOTS)
    def _(s):
        @pl.when(ids[s] >= 0)
        def _():
            fetch(s).start()

    @pl.loop(0, owners)
    def _(o):
        count[o] = 0

    empty[...] = jnp.full((8, 128), -1.0, F32)
    lane = lax.broadcasted_iota(I32, (8, 128), 1)

    @pl.loop(0, SLOTS)
    def _(s):
        tile = ids[s]

        @pl.when(tile >= 0)
        def _():
            row = tile // COLUMNS
            column = tile - row * COLUMNS
            owner = column // SIDE
            rank = count[owner]
            count[owner] = rank + 1
            route[s] = owner * PAIR + rank
            place = row * SIDE + column - owner * SIDE
            fetch(s).wait()
            last = jnp.concatenate([held[s, :, TAIL:CELLS], jnp.zeros((8, 128 - TAG), F32)], axis=1)
            tail[s] = jnp.where(lane < TAG, last, place.astype(F32))
            send(s, owner, rank).start()
            send_tail(s, owner, rank).start()

    for rank in range(PAIR):

        @pl.loop(0, owners)
        def _(o):
            @pl.when(count[o] <= rank)
            def _():
                send_empty(o, rank).start()

    @pl.loop(0, SLOTS)
    def _(s):
        @pl.when(ids[s] >= 0)
        def _():
            owner = route[s] // PAIR
            rank = route[s] - owner * PAIR
            send(s, owner, rank).wait()
            send_tail(s, owner, rank).wait()

    for rank in range(PAIR):

        @pl.loop(0, owners)
        def _(o):
            @pl.when(count[o] <= rank)
            def _():
                send_empty(o, rank).wait()


def pack_tiles(ids, stored, after, owners):
    return pl.pallas_call(
        pack_kernel,
        out_shape=jax.ShapeDtypeStruct((owners, PAIR, 8, FLAT), F32),
        in_specs=[SMEM, ANY, ANY],
        out_specs=ANY,
        scratch_shapes=[
            pltpu.VMEM((SLOTS, 8, CELLS), F32),
            pltpu.VMEM((SLOTS, 8, 128), F32),
            pltpu.VMEM((8, 128), F32),
            pltpu.SMEM((owners,), I32),
            pltpu.SMEM((SLOTS,), I32),
            pltpu.SemaphoreType.DMA((SLOTS,)),
            pltpu.SemaphoreType.DMA((SLOTS,)),
            pltpu.SemaphoreType.DMA((SLOTS,)),
            pltpu.SemaphoreType.DMA((owners, PAIR)),
        ],
        name="pack_tiles",
    )(ids, stored, after)


def split_kernel(ids, stored, after, first, own, cross, held, tail, empty, count, route, filled, in_sem, out_sem, tail_sem, empty_sem):
    owners = first.shape[0]
    chips = own.shape[0]
    me = lax.axis_index("lon")
    outs = [(first, owners), (own, chips), (cross, chips)]

    def fetch(s):
        return pltpu.make_async_copy(stored.at[s], held.at[s], in_sem.at[s])

    def each(s, act):
        for kind, (out, _) in enumerate(outs):

            @pl.when(route[s, 0] == kind)
            def _():
                to = out.at[route[s, 1]]
                act(pltpu.make_async_copy(held.at[s, :, pl.ds(0, TAIL)], to.at[:, pl.ds(0, TAIL)], out_sem.at[s]))
                act(pltpu.make_async_copy(tail.at[s], to.at[:, pl.ds(TAIL, 128)], tail_sem.at[s]))

    def each_empty(act):
        for kind, (out, size) in enumerate(outs):

            @pl.loop(0, size)
            def _(i):
                @pl.when(filled[kind, i] == 0)
                def _():
                    act(
                        pltpu.make_async_copy(
                            empty, out.at[i, :, pl.ds(TAIL, 128)], empty_sem.at[kind, i]
                        )
                    )

    @pl.loop(0, SLOTS)
    def _(s):
        @pl.when(ids[s] >= 0)
        def _():
            fetch(s).start()

    @pl.loop(0, owners)
    def _(o):
        count[o] = 0
        for kind in range(3):
            filled[kind, o] = 0

    empty[...] = jnp.full((8, 128), -1.0, F32)
    lane = lax.broadcasted_iota(I32, (8, 128), 1)

    @pl.loop(0, SLOTS)
    def _(s):
        tile = ids[s]

        @pl.when(tile >= 0)
        def _():
            row = tile // COLUMNS
            column = tile - row * COLUMNS
            owner = column // SIDE
            rank = count[owner]
            count[owner] = rank + 1
            away = owner ^ me
            kind = jnp.where(rank == 0, 0, 1 + (away & 1))
            index = jnp.where(rank == 0, owner, away >> 1)
            route[s, 0] = kind
            route[s, 1] = index
            filled[kind, index] = 1
            place = row * SIDE + column - owner * SIDE
            fetch(s).wait()
            last = jnp.concatenate([held[s, :, TAIL:CELLS], jnp.zeros((8, 128 - TAG), F32)], axis=1)
            tail[s] = jnp.where(lane < TAG, last, place.astype(F32))
            each(s, lambda copy: copy.start())

    each_empty(lambda copy: copy.start())

    @pl.loop(0, SLOTS)
    def _(s):
        @pl.when(ids[s] >= 0)
        def _():
            each(s, lambda copy: copy.wait())

    each_empty(lambda copy: copy.wait())


def split_tiles(ids, stored, after, owners):
    chips = owners // 2
    return pl.pallas_call(
        split_kernel,
        out_shape=tuple(jax.ShapeDtypeStruct((n, 8, FLAT), F32) for n in (owners, chips, chips)),
        in_specs=[SMEM, ANY, ANY],
        out_specs=(ANY,) * 3,
        scratch_shapes=[
            pltpu.VMEM((SLOTS, 8, CELLS), F32),
            pltpu.VMEM((SLOTS, 8, 128), F32),
            pltpu.VMEM((8, 128), F32),
            pltpu.SMEM((owners,), I32),
            pltpu.SMEM((SLOTS, 2), I32),
            pltpu.SMEM((3, owners), I32),
            pltpu.SemaphoreType.DMA((SLOTS,)),
            pltpu.SemaphoreType.DMA((SLOTS,)),
            pltpu.SemaphoreType.DMA((SLOTS,)),
            pltpu.SemaphoreType.DMA((3, owners)),
        ],
        name="split_tiles",
    )(ids, stored, after)


def merge_kernel(own, cross, *refs):
    chips = own.shape[0]
    outs = refs[:chips]
    clash, held, empty, own_tags, cross_tags, sem, in_sem, out_sem = refs[chips:]
    copies = [
        pltpu.make_async_copy(x.at[:, pl.ds(0, 1), pl.ds(TAIL, 128)], tags, sem.at[i])
        for i, (x, tags) in enumerate(((own, own_tags), (cross, cross_tags)))
    ]
    for copy in copies:
        copy.start()
    empty[...] = jnp.full((8, 128), -1.0, F32)
    for copy in copies:
        copy.wait()
    total = jnp.int32(0)
    has = []
    for c in range(chips):
        mine = own_tags[c, 0, TAG] >= 0
        other = cross_tags[c, 0, TAG] >= 0
        total = total + jnp.where(mine & other, 1, 0)
        has.append((mine, other))
    clash[0] = total

    def filling(c, act):
        mine, other = has[c]

        @pl.when(mine)
        def _():
            act(pltpu.make_async_copy(own.at[c], held.at[c], in_sem.at[c]))

        @pl.when(other & ~mine)
        def _():
            act(pltpu.make_async_copy(cross.at[c], held.at[c], in_sem.at[c]))

    def leaving(c, act):
        mine, other = has[c]

        @pl.when(mine | other)
        def _():
            act(pltpu.make_async_copy(held.at[c], outs[c], out_sem.at[c]))

        @pl.when(~(mine | other))
        def _():
            act(pltpu.make_async_copy(empty, outs[c].at[:, pl.ds(TAIL, 128)], out_sem.at[c]))

    for c in range(chips):
        filling(c, lambda copy: copy.start())
    for c in range(chips):
        filling(c, lambda copy: copy.wait())
        leaving(c, lambda copy: copy.start())
    for c in range(chips):
        leaving(c, lambda copy: copy.wait())


def merge_tiles(own, cross):
    chips = own.shape[0]
    return pl.pallas_call(
        merge_kernel,
        out_shape=(jax.ShapeDtypeStruct((8, FLAT), F32),) * chips + (jax.ShapeDtypeStruct((1,), I32),),
        in_specs=[ANY, ANY],
        out_specs=(ANY,) * chips + (SMEM,),
        scratch_shapes=[
            pltpu.VMEM((chips, 8, FLAT), F32),
            pltpu.VMEM((8, 128), F32),
            pltpu.SMEM((chips, 1, 128), F32),
            pltpu.SMEM((chips, 1, 128), F32),
            pltpu.SemaphoreType.DMA((2,)),
            pltpu.SemaphoreType.DMA((chips,)),
            pltpu.SemaphoreType.DMA((chips,)),
        ],
        name="merge_tiles",
    )(own, cross)


def strip_columns(load, count, first):
    lane = lax.broadcasted_iota(I32, (N + 2, 128), 1)
    strip = jnp.zeros((N + 2, 128), F32)
    for f in range(count):
        moved = pltpu.roll(load(f), (HALO * f - first) % 128, 1)
        strip = jnp.where((lane >= HALO * f) & (lane < HALO * f + HALO), moved, strip)
    return strip.T[0 : HALO * count]


def wet_field(wet, rows, row0):
    row = lax.broadcasted_iota(I32, (rows, LANES), 0) + row0
    lane = lax.broadcasted_iota(I32, (rows, LANES), 1)
    bands = []
    for r in range(SIDE):
        w = [wet[r, c].astype(F32) for c in range(SIDE)]
        bands.append(jnp.where(lane < TILE, w[0], jnp.where(lane < 2 * TILE, w[1], w[2])))
    return jnp.where(row < TILE, bands[0], jnp.where(row < 2 * TILE, bands[1], bands[2]))


def edges_kernel(wet, zd, zf, md, mf, vm, forcing, adjoint, west, east, south, north, held):
    views = [zd, zf, md, mf, vm]
    full = wet_field(wet, N + 2, 0)
    held[0, 0] = full[:, 0:128]
    held[1, 0] = full[:, 256:384]
    south[0:HALO, 0:N] = full[0:HALO, 0:N]
    north[0:HALO, 0:N] = full[N - HALO : N, 0:N]
    for f in range(1, 6):
        ref = views[f - 1]
        south[HALO * f : HALO * f + HALO, 0:N] = ref[0:HALO, :]
        north[HALO * f : HALO * f + HALO, 0:N] = ref[N - HALO : N, :]
        held[0, f, 0:N, :] = ref[:, 0:128]
        held[1, f, 0:N, 0 : N - 256] = ref[:, 256:N]
    for out, first in ((south, 0), (north, N - HALO)):
        for y in range(HALO):
            row = forcing[first + y]
            for f in range(2):
                out[HALO * (6 + f) + y, 0:N] = row[f]
            for t in range(2):
                row = adjoint[t, first + y]
                for k in range(LEV):
                    out[HALO * (8 + LEV * t + k) + y, 0:N] = row[k]

    def lines(at, start):
        for side, width in ((0, 128), (1, N - 256)):
            lanes = slice(256 * side, 256 * side + width)
            for base, ref, depth in ((6, forcing, 2), (8, adjoint.at[0], LEV), (8 + LEV, adjoint.at[1], LEV)):
                block = jnp.swapaxes(ref[pl.ds(start, 8), :, lanes], 0, 1)
                for k in range(depth):
                    held[side, base + k, at, 0:width] = block[k]

    @pl.loop(0, N // 8)
    def _(g):
        lines(pl.ds(aligned(8 * g), 8), 8 * g)

    lines(slice(N - 8, N), N - 8)

    def low(f):
        return held[0, f]

    def high(f):
        return held[1, f]

    west[...] = strip_columns(low, 16, 0)
    east[...] = strip_columns(high, 16, N - HALO - 256)


def edge_strips(wet, zd, zf, md, mf, vm, forcing, adjoint):
    columns = jax.ShapeDtypeStruct((48, N + 2), F32)
    rows = jax.ShapeDtypeStruct((48, N + 2), F32)
    return pl.pallas_call(
        edges_kernel,
        out_shape=(columns, columns, rows, rows),
        in_specs=[SMEM] + [VMEM] * 7,
        out_specs=(VMEM,) * 4,
        scratch_shapes=[pltpu.VMEM((2, 16, N + 2, 128), F32)],
        name="edge_strips",
    )(wet, zd, zf, md, mf, vm, forcing, adjoint)


def corners_kernel(south, north, west, east, to_south, to_north):
    for rows, out, first in ((south, to_south, 0), (north, to_north, N - HALO)):
        out[:, 0:N] = rows[:, 0:N]
        out[:, N : N + HALO] = west[:, first : first + HALO]
        out[:, N + HALO : N + 2 * HALO] = east[:, first : first + HALO]


def with_corners(south, north, west, east):
    shape = jax.ShapeDtypeStruct((south.shape[0], LANES), F32)
    return pl.pallas_call(
        corners_kernel,
        out_shape=(shape, shape),
        in_specs=[VMEM] * 4,
        out_specs=(VMEM,) * 2,
        name="row_strips",
    )(south, north, west, east)


def insert_halos(ext, base, count, west, east, south, north):
    blank = jnp.zeros((128 - HALO * count, N + 2), F32)
    from_west = jnp.concatenate([west[...], blank], axis=0).T
    from_east = jnp.concatenate([east[...], blank], axis=0).T
    blank = jnp.zeros((128 - HALO * count, 128), F32)
    low = jnp.concatenate([south[:, 256:384], blank], axis=0).T
    high = jnp.concatenate([north[:, 256:384], blank], axis=0).T
    at = N - 256
    for f in range(count):
        s = slice(HALO * f, HALO * f + HALO)
        field = ext.at[base + f]
        field[2, TOP : TOP + N + 2, 128 - HALO : 128] = from_west[:, s]
        field[2, TOP : TOP + N + 2, at : at + HALO] = from_east[:, s]
        for first, rows, block in ((TOP - HALO, south, low), (TOP + N, north, high)):
            for j, width in BLOCKS:
                field[j, first : first + HALO, 0:width] = rows[s, 128 * j : 128 * j + width]
            field[2, first : first + HALO, 128 - HALO : 128] = block[at : at + HALO, s]
            field[2, first : first + HALO, at : at + HALO] = block[at + HALO : at + 2 * HALO, s]


def from_east(block):
    lane = lax.broadcasted_iota(I32, (8, 128), 1)
    return lambda j: pltpu.roll(jnp.where(lane == 0, block((j + 1) % 3), block(j)), 127, 1)


def from_west(block):
    lane = lax.broadcasted_iota(I32, (8, 128), 1)
    return lambda j: pltpu.roll(jnp.where(lane == 127, block((j + 2) % 3), block(j)), 1, 1)


def stencil(src, b, coef, take):
    rows = pl.ds(b, 8)
    for j in range(3):
        center, east, west, north, south, mix = coef(j)
        for t in range(2):
            fields = [src.at[t * LEV + k] for k in range(LEV)]
            level = [field[j, rows, :] for field in fields]
            flux = [mix * (level[k] - level[k + 1]) for k in range(LEV - 1)]
            result = []
            for k in range(LEV):
                block = lambda i, field=fields[k]: field[i, rows, :]
                new = center * level[k] + east * from_east(block)(j) + west * from_west(block)(j)
                up = fields[k][j, pl.ds(b + 1, 8), :]
                down = fields[k][j, pl.ds(b - 1, 8), :]
                new = new + (north * up + south * down)
                if k > 0:
                    new = new + flux[k - 1]
                if k < LEV - 1:
                    new = new - flux[k]
                result.append(new)
            take(t, j, level, result)


def store_levels(out, t, j, values, i, rows):
    width = BLOCKS[j][1]
    block = jnp.swapaxes(jnp.stack(values), 0, 1)
    out[t, pl.ds(8 * i, rows), :, 128 * j : 128 * j + width] = block[0:rows, :, 0:width]


def adjoint_kernel(
    wet, labels, clash, zd, zf, md, mf, vm, forcing, adjoint, west, east, south, north,
    initial, forward_coef, keep, give,
    ext, other, coef, surface, coarse, piece,
):
    views = [zd, zf, md, mf, vm]
    full = wet_field(wet, N + 2, 0)
    for j, width in BLOCKS:
        ext[0, j, TOP : TOP + N + 2, :] = full[:, 128 * j : 128 * j + 128]
        for f in range(1, 6):
            ext[f, j, TOP : TOP + N, 0:width] = views[f - 1][:, 128 * j : 128 * j + width]

    def lines(at, start):
        for base, ref, depth in ((6, forcing, 2), (8, adjoint.at[0], LEV), (8 + LEV, adjoint.at[1], LEV)):
            block = jnp.swapaxes(ref[pl.ds(start, 8)], 0, 1)
            for k in range(depth):
                for j, width in BLOCKS:
                    ext[base + k, j, at, 0:width] = block[k, :, 128 * j : 128 * j + width]

    @pl.loop(0, N // 8)
    def _(g):
        lines(pl.ds(aligned(TOP + 8 * g), 8), 8 * g)

    lines(slice(TOP + N - 8, TOP + N), N - 8)
    insert_halos(ext, 0, 16, west, east, south, north)

    @pl.loop(1, CHUNKS + 2)
    def _(r):
        b = aligned(r * 8)
        rows = pl.ds(b, 8)
        faces = []
        wets = [ext[0, j, rows, :] for j in range(3)]
        for j in range(3):
            w, z_d, z_f, m_d, m_f, v = [ext[f, j, rows, :] for f in range(6)]
            east_open = w * from_east(wets.__getitem__)(j)
            north_open = w * ext[0, j, pl.ds(b + 1, 8), :]
            de = z_d * east_open
            ue = 0.5 * z_f * east_open
            dn = m_d * north_open
            vn = 0.5 * m_f * north_open
            faces.append((de + ue, ue - de))
            coef[0, j, rows, :] = de + ue
            coef[2, j, rows, :] = dn + vn
            forward_coef[1, j, rows, :] = de - ue
            forward_coef[3, j, rows, :] = dn - vn
            forward_coef[5, j, rows, :] = v * w
            forward_coef[6, j, rows, :] = ext[6, j, rows, :] * w
            forward_coef[7, j, rows, :] = ext[7, j, rows, :] * w
        for j in range(3):
            ea_west = from_west(lambda i: faces[i][0])(j)
            eb_west = from_west(lambda i: faces[i][1])(j)
            na_south = coef[2, j, pl.ds(b - 1, 8), :]
            minus_nb_south = forward_coef[3, j, pl.ds(b - 1, 8), :]
            forward_coef[0, j, rows, :] = 1.0 + (
                (eb_west - faces[j][0]) - (minus_nb_south + coef[2, j, rows, :])
            )
            forward_coef[2, j, rows, :] = ea_west
            forward_coef[4, j, rows, :] = na_south
            coef[1, j, rows, :] = -eb_west
            coef[3, j, rows, :] = minus_nb_south

    def load_coef(b):
        rows = pl.ds(b, 8)
        return lambda j: (
            [forward_coef[0, j, rows, :]]
            + [coef[i, j, rows, :] for i in range(4)]
            + [forward_coef[5, j, rows, :]]
        )

    lam = ext.at[pl.ds(8, 8)]

    def step(src, dst, first):
        @pl.loop(0, CHUNKS // 2 + 1)
        def _(r):
            for u in range(2):
                b = aligned(r * 16 + 8 * u + 8)
                rows = pl.ds(b, 8)

                def take(t, j, old, new):
                    for k in range(LEV):
                        dst[t * LEV + k, j, rows, :] = new[k]
                    surface[t, j, rows, :] = old[0] if first else surface[t, j, rows, :] + old[0]

                stencil(src, b, load_coef(b), take)

    step(lam, other, True)
    step(other, lam, False)

    def finish(i, count):
        b = aligned(TOP + 8 * i)
        rows = pl.ds(b, 8)

        def take(t, j, old, new):
            w = ext[0, j, rows, :]
            store_levels(initial, t, j, [w * value for value in new], i, count)
            surface[t, j, rows, :] = w * (surface[t, j, rows, :] + old[0])

        stencil(lam, b, load_coef(b), take)

    @pl.loop(0, N // 16)
    def _(i):
        finish(2 * i, 8)
        finish(2 * i + 1, 8)

    finish(N // 8 - 1, 8)
    finish(N // 8, N % 8)

    BF = jnp.bfloat16

    def parts(x):
        hi = x.astype(BF)
        rest = x - hi.astype(F32)
        mid = rest.astype(BF)
        return hi, mid, (rest - mid.astype(F32)).astype(BF)

    def band(shape, out_axis):
        i = lax.broadcasted_iota(I32, shape, out_axis) * 3
        j = lax.broadcasted_iota(I32, shape, 1 - out_axis)
        return ((j >= i) & (j < i + 3) & (j < N)).astype(F32).astype(BF)

    by_row = band((96, N + 2), 0)
    by_lane = band((LANES, 128), 1)
    shape = (N + 2, 128)
    for t in range(2):
        full = jnp.zeros((96, 128), F32)
        for j, width in BLOCKS:
            inside = (lax.broadcasted_iota(I32, shape, 0) < N) & (
                lax.broadcasted_iota(I32, shape, 1) < width
            )
            cells = jnp.where(inside, surface[t, j, TOP : TOP + N + 2, :], 0.0)
            half = sum(jnp.dot(by_row, p, preferred_element_type=F32) for p in parts(cells))
            for p in parts(half):
                full += jnp.dot(p, by_lane[128 * j : 128 * j + 128], preferred_element_type=F32)
        coarse[t] = full / 9.0
    owners = keep.shape[0] // 4
    here = lax.axis_index("lat")
    last = lax.broadcasted_iota(I32, (16, 128), 0) == 15
    piece[...] = jnp.where(last, clash[0].astype(F32), 0.0)
    keep[...] = jnp.broadcast_to(piece[...], keep.shape)
    give[...] = jnp.broadcast_to(piece[...], give.shape)
    part = COARSE // 2
    for r in range(SIDE):
        for c in range(SIDE):
            for t in range(2):
                for h in range(2):
                    at = COARSE * r + part * h
                    lane = 64 * h + COARSE * t
                    piece[0:part, lane : lane + COARSE] = coarse[
                        t, at : at + part, COARSE * c : COARSE * c + COARSE
                    ]
            label = labels[r, c]
            row = label // owners
            away = row ^ here
            at = ((away & 1) * 2 + (away >> 2)) * owners + label - row * owners

            @pl.when((away & 2) == 0)
            def _():
                keep[at] = piece[...]

            @pl.when((away & 2) != 0)
            def _():
                give[at] = piece[...]


def adjoint_window(wet, labels, clash, zd, zf, md, mf, vm, forcing, adjoint, west, east, south, north, owners):
    return pl.pallas_call(
        adjoint_kernel,
        out_shape=(
            jax.ShapeDtypeStruct((2, N, LEV, N), F32),
            jax.ShapeDtypeStruct((8, 3, ROWS, 128), F32),
            jax.ShapeDtypeStruct((4 * owners, 16, 128), F32),
            jax.ShapeDtypeStruct((4 * owners, 16, 128), F32),
        ),
        in_specs=[SMEM] * 3 + [VMEM] * 11,
        out_specs=(VMEM,) * 4,
        scratch_shapes=[
            pltpu.VMEM((16, 3, ROWS, 128), F32),
            pltpu.VMEM((8, 3, ROWS, 128), F32),
            pltpu.VMEM((4, 3, ROWS, 128), F32),
            pltpu.VMEM((2, 3, ROWS, 128), F32),
            pltpu.VMEM((2, 96, 128), F32),
            pltpu.VMEM((16, 128), F32),
        ],
        name="adjoint_window",
    )(wet, labels, clash, zd, zf, md, mf, vm, forcing, adjoint, west, east, south, north)


def unpack_kernel(extra, first, *refs):
    seconds = refs[:extra]
    state, west, east, south, north, tags, more_tags, present, tiles, lined, tag_sem, tile_sem = refs[extra:]
    slots = first.shape[0]
    copies = [pltpu.make_async_copy(first.at[:, pl.ds(0, 1), pl.ds(TAIL, 128)], tags, tag_sem.at[0])]
    for c, second in enumerate(seconds):
        copies.append(
            pltpu.make_async_copy(second.at[pl.ds(0, 1), pl.ds(TAIL, 128)], more_tags.at[c], tag_sem.at[1 + c])
        )
    for copy in copies:
        copy.start()
    places = SIDE * SIDE

    @pl.loop(0, places)
    def _(p):
        present[p] = 0

    for copy in copies:
        copy.wait()

    def fetch(source, p):
        return pltpu.make_async_copy(source, tiles.at[p], tile_sem.at[p])

    def take(source, tag):
        place = tag.astype(I32)

        @pl.when(place >= 0)
        def _():
            present[place] = 1
            fetch(source, place).start()

    @pl.loop(0, slots)
    def _(i):
        take(first.at[i], tags[i, 0, TAG])

    for c, second in enumerate(seconds):
        take(second, more_tags[c, 0, TAG])

    @pl.loop(0, places)
    def _(p):
        @pl.when(present[p] == 0)
        def _():
            tiles[p] = jnp.zeros((8, FLAT), F32)

    @pl.loop(0, SIDE)
    def _(r):
        for c in range(SIDE):

            @pl.when(present[r * SIDE + c] != 0)
            def _():
                fetch(first.at[0], r * SIDE + c).wait()

        for y in range(TILE):
            for c in range(SIDE):
                lined[r * TILE + y, :, TILE * c : TILE * c + TILE] = tiles[
                    r * SIDE + c, :, TILE * y : TILE * y + TILE
                ]

    @pl.loop(0, CHUNKS)
    def _(g):
        block = jnp.swapaxes(lined[pl.ds(8 * g, 8)], 0, 1)
        for j in range(3):
            state[:, j, pl.ds(aligned(TOP + 8 * g), 8), :] = block[:, :, 128 * j : 128 * j + 128]

    west[...] = strip_columns(lambda f: state[f, 0, TOP : TOP + N + 2, :], 8, 0)
    east[...] = strip_columns(lambda f: state[f, 2, TOP : TOP + N + 2, :], 8, N - HALO - 256)
    for f in range(8):
        for j, width in BLOCKS:
            lanes = slice(128 * j, 128 * j + width)
            rows = slice(HALO * f, HALO * f + HALO)
            south[rows, lanes] = state[f, j, TOP : TOP + HALO, 0:width]
            north[rows, lanes] = state[f, j, TOP + N - HALO : TOP + N, 0:width]


def unpack_tiles(first, *seconds):
    strip = jax.ShapeDtypeStruct((24, N + 2), F32)
    extra = len(seconds)
    return pl.pallas_call(
        functools.partial(unpack_kernel, extra),
        out_shape=(jax.ShapeDtypeStruct((8, 3, ROWS, 128), F32),) + (strip,) * 4,
        in_specs=[ANY] * (1 + extra),
        out_specs=(VMEM,) * 5,
        scratch_shapes=[
            pltpu.SMEM((first.shape[0], 1, 128), F32),
            pltpu.SMEM((8, 1, 128), F32),
            pltpu.SMEM((SIDE * SIDE,), I32),
            pltpu.VMEM((SIDE * SIDE, 8, FLAT), F32),
            pltpu.VMEM((8 * CHUNKS, 8, LANES), F32),
            pltpu.SemaphoreType.DMA((9,)),
            pltpu.SemaphoreType.DMA((SIDE * SIDE,)),
        ],
        name="unpack_tiles",
    )(first, *seconds)


def forward_kernel(state, coef, west, east, south, north, final, first, second, sem):
    copy = pltpu.make_async_copy(state, first, sem)
    copy.start()
    copy.wait()
    insert_halos(first, 0, 8, west, east, south, north)

    def load_coef(b):
        rows = pl.ds(b, 8)
        return lambda j: [coef[i, j, rows, :] for i in range(6)]

    def step(src, dst):
        @pl.loop(0, CHUNKS // 2 + 1)
        def _(r):
            for u in range(2):
                b = aligned(r * 16 + 8 * u + 8)
                rows = pl.ds(b, 8)

                def take(t, j, old, new):
                    dst[t * LEV, j, rows, :] = new[0] + coef[6 + t, j, rows, :]
                    for k in range(1, LEV):
                        dst[t * LEV + k, j, rows, :] = new[k]

                stencil(src, b, load_coef(b), take)

    step(first, second)
    step(second, first)

    def finish(i, count):
        b = aligned(TOP + 8 * i)

        def take(t, j, old, new):
            top = new[0] + coef[6 + t, j, pl.ds(b, 8), :]
            store_levels(final, t, j, [top] + new[1:], i, count)

        stencil(first, b, load_coef(b), take)

    @pl.loop(0, N // 16)
    def _(i):
        finish(2 * i, 8)
        finish(2 * i + 1, 8)

    finish(N // 8 - 1, 8)
    finish(N // 8, N % 8)


def forward_window(state, coef, west, east, south, north):
    return pl.pallas_call(
        forward_kernel,
        out_shape=jax.ShapeDtypeStruct((2, N, LEV, N), F32),
        in_specs=[ANY] + [VMEM] * 5,
        out_specs=VMEM,
        scratch_shapes=[
            pltpu.VMEM((8, 3, ROWS, 128), F32),
            pltpu.VMEM((8, 3, ROWS, 128), F32),
            pltpu.SemaphoreType.DMA,
        ],
        name="forward_window",
    )(state, coef, west, east, south, north)


def neighbours(low, high, axis, periodic):
    count = lax.axis_size(axis)
    up = [(i, i + 1) for i in range(count - 1)] + ([(count - 1, 0)] if periodic else [])
    down = [(b, a) for a, b in up]
    return lax.ppermute(high, axis, up), lax.ppermute(low, axis, down)


def xor_permute(x, axis, bits):
    return lax.ppermute(x, axis, [(i, i ^ bits) for i in range(lax.axis_size(axis))])


def per_device(
    stored_tiles, stored_ids, wet_tiles, control_map, zonal_diffusivity, meridional_diffusivity,
    zonal_flow, meridional_flow, vertical_mixing, forcing, final_adjoint,
):
    owners = lax.axis_size("lon")
    fields = (
        zonal_diffusivity, zonal_flow, meridional_diffusivity, meridional_flow, vertical_mixing,
        forcing.transpose(1, 0, 2), final_adjoint.transpose(0, 2, 1, 3),
    )
    low, high, bottom, top = edge_strips(wet_tiles, *fields)
    west, east = neighbours(low, high, "lon", True)
    first, own, cross = split_tiles(stored_ids, stored_tiles, low, owners)
    first, west, east = lax.optimization_barrier((first, west, east))
    first = lax.all_to_all(first, "lon", split_axis=0, concat_axis=0, tiled=True)
    cross = xor_permute(cross, "lon", 1)
    south, north = neighbours(*with_corners(bottom, top, west, east), "lat", False)
    *seconds, clash = merge_tiles(own, cross)
    seconds = [seconds[0]] + [xor_permute(x, "lon", 2 * c) for c, x in enumerate(seconds) if c > 0]
    initial, coef, keep, give = adjoint_window(
        wet_tiles, control_map, clash, *fields, west, east, south, north, owners
    )
    for bit in (2, 1, 4):
        keep = keep + xor_permute(give, "lat", bit)
        half = keep.shape[0] // 2
        if bit != 4:
            keep, give = keep[:half], keep[half:]
    gathered = lax.all_to_all(keep, "lon", split_axis=0, concat_axis=0, tiled=True)
    total = jnp.sum(gathered, axis=0)
    clashes = total[15, 0]
    total = total[: COARSE // 2]
    total = jnp.stack([total[:, :60], total[:, 64:124]]).reshape(2, COARSE // 2, 2, COARSE)
    control = total.transpose(2, 0, 1, 3).reshape(1, 2, COARSE * COARSE)

    def halos(low, high, bottom, top):
        west, east = neighbours(low, high, "lon", True)
        return (west, east) + neighbours(*with_corners(bottom, top, west, east), "lat", False)

    state, *strips = unpack_tiles(first, *seconds)
    strips = halos(*strips)

    def ready(ids, stored, coef, state, *strips):
        return forward_window(state, coef, *strips)

    def complete(ids, stored, coef, state, *strips):
        outgoing = pack_tiles(ids, stored, coef, owners)
        arrived = lax.all_to_all(outgoing, "lon", split_axis=0, concat_axis=0, tiled=True)
        state, *strips = unpack_tiles(arrived.reshape(owners * PAIR, 8, FLAT))
        return forward_window(state, coef, *halos(*strips))

    final = lax.cond(clashes > 0, complete, ready, stored_ids, stored_tiles, coef, state, *strips)
    return final.transpose(0, 2, 1, 3), initial.transpose(0, 2, 1, 3), control


def solution(mesh):
    grid = P("lat", "lon")
    return jax.shard_map(
        per_device,
        mesh=mesh,
        in_specs=(
            P(("lat", "lon"), None, None), P(("lat", "lon")), grid, grid, grid, grid, grid, grid, grid,
            P(None, "lat", "lon"), P(None, None, "lat", "lon"),
        ),
        out_specs=(
            P(None, None, "lat", "lon"), P(None, None, "lat", "lon"), P(("lat", "lon"), None, None),
        ),
        check_vma=False,
    )
```

```python
import functools

import jax
import jax.numpy as jnp
from jax import lax
from jax.experimental import pallas as pl
from jax.experimental.pallas import tpu as pltpu
from jax.sharding import PartitionSpec as P


F32 = jnp.float32
I32 = jnp.int32
TILE = 90
SIDE = 3
COLUMNS = 48
HALO = 3
SLOTS = 27
PAIR = 2
LEV = 4
CELLS = TILE * TILE
N = TILE * SIDE
FLAT = 8192
TAIL = 8064
TAG = CELLS - TAIL
TOP = 16
ROWS = 304
LANES = 384
BLOCKS = ((0, 128), (1, 128), (2, N - 256))
CHUNKS = 34
COARSE = 30
VMEM = pl.BlockSpec(memory_space=pltpu.VMEM)
SMEM = pl.BlockSpec(memory_space=pltpu.SMEM)
ANY = pl.BlockSpec(memory_space=pl.ANY)


def aligned(x):
    return pl.multiple_of(x, 8)


def pack_kernel(ids, stored, after, out, held, tail, empty, count, route, in_sem, out_sem, tail_sem, empty_sem):
    owners = out.shape[0]

    def fetch(s):
        return pltpu.make_async_copy(stored.at[s], held.at[s], in_sem.at[s])

    def send(s, owner, rank):
        return pltpu.make_async_copy(
            held.at[s, :, pl.ds(0, TAIL)], out.at[owner, rank, :, pl.ds(0, TAIL)], out_sem.at[s]
        )

    def send_tail(s, owner, rank):
        return pltpu.make_async_copy(
            tail.at[s], out.at[owner, rank, :, pl.ds(TAIL, 128)], tail_sem.at[s]
        )

    def send_empty(owner, rank):
        return pltpu.make_async_copy(
            empty, out.at[owner, rank, :, pl.ds(TAIL, 128)], empty_sem.at[owner, rank]
        )

    @pl.loop(0, SLOTS)
    def _(s):
        @pl.when(ids[s] >= 0)
        def _():
            fetch(s).start()

    @pl.loop(0, owners)
    def _(o):
        count[o] = 0

    empty[...] = jnp.full((8, 128), -1.0, F32)
    lane = lax.broadcasted_iota(I32, (8, 128), 1)

    @pl.loop(0, SLOTS)
    def _(s):
        tile = ids[s]

        @pl.when(tile >= 0)
        def _():
            row = tile // COLUMNS
            column = tile - row * COLUMNS
            owner = column // SIDE
            rank = count[owner]
            count[owner] = rank + 1
            route[s] = owner * PAIR + rank
            place = row * SIDE + column - owner * SIDE
            fetch(s).wait()
            last = jnp.concatenate([held[s, :, TAIL:CELLS], jnp.zeros((8, 128 - TAG), F32)], axis=1)
            tail[s] = jnp.where(lane < TAG, last, place.astype(F32))
            send(s, owner, rank).start()
            send_tail(s, owner, rank).start()

    for rank in range(PAIR):

        @pl.loop(0, owners)
        def _(o):
            @pl.when(count[o] <= rank)
            def _():
                send_empty(o, rank).start()

    @pl.loop(0, SLOTS)
    def _(s):
        @pl.when(ids[s] >= 0)
        def _():
            owner = route[s] // PAIR
            rank = route[s] - owner * PAIR
            send(s, owner, rank).wait()
            send_tail(s, owner, rank).wait()

    for rank in range(PAIR):

        @pl.loop(0, owners)
        def _(o):
            @pl.when(count[o] <= rank)
            def _():
                send_empty(o, rank).wait()


def pack_tiles(ids, stored, after, owners):
    return pl.pallas_call(
        pack_kernel,
        out_shape=jax.ShapeDtypeStruct((owners, PAIR, 8, FLAT), F32),
        in_specs=[SMEM, ANY, ANY],
        out_specs=ANY,
        scratch_shapes=[
            pltpu.VMEM((SLOTS, 8, CELLS), F32),
            pltpu.VMEM((SLOTS, 8, 128), F32),
            pltpu.VMEM((8, 128), F32),
            pltpu.SMEM((owners,), I32),
            pltpu.SMEM((SLOTS,), I32),
            pltpu.SemaphoreType.DMA((SLOTS,)),
            pltpu.SemaphoreType.DMA((SLOTS,)),
            pltpu.SemaphoreType.DMA((SLOTS,)),
            pltpu.SemaphoreType.DMA((owners, PAIR)),
        ],
        name="pack_tiles",
    )(ids, stored, after)


def split_kernel(ids, stored, after, first, own, cross, held, tail, empty, count, route, filled, in_sem, out_sem, tail_sem, empty_sem):
    owners = first.shape[0]
    chips = own.shape[0]
    me = lax.axis_index("lon")
    outs = [(first, owners), (own, chips), (cross, chips)]

    def fetch(s):
        return pltpu.make_async_copy(stored.at[s], held.at[s], in_sem.at[s])

    def each(s, act):
        for kind, (out, _) in enumerate(outs):

            @pl.when(route[s, 0] == kind)
            def _():
                to = out.at[route[s, 1]]
                act(pltpu.make_async_copy(held.at[s, :, pl.ds(0, TAIL)], to.at[:, pl.ds(0, TAIL)], out_sem.at[s]))
                act(pltpu.make_async_copy(tail.at[s], to.at[:, pl.ds(TAIL, 128)], tail_sem.at[s]))

    def each_empty(act):
        for kind, (out, size) in enumerate(outs):

            @pl.loop(0, size)
            def _(i):
                @pl.when(filled[kind, i] == 0)
                def _():
                    act(
                        pltpu.make_async_copy(
                            empty, out.at[i, :, pl.ds(TAIL, 128)], empty_sem.at[kind, i]
                        )
                    )

    @pl.loop(0, SLOTS)
    def _(s):
        @pl.when(ids[s] >= 0)
        def _():
            fetch(s).start()

    @pl.loop(0, owners)
    def _(o):
        count[o] = 0
        for kind in range(3):
            filled[kind, o] = 0

    empty[...] = jnp.full((8, 128), -1.0, F32)
    lane = lax.broadcasted_iota(I32, (8, 128), 1)

    @pl.loop(0, SLOTS)
    def _(s):
        tile = ids[s]

        @pl.when(tile >= 0)
        def _():
            row = tile // COLUMNS
            column = tile - row * COLUMNS
            owner = column // SIDE
            rank = count[owner]
            count[owner] = rank + 1
            away = owner ^ me
            kind = jnp.where(rank == 0, 0, 1 + (away & 1))
            index = jnp.where(rank == 0, owner, away >> 1)
            route[s, 0] = kind
            route[s, 1] = index
            filled[kind, index] = 1
            place = row * SIDE + column - owner * SIDE
            fetch(s).wait()
            last = jnp.concatenate([held[s, :, TAIL:CELLS], jnp.zeros((8, 128 - TAG), F32)], axis=1)
            tail[s] = jnp.where(lane < TAG, last, place.astype(F32))
            each(s, lambda copy: copy.start())

    each_empty(lambda copy: copy.start())

    @pl.loop(0, SLOTS)
    def _(s):
        @pl.when(ids[s] >= 0)
        def _():
            each(s, lambda copy: copy.wait())

    each_empty(lambda copy: copy.wait())


def split_tiles(ids, stored, after, owners):
    chips = owners // 2
    return pl.pallas_call(
        split_kernel,
        out_shape=tuple(jax.ShapeDtypeStruct((n, 8, FLAT), F32) for n in (owners, chips, chips)),
        in_specs=[SMEM, ANY, ANY],
        out_specs=(ANY,) * 3,
        scratch_shapes=[
            pltpu.VMEM((SLOTS, 8, CELLS), F32),
            pltpu.VMEM((SLOTS, 8, 128), F32),
            pltpu.VMEM((8, 128), F32),
            pltpu.SMEM((owners,), I32),
            pltpu.SMEM((SLOTS, 2), I32),
            pltpu.SMEM((3, owners), I32),
            pltpu.SemaphoreType.DMA((SLOTS,)),
            pltpu.SemaphoreType.DMA((SLOTS,)),
            pltpu.SemaphoreType.DMA((SLOTS,)),
            pltpu.SemaphoreType.DMA((3, owners)),
        ],
        name="split_tiles",
    )(ids, stored, after)


def merge_kernel(own, cross, *refs):
    chips = own.shape[0]
    outs = refs[:chips]
    clash, held, empty, own_tags, cross_tags, sem, in_sem, out_sem = refs[chips:]
    copies = [
        pltpu.make_async_copy(x.at[:, pl.ds(0, 1), pl.ds(TAIL, 128)], tags, sem.at[i])
        for i, (x, tags) in enumerate(((own, own_tags), (cross, cross_tags)))
    ]
    for copy in copies:
        copy.start()
    empty[...] = jnp.full((8, 128), -1.0, F32)
    for copy in copies:
        copy.wait()
    total = jnp.int32(0)
    has = []
    for c in range(chips):
        mine = own_tags[c, 0, TAG] >= 0
        other = cross_tags[c, 0, TAG] >= 0
        total = total + jnp.where(mine & other, 1, 0)
        has.append((mine, other))
    clash[0] = total

    def filling(c, act):
        mine, other = has[c]

        @pl.when(mine)
        def _():
            act(pltpu.make_async_copy(own.at[c], held.at[c], in_sem.at[c]))

        @pl.when(other & ~mine)
        def _():
            act(pltpu.make_async_copy(cross.at[c], held.at[c], in_sem.at[c]))

    def leaving(c, act):
        mine, other = has[c]

        @pl.when(mine | other)
        def _():
            act(pltpu.make_async_copy(held.at[c], outs[c], out_sem.at[c]))

        @pl.when(~(mine | other))
        def _():
            act(pltpu.make_async_copy(empty, outs[c].at[:, pl.ds(TAIL, 128)], out_sem.at[c]))

    for c in range(chips):
        filling(c, lambda copy: copy.start())
    for c in range(chips):
        filling(c, lambda copy: copy.wait())
        leaving(c, lambda copy: copy.start())
    for c in range(chips):
        leaving(c, lambda copy: copy.wait())


def merge_tiles(own, cross):
    chips = own.shape[0]
    return pl.pallas_call(
        merge_kernel,
        out_shape=(jax.ShapeDtypeStruct((8, FLAT), F32),) * chips + (jax.ShapeDtypeStruct((1,), I32),),
        in_specs=[ANY, ANY],
        out_specs=(ANY,) * chips + (SMEM,),
        scratch_shapes=[
            pltpu.VMEM((chips, 8, FLAT), F32),
            pltpu.VMEM((8, 128), F32),
            pltpu.SMEM((chips, 1, 128), F32),
            pltpu.SMEM((chips, 1, 128), F32),
            pltpu.SemaphoreType.DMA((2,)),
            pltpu.SemaphoreType.DMA((chips,)),
            pltpu.SemaphoreType.DMA((chips,)),
        ],
        name="merge_tiles",
    )(own, cross)


def strip_columns(load, count, first):
    lane = lax.broadcasted_iota(I32, (N + 2, 128), 1)
    strip = jnp.zeros((N + 2, 128), F32)
    for f in range(count):
        moved = pltpu.roll(load(f), (HALO * f - first) % 128, 1)
        strip = jnp.where((lane >= HALO * f) & (lane < HALO * f + HALO), moved, strip)
    return strip.T[0 : HALO * count]


def wet_field(wet, rows, row0):
    row = lax.broadcasted_iota(I32, (rows, LANES), 0) + row0
    lane = lax.broadcasted_iota(I32, (rows, LANES), 1)
    bands = []
    for r in range(SIDE):
        w = [wet[r, c].astype(F32) for c in range(SIDE)]
        bands.append(jnp.where(lane < TILE, w[0], jnp.where(lane < 2 * TILE, w[1], w[2])))
    return jnp.where(row < TILE, bands[0], jnp.where(row < 2 * TILE, bands[1], bands[2]))


def edges_kernel(wet, zd, zf, md, mf, vm, forcing, adjoint, west, east, south, north, held):
    views = [zd, zf, md, mf, vm]
    full = wet_field(wet, N + 2, 0)
    held[0, 0] = full[:, 0:128]
    held[1, 0] = full[:, 256:384]
    south[0:HALO, 0:N] = full[0:HALO, 0:N]
    north[0:HALO, 0:N] = full[N - HALO : N, 0:N]
    for f in range(1, 6):
        ref = views[f - 1]
        south[HALO * f : HALO * f + HALO, 0:N] = ref[0:HALO, :]
        north[HALO * f : HALO * f + HALO, 0:N] = ref[N - HALO : N, :]
        held[0, f, 0:N, :] = ref[:, 0:128]
        held[1, f, 0:N, 0 : N - 256] = ref[:, 256:N]
    for out, first in ((south, 0), (north, N - HALO)):
        for y in range(HALO):
            row = forcing[first + y]
            for f in range(2):
                out[HALO * (6 + f) + y, 0:N] = row[f]
            for t in range(2):
                row = adjoint[t, first + y]
                for k in range(LEV):
                    out[HALO * (8 + LEV * t + k) + y, 0:N] = row[k]

    def lines(at, start):
        for side, width in ((0, 128), (1, N - 256)):
            lanes = slice(256 * side, 256 * side + width)
            for base, ref, depth in ((6, forcing, 2), (8, adjoint.at[0], LEV), (8 + LEV, adjoint.at[1], LEV)):
                block = jnp.swapaxes(ref[pl.ds(start, 8), :, lanes], 0, 1)
                for k in range(depth):
                    held[side, base + k, at, 0:width] = block[k]

    @pl.loop(0, N // 8)
    def _(g):
        lines(pl.ds(aligned(8 * g), 8), 8 * g)

    lines(slice(N - 8, N), N - 8)

    def low(f):
        return held[0, f]

    def high(f):
        return held[1, f]

    west[...] = strip_columns(low, 16, 0)
    east[...] = strip_columns(high, 16, N - HALO - 256)


def edge_strips(wet, zd, zf, md, mf, vm, forcing, adjoint):
    columns = jax.ShapeDtypeStruct((48, N + 2), F32)
    rows = jax.ShapeDtypeStruct((48, N + 2), F32)
    return pl.pallas_call(
        edges_kernel,
        out_shape=(columns, columns, rows, rows),
        in_specs=[SMEM] + [VMEM] * 7,
        out_specs=(VMEM,) * 4,
        scratch_shapes=[pltpu.VMEM((2, 16, N + 2, 128), F32)],
        name="edge_strips",
    )(wet, zd, zf, md, mf, vm, forcing, adjoint)


def corners_kernel(south, north, west, east, to_south, to_north):
    for rows, out, first in ((south, to_south, 0), (north, to_north, N - HALO)):
        out[:, 0:N] = rows[:, 0:N]
        out[:, N : N + HALO] = west[:, first : first + HALO]
        out[:, N + HALO : N + 2 * HALO] = east[:, first : first + HALO]


def with_corners(south, north, west, east):
    shape = jax.ShapeDtypeStruct((south.shape[0], LANES), F32)
    return pl.pallas_call(
        corners_kernel,
        out_shape=(shape, shape),
        in_specs=[VMEM] * 4,
        out_specs=(VMEM,) * 2,
        name="row_strips",
    )(south, north, west, east)


def insert_halos(ext, base, count, west, east, south, north):
    blank = jnp.zeros((128 - HALO * count, N + 2), F32)
    from_west = jnp.concatenate([west[...], blank], axis=0).T
    from_east = jnp.concatenate([east[...], blank], axis=0).T
    blank = jnp.zeros((128 - HALO * count, 128), F32)
    low = jnp.concatenate([south[:, 256:384], blank], axis=0).T
    high = jnp.concatenate([north[:, 256:384], blank], axis=0).T
    at = N - 256
    for f in range(count):
        s = slice(HALO * f, HALO * f + HALO)
        field = ext.at[base + f]
        field[2, TOP : TOP + N + 2, 128 - HALO : 128] = from_west[:, s]
        field[2, TOP : TOP + N + 2, at : at + HALO] = from_east[:, s]
        for first, rows, block in ((TOP - HALO, south, low), (TOP + N, north, high)):
            for j, width in BLOCKS:
                field[j, first : first + HALO, 0:width] = rows[s, 128 * j : 128 * j + width]
            field[2, first : first + HALO, 128 - HALO : 128] = block[at : at + HALO, s]
            field[2, first : first + HALO, at : at + HALO] = block[at + HALO : at + 2 * HALO, s]


def from_east(block):
    lane = lax.broadcasted_iota(I32, (8, 128), 1)
    return lambda j: pltpu.roll(jnp.where(lane == 0, block((j + 1) % 3), block(j)), 127, 1)


def from_west(block):
    lane = lax.broadcasted_iota(I32, (8, 128), 1)
    return lambda j: pltpu.roll(jnp.where(lane == 127, block((j + 2) % 3), block(j)), 1, 1)


def stencil(src, b, coef, take):
    rows = pl.ds(b, 8)
    for j in range(3):
        center, east, west, north, south, mix = coef(j)
        for t in range(2):
            fields = [src.at[t * LEV + k] for k in range(LEV)]
            level = [field[j, rows, :] for field in fields]
            flux = [mix * (level[k] - level[k + 1]) for k in range(LEV - 1)]
            result = []
            for k in range(LEV):
                block = lambda i, field=fields[k]: field[i, rows, :]
                new = center * level[k] + east * from_east(block)(j) + west * from_west(block)(j)
                up = fields[k][j, pl.ds(b + 1, 8), :]
                down = fields[k][j, pl.ds(b - 1, 8), :]
                new = new + (north * up + south * down)
                if k > 0:
                    new = new + flux[k - 1]
                if k < LEV - 1:
                    new = new - flux[k]
                result.append(new)
            take(t, j, level, result)


def store_levels(out, t, j, values, i, rows):
    width = BLOCKS[j][1]
    block = jnp.swapaxes(jnp.stack(values), 0, 1)
    out[t, pl.ds(8 * i, rows), :, 128 * j : 128 * j + width] = block[0:rows, :, 0:width]


def adjoint_kernel(
    wet, labels, clash, zd, zf, md, mf, vm, forcing, adjoint, west, east, south, north,
    initial, forward_coef, keep, give,
    ext, other, coef, surface, coarse, piece,
):
    views = [zd, zf, md, mf, vm]
    full = wet_field(wet, N + 2, 0)
    for j, width in BLOCKS:
        ext[0, j, TOP : TOP + N + 2, :] = full[:, 128 * j : 128 * j + 128]
        for f in range(1, 6):
            ext[f, j, TOP : TOP + N, 0:width] = views[f - 1][:, 128 * j : 128 * j + width]

    def lines(at, start):
        for base, ref, depth in ((6, forcing, 2), (8, adjoint.at[0], LEV), (8 + LEV, adjoint.at[1], LEV)):
            block = jnp.swapaxes(ref[pl.ds(start, 8)], 0, 1)
            for k in range(depth):
                for j, width in BLOCKS:
                    ext[base + k, j, at, 0:width] = block[k, :, 128 * j : 128 * j + width]

    @pl.loop(0, N // 8)
    def _(g):
        lines(pl.ds(aligned(TOP + 8 * g), 8), 8 * g)

    lines(slice(TOP + N - 8, TOP + N), N - 8)
    insert_halos(ext, 0, 16, west, east, south, north)

    @pl.loop(1, CHUNKS + 2)
    def _(r):
        b = aligned(r * 8)
        rows = pl.ds(b, 8)
        faces = []
        wets = [ext[0, j, rows, :] for j in range(3)]
        for j in range(3):
            w, z_d, z_f, m_d, m_f, v = [ext[f, j, rows, :] for f in range(6)]
            east_open = w * from_east(wets.__getitem__)(j)
            north_open = w * ext[0, j, pl.ds(b + 1, 8), :]
            de = z_d * east_open
            ue = 0.5 * z_f * east_open
            dn = m_d * north_open
            vn = 0.5 * m_f * north_open
            faces.append((de + ue, ue - de))
            coef[0, j, rows, :] = de + ue
            coef[2, j, rows, :] = dn + vn
            forward_coef[1, j, rows, :] = de - ue
            forward_coef[3, j, rows, :] = dn - vn
            forward_coef[5, j, rows, :] = v * w
            forward_coef[6, j, rows, :] = ext[6, j, rows, :] * w
            forward_coef[7, j, rows, :] = ext[7, j, rows, :] * w
        for j in range(3):
            ea_west = from_west(lambda i: faces[i][0])(j)
            eb_west = from_west(lambda i: faces[i][1])(j)
            na_south = coef[2, j, pl.ds(b - 1, 8), :]
            minus_nb_south = forward_coef[3, j, pl.ds(b - 1, 8), :]
            forward_coef[0, j, rows, :] = 1.0 + (
                (eb_west - faces[j][0]) - (minus_nb_south + coef[2, j, rows, :])
            )
            forward_coef[2, j, rows, :] = ea_west
            forward_coef[4, j, rows, :] = na_south
            coef[1, j, rows, :] = -eb_west
            coef[3, j, rows, :] = minus_nb_south

    def load_coef(b):
        rows = pl.ds(b, 8)
        return lambda j: (
            [forward_coef[0, j, rows, :]]
            + [coef[i, j, rows, :] for i in range(4)]
            + [forward_coef[5, j, rows, :]]
        )

    lam = ext.at[pl.ds(8, 8)]

    def step(src, dst, first):
        @pl.loop(0, CHUNKS // 2 + 1)
        def _(r):
            for u in range(2):
                b = aligned(r * 16 + 8 * u + 8)
                rows = pl.ds(b, 8)

                def take(t, j, old, new):
                    for k in range(LEV):
                        dst[t * LEV + k, j, rows, :] = new[k]
                    surface[t, j, rows, :] = old[0] if first else surface[t, j, rows, :] + old[0]

                stencil(src, b, load_coef(b), take)

    step(lam, other, True)
    step(other, lam, False)

    def finish(i, count):
        b = aligned(TOP + 8 * i)
        rows = pl.ds(b, 8)

        def take(t, j, old, new):
            w = ext[0, j, rows, :]
            store_levels(initial, t, j, [w * value for value in new], i, count)
            surface[t, j, rows, :] = w * (surface[t, j, rows, :] + old[0])

        stencil(lam, b, load_coef(b), take)

    @pl.loop(0, N // 16)
    def _(i):
        finish(2 * i, 8)
        finish(2 * i + 1, 8)

    finish(N // 8 - 1, 8)
    finish(N // 8, N % 8)

    BF = jnp.bfloat16

    def parts(x):
        hi = x.astype(BF)
        rest = x - hi.astype(F32)
        mid = rest.astype(BF)
        return hi, mid, (rest - mid.astype(F32)).astype(BF)

    def band(shape, out_axis):
        i = lax.broadcasted_iota(I32, shape, out_axis) * 3
        j = lax.broadcasted_iota(I32, shape, 1 - out_axis)
        return ((j >= i) & (j < i + 3) & (j < N)).astype(F32).astype(BF)

    by_row = band((96, N + 2), 0)
    by_lane = band((LANES, 128), 1)
    shape = (N + 2, 128)
    for t in range(2):
        full = jnp.zeros((96, 128), F32)
        for j, width in BLOCKS:
            inside = (lax.broadcasted_iota(I32, shape, 0) < N) & (
                lax.broadcasted_iota(I32, shape, 1) < width
            )
            cells = jnp.where(inside, surface[t, j, TOP : TOP + N + 2, :], 0.0)
            half = sum(jnp.dot(by_row, p, preferred_element_type=F32) for p in parts(cells))
            for p in parts(half):
                full += jnp.dot(p, by_lane[128 * j : 128 * j + 128], preferred_element_type=F32)
        coarse[t] = full / 9.0
    chips = keep.shape[0] // 8
    owners = 2 * chips
    here = lax.axis_index("lat")
    me = lax.axis_index("lon")
    last = lax.broadcasted_iota(I32, (16, 128), 0) == 15
    piece[...] = jnp.where(last, clash[0].astype(F32), 0.0)
    keep[...] = jnp.broadcast_to(piece[...], keep.shape)
    give[...] = jnp.broadcast_to(piece[...], give.shape)
    part = COARSE // 2
    for r in range(SIDE):
        for c in range(SIDE):
            for t in range(2):
                for h in range(2):
                    at = COARSE * r + part * h
                    lane = 64 * h + COARSE * t
                    piece[0:part, lane : lane + COARSE] = coarse[
                        t, at : at + part, COARSE * c : COARSE * c + COARSE
                    ]
            label = labels[r, c]
            row = label // owners
            away = row ^ here
            column = label - row * owners
            at = ((away & 2) * 2 + (away & 1) * 2 + (away >> 2)) * chips + (column >> 1)
            other = (column ^ me) & 1

            @pl.when(other == 0)
            def _():
                keep[at] = piece[...]

            @pl.when(other != 0)
            def _():
                give[at] = piece[...]


def adjoint_window(wet, labels, clash, zd, zf, md, mf, vm, forcing, adjoint, west, east, south, north, owners):
    return pl.pallas_call(
        adjoint_kernel,
        out_shape=(
            jax.ShapeDtypeStruct((2, N, LEV, N), F32),
            jax.ShapeDtypeStruct((8, 3, ROWS, 128), F32),
            jax.ShapeDtypeStruct((4 * owners, 16, 128), F32),
            jax.ShapeDtypeStruct((4 * owners, 16, 128), F32),
        ),
        in_specs=[SMEM] * 3 + [VMEM] * 11,
        out_specs=(VMEM,) * 4,
        scratch_shapes=[
            pltpu.VMEM((16, 3, ROWS, 128), F32),
            pltpu.VMEM((8, 3, ROWS, 128), F32),
            pltpu.VMEM((4, 3, ROWS, 128), F32),
            pltpu.VMEM((2, 3, ROWS, 128), F32),
            pltpu.VMEM((2, 96, 128), F32),
            pltpu.VMEM((16, 128), F32),
        ],
        name="adjoint_window",
    )(wet, labels, clash, zd, zf, md, mf, vm, forcing, adjoint, west, east, south, north)


def unpack_kernel(extra, first, *refs):
    seconds = refs[:extra]
    state, west, east, south, north, tags, more_tags, present, tiles, lined, tag_sem, tile_sem = refs[extra:]
    slots = first.shape[0]
    copies = [pltpu.make_async_copy(first.at[:, pl.ds(0, 1), pl.ds(TAIL, 128)], tags, tag_sem.at[0])]
    for c, second in enumerate(seconds):
        copies.append(
            pltpu.make_async_copy(second.at[pl.ds(0, 1), pl.ds(TAIL, 128)], more_tags.at[c], tag_sem.at[1 + c])
        )
    for copy in copies:
        copy.start()
    places = SIDE * SIDE

    @pl.loop(0, places)
    def _(p):
        present[p] = 0

    for copy in copies:
        copy.wait()

    def fetch(source, p):
        return pltpu.make_async_copy(source, tiles.at[p], tile_sem.at[p])

    def take(source, tag):
        place = tag.astype(I32)

        @pl.when(place >= 0)
        def _():
            present[place] = 1
            fetch(source, place).start()

    @pl.loop(0, slots)
    def _(i):
        take(first.at[i], tags[i, 0, TAG])

    for c, second in enumerate(seconds):
        take(second, more_tags[c, 0, TAG])

    @pl.loop(0, places)
    def _(p):
        @pl.when(present[p] == 0)
        def _():
            tiles[p] = jnp.zeros((8, FLAT), F32)

    @pl.loop(0, SIDE)
    def _(r):
        for c in range(SIDE):

            @pl.when(present[r * SIDE + c] != 0)
            def _():
                fetch(first.at[0], r * SIDE + c).wait()

        for y in range(TILE):
            for c in range(SIDE):
                lined[r * TILE + y, :, TILE * c : TILE * c + TILE] = tiles[
                    r * SIDE + c, :, TILE * y : TILE * y + TILE
                ]

    @pl.loop(0, CHUNKS)
    def _(g):
        block = jnp.swapaxes(lined[pl.ds(8 * g, 8)], 0, 1)
        for j in range(3):
            state[:, j, pl.ds(aligned(TOP + 8 * g), 8), :] = block[:, :, 128 * j : 128 * j + 128]

    west[...] = strip_columns(lambda f: state[f, 0, TOP : TOP + N + 2, :], 8, 0)
    east[...] = strip_columns(lambda f: state[f, 2, TOP : TOP + N + 2, :], 8, N - HALO - 256)
    for f in range(8):
        for j, width in BLOCKS:
            lanes = slice(128 * j, 128 * j + width)
            rows = slice(HALO * f, HALO * f + HALO)
            south[rows, lanes] = state[f, j, TOP : TOP + HALO, 0:width]
            north[rows, lanes] = state[f, j, TOP + N - HALO : TOP + N, 0:width]


def unpack_tiles(first, *seconds):
    strip = jax.ShapeDtypeStruct((24, N + 2), F32)
    extra = len(seconds)
    return pl.pallas_call(
        functools.partial(unpack_kernel, extra),
        out_shape=(jax.ShapeDtypeStruct((8, 3, ROWS, 128), F32),) + (strip,) * 4,
        in_specs=[ANY] * (1 + extra),
        out_specs=(VMEM,) * 5,
        scratch_shapes=[
            pltpu.SMEM((first.shape[0], 1, 128), F32),
            pltpu.SMEM((8, 1, 128), F32),
            pltpu.SMEM((SIDE * SIDE,), I32),
            pltpu.VMEM((SIDE * SIDE, 8, FLAT), F32),
            pltpu.VMEM((8 * CHUNKS, 8, LANES), F32),
            pltpu.SemaphoreType.DMA((9,)),
            pltpu.SemaphoreType.DMA((SIDE * SIDE,)),
        ],
        name="unpack_tiles",
    )(first, *seconds)


def forward_kernel(state, coef, west, east, south, north, final, first, second, sem):
    copy = pltpu.make_async_copy(state, first, sem)
    copy.start()
    copy.wait()
    insert_halos(first, 0, 8, west, east, south, north)

    def load_coef(b):
        rows = pl.ds(b, 8)
        return lambda j: [coef[i, j, rows, :] for i in range(6)]

    def step(src, dst):
        @pl.loop(0, CHUNKS // 2 + 1)
        def _(r):
            for u in range(2):
                b = aligned(r * 16 + 8 * u + 8)
                rows = pl.ds(b, 8)

                def take(t, j, old, new):
                    dst[t * LEV, j, rows, :] = new[0] + coef[6 + t, j, rows, :]
                    for k in range(1, LEV):
                        dst[t * LEV + k, j, rows, :] = new[k]

                stencil(src, b, load_coef(b), take)

    step(first, second)
    step(second, first)

    def finish(i, count):
        b = aligned(TOP + 8 * i)

        def take(t, j, old, new):
            top = new[0] + coef[6 + t, j, pl.ds(b, 8), :]
            store_levels(final, t, j, [top] + new[1:], i, count)

        stencil(first, b, load_coef(b), take)

    @pl.loop(0, N // 16)
    def _(i):
        finish(2 * i, 8)
        finish(2 * i + 1, 8)

    finish(N // 8 - 1, 8)
    finish(N // 8, N % 8)


def forward_window(state, coef, west, east, south, north):
    return pl.pallas_call(
        forward_kernel,
        out_shape=jax.ShapeDtypeStruct((2, N, LEV, N), F32),
        in_specs=[ANY] + [VMEM] * 5,
        out_specs=VMEM,
        scratch_shapes=[
            pltpu.VMEM((8, 3, ROWS, 128), F32),
            pltpu.VMEM((8, 3, ROWS, 128), F32),
            pltpu.SemaphoreType.DMA,
        ],
        name="forward_window",
    )(state, coef, west, east, south, north)


def neighbours(low, high, axis, periodic):
    count = lax.axis_size(axis)
    up = [(i, i + 1) for i in range(count - 1)] + ([(count - 1, 0)] if periodic else [])
    down = [(b, a) for a, b in up]
    return lax.ppermute(high, axis, up), lax.ppermute(low, axis, down)


def xor_permute(x, axis, bits):
    return lax.ppermute(x, axis, [(i, i ^ bits) for i in range(lax.axis_size(axis))])


def per_device(
    stored_tiles, stored_ids, wet_tiles, control_map, zonal_diffusivity, meridional_diffusivity,
    zonal_flow, meridional_flow, vertical_mixing, forcing, final_adjoint,
):
    owners = lax.axis_size("lon")
    fields = (
        zonal_diffusivity, zonal_flow, meridional_diffusivity, meridional_flow, vertical_mixing,
        forcing.transpose(1, 0, 2), final_adjoint.transpose(0, 2, 1, 3),
    )
    low, high, bottom, top = edge_strips(wet_tiles, *fields)
    west, east = neighbours(low, high, "lon", True)
    first, own, cross = split_tiles(stored_ids, stored_tiles, low, owners)
    first, west, east = lax.optimization_barrier((first, west, east))
    first = lax.all_to_all(first, "lon", split_axis=0, concat_axis=0, tiled=True)
    cross = xor_permute(cross, "lon", 1)
    south, north = neighbours(*with_corners(bottom, top, west, east), "lat", False)
    *seconds, clash = merge_tiles(own, cross)
    seconds = [seconds[0]] + [xor_permute(x, "lon", 2 * c) for c, x in enumerate(seconds) if c > 0]
    initial, coef, keep, give = adjoint_window(
        wet_tiles, control_map, clash, *fields, west, east, south, north, owners
    )
    keep = keep + xor_permute(give, "lon", 1)
    for bit in (2, 1, 4):
        half = keep.shape[0] // 2
        keep = keep[:half] + xor_permute(keep[half:], "lat", bit)
    parity = [list(range(c, owners, 2)) for c in range(2)]
    gathered = lax.all_to_all(
        keep, "lon", split_axis=0, concat_axis=0, axis_index_groups=parity, tiled=True
    )
    total = jnp.sum(gathered, axis=0)
    clashes = total[15, 0]
    total = total[: COARSE // 2]
    total = jnp.stack([total[:, :60], total[:, 64:124]]).reshape(2, COARSE // 2, 2, COARSE)
    control = total.transpose(2, 0, 1, 3).reshape(1, 2, COARSE * COARSE)

    def halos(low, high, bottom, top):
        west, east = neighbours(low, high, "lon", True)
        to_south, to_north = with_corners(bottom, top, west, east)
        return (west, east) + neighbours(to_south, to_north, "lat", False)

    state, *strips = unpack_tiles(first, *seconds)
    strips = halos(*strips)
    final = forward_window(state, coef, *strips)

    def complete(carry):
        outgoing = pack_tiles(stored_ids, stored_tiles, carry[0], owners)
        arrived = lax.all_to_all(outgoing, "lon", split_axis=0, concat_axis=0, tiled=True)
        state, *strips = unpack_tiles(arrived.reshape(owners * PAIR, 8, FLAT))
        return forward_window(state, coef, *halos(*strips)), jnp.float32(0)

    final, _ = lax.while_loop(lambda carry: carry[1] > 0, complete, (final, clashes))
    return final.transpose(0, 2, 1, 3), initial.transpose(0, 2, 1, 3), control


def solution(mesh):
    grid = P("lat", "lon")
    return jax.shard_map(
        per_device,
        mesh=mesh,
        in_specs=(
            P(("lat", "lon"), None, None), P(("lat", "lon")), grid, grid, grid, grid, grid, grid, grid,
            P(None, "lat", "lon"), P(None, None, "lat", "lon"),
        ),
        out_specs=(
            P(None, None, "lat", "lon"), P(None, None, "lat", "lon"), P(("lat", "lon"), None, None),
        ),
        check_vma=False,
    )
```

```python
import functools

import jax
import jax.numpy as jnp
from jax import lax
from jax.experimental import pallas as pl
from jax.experimental.pallas import tpu as pltpu
from jax.sharding import PartitionSpec as P


F32 = jnp.float32
I32 = jnp.int32
TILE = 90
SIDE = 3
COLUMNS = 48
HALO = 3
SLOTS = 27
PAIR = 2
LEV = 4
CELLS = TILE * TILE
N = TILE * SIDE
FLAT = 8192
TAIL = 8064
TAG = CELLS - TAIL
TOP = 16
ROWS = 304
LANES = 384
BLOCKS = ((0, 128), (1, 128), (2, N - 256))
CHUNKS = 34
COARSE = 30
VMEM = pl.BlockSpec(memory_space=pltpu.VMEM)
SMEM = pl.BlockSpec(memory_space=pltpu.SMEM)
ANY = pl.BlockSpec(memory_space=pl.ANY)


def aligned(x):
    return pl.multiple_of(x, 8)


def pack_kernel(ids, stored, after, out, held, tail, empty, count, route, in_sem, out_sem, tail_sem, empty_sem):
    owners = out.shape[0]

    def fetch(s):
        return pltpu.make_async_copy(stored.at[s], held.at[s], in_sem.at[s])

    def send(s, owner, rank):
        return pltpu.make_async_copy(
            held.at[s, :, pl.ds(0, TAIL)], out.at[owner, rank, :, pl.ds(0, TAIL)], out_sem.at[s]
        )

    def send_tail(s, owner, rank):
        return pltpu.make_async_copy(
            tail.at[s], out.at[owner, rank, :, pl.ds(TAIL, 128)], tail_sem.at[s]
        )

    def send_empty(owner, rank):
        return pltpu.make_async_copy(
            empty, out.at[owner, rank, :, pl.ds(TAIL, 128)], empty_sem.at[owner, rank]
        )

    @pl.loop(0, SLOTS)
    def _(s):
        @pl.when(ids[s] >= 0)
        def _():
            fetch(s).start()

    @pl.loop(0, owners)
    def _(o):
        count[o] = 0

    empty[...] = jnp.full((8, 128), -1.0, F32)
    lane = lax.broadcasted_iota(I32, (8, 128), 1)

    @pl.loop(0, SLOTS)
    def _(s):
        tile = ids[s]

        @pl.when(tile >= 0)
        def _():
            row = tile // COLUMNS
            column = tile - row * COLUMNS
            owner = column // SIDE
            rank = count[owner]
            count[owner] = rank + 1
            route[s] = owner * PAIR + rank
            place = row * SIDE + column - owner * SIDE
            fetch(s).wait()
            last = jnp.concatenate([held[s, :, TAIL:CELLS], jnp.zeros((8, 128 - TAG), F32)], axis=1)
            tail[s] = jnp.where(lane < TAG, last, place.astype(F32))
            send(s, owner, rank).start()
            send_tail(s, owner, rank).start()

    for rank in range(PAIR):

        @pl.loop(0, owners)
        def _(o):
            @pl.when(count[o] <= rank)
            def _():
                send_empty(o, rank).start()

    @pl.loop(0, SLOTS)
    def _(s):
        @pl.when(ids[s] >= 0)
        def _():
            owner = route[s] // PAIR
            rank = route[s] - owner * PAIR
            send(s, owner, rank).wait()
            send_tail(s, owner, rank).wait()

    for rank in range(PAIR):

        @pl.loop(0, owners)
        def _(o):
            @pl.when(count[o] <= rank)
            def _():
                send_empty(o, rank).wait()


def pack_tiles(ids, stored, after, owners):
    return pl.pallas_call(
        pack_kernel,
        out_shape=jax.ShapeDtypeStruct((owners, PAIR, 8, FLAT), F32),
        in_specs=[SMEM, ANY, ANY],
        out_specs=ANY,
        scratch_shapes=[
            pltpu.VMEM((SLOTS, 8, CELLS), F32),
            pltpu.VMEM((SLOTS, 8, 128), F32),
            pltpu.VMEM((8, 128), F32),
            pltpu.SMEM((owners,), I32),
            pltpu.SMEM((SLOTS,), I32),
            pltpu.SemaphoreType.DMA((SLOTS,)),
            pltpu.SemaphoreType.DMA((SLOTS,)),
            pltpu.SemaphoreType.DMA((SLOTS,)),
            pltpu.SemaphoreType.DMA((owners, PAIR)),
        ],
        name="pack_tiles",
    )(ids, stored, after)


def split_kernel(edges, ids, stored, first, own, cross, held, tail, empty, count, route, filled, in_sem, out_sem, tail_sem, empty_sem):
    owners = first.shape[0]
    chips = own.shape[0]
    me = lax.axis_index("lon")
    outs = [(first, owners), (own, chips), (cross, chips)]

    def fetch(s):
        return pltpu.make_async_copy(stored.at[s], held.at[s], in_sem.at[s])

    def each(s, act):
        for kind, (out, _) in enumerate(outs):

            @pl.when(route[s, 0] == kind)
            def _():
                to = out.at[route[s, 1]]
                act(pltpu.make_async_copy(held.at[s, :, pl.ds(0, TAIL)], to.at[:, pl.ds(0, TAIL)], out_sem.at[s]))
                act(pltpu.make_async_copy(tail.at[s], to.at[:, pl.ds(TAIL, 128)], tail_sem.at[s]))

    def each_empty(act):
        for kind, (out, size) in enumerate(outs):

            @pl.loop(0, size)
            def _(i):
                @pl.when(filled[kind, i] == 0)
                def _():
                    act(
                        pltpu.make_async_copy(
                            empty, out.at[i, :, pl.ds(TAIL, 128)], empty_sem.at[kind, i]
                        )
                    )

    @pl.loop(0, SLOTS)
    def _(s):
        @pl.when(ids[s] >= 0)
        def _():
            fetch(s).start()

    @pl.loop(0, owners)
    def _(o):
        count[o] = 0
        for kind in range(3):
            filled[kind, o] = 0

    edges()
    empty[...] = jnp.full((8, 128), -1.0, F32)
    lane = lax.broadcasted_iota(I32, (8, 128), 1)

    @pl.loop(0, SLOTS)
    def _(s):
        tile = ids[s]

        @pl.when(tile >= 0)
        def _():
            row = tile // COLUMNS
            column = tile - row * COLUMNS
            owner = column // SIDE
            rank = count[owner]
            count[owner] = rank + 1
            away = owner ^ me
            kind = jnp.where(rank == 0, 0, 1 + (away & 1))
            index = jnp.where(rank == 0, owner, away >> 1)
            route[s, 0] = kind
            route[s, 1] = index
            filled[kind, index] = 1
            place = row * SIDE + column - owner * SIDE
            fetch(s).wait()
            last = jnp.concatenate([held[s, :, TAIL:CELLS], jnp.zeros((8, 128 - TAG), F32)], axis=1)
            tail[s] = jnp.where(lane < TAG, last, place.astype(F32))
            each(s, lambda copy: copy.start())

    each_empty(lambda copy: copy.start())

    @pl.loop(0, SLOTS)
    def _(s):
        @pl.when(ids[s] >= 0)
        def _():
            each(s, lambda copy: copy.wait())

    each_empty(lambda copy: copy.wait())


def merge_kernel(own, cross, *refs):
    chips = own.shape[0]
    outs = refs[:chips]
    clash, held, empty, own_tags, cross_tags, sem, in_sem, out_sem = refs[chips:]
    copies = [
        pltpu.make_async_copy(x.at[:, pl.ds(0, 1), pl.ds(TAIL, 128)], tags, sem.at[i])
        for i, (x, tags) in enumerate(((own, own_tags), (cross, cross_tags)))
    ]
    for copy in copies:
        copy.start()
    empty[...] = jnp.full((8, 128), -1.0, F32)
    for copy in copies:
        copy.wait()
    total = jnp.int32(0)
    has = []
    for c in range(chips):
        mine = own_tags[c, 0, TAG] >= 0
        other = cross_tags[c, 0, TAG] >= 0
        total = total + jnp.where(mine & other, 1, 0)
        has.append((mine, other))
    clash[0] = total

    def filling(c, act):
        mine, other = has[c]

        @pl.when(mine)
        def _():
            act(pltpu.make_async_copy(own.at[c], held.at[c], in_sem.at[c]))

        @pl.when(other & ~mine)
        def _():
            act(pltpu.make_async_copy(cross.at[c], held.at[c], in_sem.at[c]))

    def leaving(c, act):
        mine, other = has[c]

        @pl.when(mine | other)
        def _():
            act(pltpu.make_async_copy(held.at[c], outs[c], out_sem.at[c]))

        @pl.when(~(mine | other))
        def _():
            act(pltpu.make_async_copy(empty, outs[c].at[:, pl.ds(TAIL, 128)], out_sem.at[c]))

    for c in range(chips):
        filling(c, lambda copy: copy.start())
    for c in range(chips):
        filling(c, lambda copy: copy.wait())
        leaving(c, lambda copy: copy.start())
    for c in range(chips):
        leaving(c, lambda copy: copy.wait())


def merge_tiles(own, cross):
    chips = own.shape[0]
    return pl.pallas_call(
        merge_kernel,
        out_shape=(jax.ShapeDtypeStruct((8, FLAT), F32),) * chips + (jax.ShapeDtypeStruct((1,), I32),),
        in_specs=[ANY, ANY],
        out_specs=(ANY,) * chips + (SMEM,),
        scratch_shapes=[
            pltpu.VMEM((chips, 8, FLAT), F32),
            pltpu.VMEM((8, 128), F32),
            pltpu.SMEM((chips, 1, 128), F32),
            pltpu.SMEM((chips, 1, 128), F32),
            pltpu.SemaphoreType.DMA((2,)),
            pltpu.SemaphoreType.DMA((chips,)),
            pltpu.SemaphoreType.DMA((chips,)),
        ],
        name="merge_tiles",
    )(own, cross)


def strip_columns(load, count, first):
    lane = lax.broadcasted_iota(I32, (N + 2, 128), 1)
    strip = jnp.zeros((N + 2, 128), F32)
    for f in range(count):
        moved = pltpu.roll(load(f), (HALO * f - first) % 128, 1)
        strip = jnp.where((lane >= HALO * f) & (lane < HALO * f + HALO), moved, strip)
    return strip.T[0 : HALO * count]


def wet_field(wet, rows, row0):
    row = lax.broadcasted_iota(I32, (rows, LANES), 0) + row0
    lane = lax.broadcasted_iota(I32, (rows, LANES), 1)
    bands = []
    for r in range(SIDE):
        w = [wet[r, c].astype(F32) for c in range(SIDE)]
        bands.append(jnp.where(lane < TILE, w[0], jnp.where(lane < 2 * TILE, w[1], w[2])))
    return jnp.where(row < TILE, bands[0], jnp.where(row < 2 * TILE, bands[1], bands[2]))


def edges_kernel(wet, zd, zf, md, mf, vm, forcing, adjoint, west, east, south, north, held):
    views = [zd, zf, md, mf, vm]
    full = wet_field(wet, N + 2, 0)
    held[0, 0] = full[:, 0:128]
    held[1, 0] = full[:, 256:384]
    south[0:HALO, 0:N] = full[0:HALO, 0:N]
    north[0:HALO, 0:N] = full[N - HALO : N, 0:N]
    for f in range(1, 6):
        ref = views[f - 1]
        south[HALO * f : HALO * f + HALO, 0:N] = ref[0:HALO, :]
        north[HALO * f : HALO * f + HALO, 0:N] = ref[N - HALO : N, :]
        held[0, f, 0:N, :] = ref[:, 0:128]
        held[1, f, 0:N, 0 : N - 256] = ref[:, 256:N]
    for out, first in ((south, 0), (north, N - HALO)):
        for y in range(HALO):
            row = forcing[first + y]
            for f in range(2):
                out[HALO * (6 + f) + y, 0:N] = row[f]
            for t in range(2):
                row = adjoint[t, first + y]
                for k in range(LEV):
                    out[HALO * (8 + LEV * t + k) + y, 0:N] = row[k]

    def lines(at, start):
        for side, width in ((0, 128), (1, N - 256)):
            lanes = slice(256 * side, 256 * side + width)
            for base, ref, depth in ((6, forcing, 2), (8, adjoint.at[0], LEV), (8 + LEV, adjoint.at[1], LEV)):
                block = jnp.swapaxes(ref[pl.ds(start, 8), :, lanes], 0, 1)
                for k in range(depth):
                    held[side, base + k, at, 0:width] = block[k]

    @pl.loop(0, N // 8)
    def _(g):
        lines(pl.ds(aligned(8 * g), 8), 8 * g)

    lines(slice(N - 8, N), N - 8)

    def low(f):
        return held[0, f]

    def high(f):
        return held[1, f]

    west[...] = strip_columns(low, 16, 0)
    east[...] = strip_columns(high, 16, N - HALO - 256)


def head_kernel(ids, stored, *refs):
    inputs, strips, tiles = refs[:8], refs[8:12], refs[12:15]
    edge_scratch, scratch = refs[15], refs[16:]
    split_kernel(lambda: edges_kernel(*inputs, *strips, edge_scratch), ids, stored, *tiles, *scratch)


def strips_and_tiles(ids, stored, owners, *fields):
    chips = owners // 2
    strip = jax.ShapeDtypeStruct((48, N + 2), F32)
    return pl.pallas_call(
        head_kernel,
        out_shape=(strip,) * 4
        + tuple(jax.ShapeDtypeStruct((n, 8, FLAT), F32) for n in (owners, chips, chips)),
        in_specs=[SMEM, ANY, SMEM] + [VMEM] * 7,
        out_specs=(VMEM,) * 4 + (ANY,) * 3,
        scratch_shapes=[
            pltpu.VMEM((2, 16, N + 2, 128), F32),
            pltpu.VMEM((SLOTS, 8, CELLS), F32),
            pltpu.VMEM((SLOTS, 8, 128), F32),
            pltpu.VMEM((8, 128), F32),
            pltpu.SMEM((owners,), I32),
            pltpu.SMEM((SLOTS, 2), I32),
            pltpu.SMEM((3, owners), I32),
            pltpu.SemaphoreType.DMA((SLOTS,)),
            pltpu.SemaphoreType.DMA((SLOTS,)),
            pltpu.SemaphoreType.DMA((SLOTS,)),
            pltpu.SemaphoreType.DMA((3, owners)),
        ],
        name="strips_and_tiles",
    )(ids, stored, *fields)


def corners_kernel(south, north, west, east, to_south, to_north):
    for rows, out, first in ((south, to_south, 0), (north, to_north, N - HALO)):
        out[:, 0:N] = rows[:, 0:N]
        out[:, N : N + HALO] = west[:, first : first + HALO]
        out[:, N + HALO : N + 2 * HALO] = east[:, first : first + HALO]


def with_corners(south, north, west, east):
    shape = jax.ShapeDtypeStruct((south.shape[0], LANES), F32)
    return pl.pallas_call(
        corners_kernel,
        out_shape=(shape, shape),
        in_specs=[VMEM] * 4,
        out_specs=(VMEM,) * 2,
        name="row_strips",
    )(south, north, west, east)


def insert_halos(ext, base, count, west, east, south, north):
    blank = jnp.zeros((128 - HALO * count, N + 2), F32)
    from_west = jnp.concatenate([west[...], blank], axis=0).T
    from_east = jnp.concatenate([east[...], blank], axis=0).T
    blank = jnp.zeros((128 - HALO * count, 128), F32)
    low = jnp.concatenate([south[:, 256:384], blank], axis=0).T
    high = jnp.concatenate([north[:, 256:384], blank], axis=0).T
    at = N - 256
    for f in range(count):
        s = slice(HALO * f, HALO * f + HALO)
        field = ext.at[base + f]
        field[2, TOP : TOP + N + 2, 128 - HALO : 128] = from_west[:, s]
        field[2, TOP : TOP + N + 2, at : at + HALO] = from_east[:, s]
        for first, rows, block in ((TOP - HALO, south, low), (TOP + N, north, high)):
            for j, width in BLOCKS:
                field[j, first : first + HALO, 0:width] = rows[s, 128 * j : 128 * j + width]
            field[2, first : first + HALO, 128 - HALO : 128] = block[at : at + HALO, s]
            field[2, first : first + HALO, at : at + HALO] = block[at + HALO : at + 2 * HALO, s]


def from_east(block):
    lane = lax.broadcasted_iota(I32, (8, 128), 1)
    return lambda j: pltpu.roll(jnp.where(lane == 0, block((j + 1) % 3), block(j)), 127, 1)


def from_west(block):
    lane = lax.broadcasted_iota(I32, (8, 128), 1)
    return lambda j: pltpu.roll(jnp.where(lane == 127, block((j + 2) % 3), block(j)), 1, 1)


def stencil(src, b, coef, take):
    rows = pl.ds(b, 8)
    for j in range(3):
        center, east, west, north, south, mix = coef(j)
        for t in range(2):
            fields = [src.at[t * LEV + k] for k in range(LEV)]
            level = [field[j, rows, :] for field in fields]
            flux = [mix * (level[k] - level[k + 1]) for k in range(LEV - 1)]
            result = []
            for k in range(LEV):
                block = lambda i, field=fields[k]: field[i, rows, :]
                new = center * level[k] + east * from_east(block)(j) + west * from_west(block)(j)
                up = fields[k][j, pl.ds(b + 1, 8), :]
                down = fields[k][j, pl.ds(b - 1, 8), :]
                new = new + (north * up + south * down)
                if k > 0:
                    new = new + flux[k - 1]
                if k < LEV - 1:
                    new = new - flux[k]
                result.append(new)
            take(t, j, level, result)


def store_levels(out, t, j, values, i, rows):
    width = BLOCKS[j][1]
    block = jnp.swapaxes(jnp.stack(values), 0, 1)
    out[t, pl.ds(8 * i, rows), :, 128 * j : 128 * j + width] = block[0:rows, :, 0:width]


def adjoint_kernel(
    wet, labels, clash, zd, zf, md, mf, vm, forcing, adjoint, west, east, south, north,
    initial, forward_coef, keep, give,
    ext, other, coef, surface, coarse, piece,
):
    views = [zd, zf, md, mf, vm]
    full = wet_field(wet, N + 2, 0)
    for j, width in BLOCKS:
        ext[0, j, TOP : TOP + N + 2, :] = full[:, 128 * j : 128 * j + 128]
        for f in range(1, 6):
            ext[f, j, TOP : TOP + N, 0:width] = views[f - 1][:, 128 * j : 128 * j + width]

    def lines(at, start):
        for base, ref, depth in ((6, forcing, 2), (8, adjoint.at[0], LEV), (8 + LEV, adjoint.at[1], LEV)):
            block = jnp.swapaxes(ref[pl.ds(start, 8)], 0, 1)
            for k in range(depth):
                for j, width in BLOCKS:
                    ext[base + k, j, at, 0:width] = block[k, :, 128 * j : 128 * j + width]

    @pl.loop(0, N // 8)
    def _(g):
        lines(pl.ds(aligned(TOP + 8 * g), 8), 8 * g)

    lines(slice(TOP + N - 8, TOP + N), N - 8)
    insert_halos(ext, 0, 16, west, east, south, north)

    @pl.loop(1, CHUNKS + 2)
    def _(r):
        b = aligned(r * 8)
        rows = pl.ds(b, 8)
        faces = []
        wets = [ext[0, j, rows, :] for j in range(3)]
        for j in range(3):
            w, z_d, z_f, m_d, m_f, v = [ext[f, j, rows, :] for f in range(6)]
            east_open = w * from_east(wets.__getitem__)(j)
            north_open = w * ext[0, j, pl.ds(b + 1, 8), :]
            de = z_d * east_open
            ue = 0.5 * z_f * east_open
            dn = m_d * north_open
            vn = 0.5 * m_f * north_open
            faces.append((de + ue, ue - de))
            coef[0, j, rows, :] = de + ue
            coef[2, j, rows, :] = dn + vn
            forward_coef[1, j, rows, :] = de - ue
            forward_coef[3, j, rows, :] = dn - vn
            forward_coef[5, j, rows, :] = v * w
            forward_coef[6, j, rows, :] = ext[6, j, rows, :] * w
            forward_coef[7, j, rows, :] = ext[7, j, rows, :] * w
        for j in range(3):
            ea_west = from_west(lambda i: faces[i][0])(j)
            eb_west = from_west(lambda i: faces[i][1])(j)
            na_south = coef[2, j, pl.ds(b - 1, 8), :]
            minus_nb_south = forward_coef[3, j, pl.ds(b - 1, 8), :]
            forward_coef[0, j, rows, :] = 1.0 + (
                (eb_west - faces[j][0]) - (minus_nb_south + coef[2, j, rows, :])
            )
            forward_coef[2, j, rows, :] = ea_west
            forward_coef[4, j, rows, :] = na_south
            coef[1, j, rows, :] = -eb_west
            coef[3, j, rows, :] = minus_nb_south

    def load_coef(b):
        rows = pl.ds(b, 8)
        return lambda j: (
            [forward_coef[0, j, rows, :]]
            + [coef[i, j, rows, :] for i in range(4)]
            + [forward_coef[5, j, rows, :]]
        )

    lam = ext.at[pl.ds(8, 8)]

    def step(src, dst, first):
        @pl.loop(0, CHUNKS // 2 + 1)
        def _(r):
            for u in range(2):
                b = aligned(r * 16 + 8 * u + 8)
                rows = pl.ds(b, 8)

                def take(t, j, old, new):
                    for k in range(LEV):
                        dst[t * LEV + k, j, rows, :] = new[k]
                    surface[t, j, rows, :] = old[0] if first else surface[t, j, rows, :] + old[0]

                stencil(src, b, load_coef(b), take)

    step(lam, other, True)
    step(other, lam, False)

    def finish(i, count):
        b = aligned(TOP + 8 * i)
        rows = pl.ds(b, 8)

        def take(t, j, old, new):
            w = ext[0, j, rows, :]
            store_levels(initial, t, j, [w * value for value in new], i, count)
            surface[t, j, rows, :] = w * (surface[t, j, rows, :] + old[0])

        stencil(lam, b, load_coef(b), take)

    @pl.loop(0, N // 16)
    def _(i):
        finish(2 * i, 8)
        finish(2 * i + 1, 8)

    finish(N // 8 - 1, 8)
    finish(N // 8, N % 8)

    BF = jnp.bfloat16

    def parts(x):
        hi = x.astype(BF)
        rest = x - hi.astype(F32)
        mid = rest.astype(BF)
        return hi, mid, (rest - mid.astype(F32)).astype(BF)

    def band(shape, out_axis):
        i = lax.broadcasted_iota(I32, shape, out_axis) * 3
        j = lax.broadcasted_iota(I32, shape, 1 - out_axis)
        return ((j >= i) & (j < i + 3) & (j < N)).astype(F32).astype(BF)

    by_row = band((96, N + 2), 0)
    by_lane = band((LANES, 128), 1)
    shape = (N + 2, 128)
    for t in range(2):
        full = jnp.zeros((96, 128), F32)
        for j, width in BLOCKS:
            inside = (lax.broadcasted_iota(I32, shape, 0) < N) & (
                lax.broadcasted_iota(I32, shape, 1) < width
            )
            cells = jnp.where(inside, surface[t, j, TOP : TOP + N + 2, :], 0.0)
            half = sum(jnp.dot(by_row, p, preferred_element_type=F32) for p in parts(cells))
            for p in parts(half):
                full += jnp.dot(p, by_lane[128 * j : 128 * j + 128], preferred_element_type=F32)
        coarse[t] = full / 9.0
    chips = keep.shape[0] // 8
    owners = 2 * chips
    here = lax.axis_index("lat")
    me = lax.axis_index("lon")
    last = lax.broadcasted_iota(I32, (16, 128), 0) == 15
    piece[...] = jnp.where(last, clash[0].astype(F32), 0.0)
    keep[...] = jnp.broadcast_to(piece[...], keep.shape)
    give[...] = jnp.broadcast_to(piece[...], give.shape)
    part = COARSE // 2
    for r in range(SIDE):
        for c in range(SIDE):
            for t in range(2):
                for h in range(2):
                    at = COARSE * r + part * h
                    lane = 64 * h + COARSE * t
                    piece[0:part, lane : lane + COARSE] = coarse[
                        t, at : at + part, COARSE * c : COARSE * c + COARSE
                    ]
            label = labels[r, c]
            row = label // owners
            away = row ^ here
            column = label - row * owners
            at = ((away & 2) * 2 + (away & 1) * 2 + (away >> 2)) * chips + (column >> 1)
            other = (column ^ me) & 1

            @pl.when(other == 0)
            def _():
                keep[at] = piece[...]

            @pl.when(other != 0)
            def _():
                give[at] = piece[...]


def adjoint_window(wet, labels, clash, zd, zf, md, mf, vm, forcing, adjoint, west, east, south, north, owners):
    return pl.pallas_call(
        adjoint_kernel,
        out_shape=(
            jax.ShapeDtypeStruct((2, N, LEV, N), F32),
            jax.ShapeDtypeStruct((8, 3, ROWS, 128), F32),
            jax.ShapeDtypeStruct((4 * owners, 16, 128), F32),
            jax.ShapeDtypeStruct((4 * owners, 16, 128), F32),
        ),
        in_specs=[SMEM] * 3 + [VMEM] * 11,
        out_specs=(VMEM,) * 4,
        scratch_shapes=[
            pltpu.VMEM((16, 3, ROWS, 128), F32),
            pltpu.VMEM((8, 3, ROWS, 128), F32),
            pltpu.VMEM((4, 3, ROWS, 128), F32),
            pltpu.VMEM((2, 3, ROWS, 128), F32),
            pltpu.VMEM((2, 96, 128), F32),
            pltpu.VMEM((16, 128), F32),
        ],
        name="adjoint_window",
    )(wet, labels, clash, zd, zf, md, mf, vm, forcing, adjoint, west, east, south, north)


def unpack_kernel(extra, first, *refs):
    seconds = refs[:extra]
    state, west, east, south, north, tags, more_tags, present, tiles, lined, tag_sem, tile_sem = refs[extra:]
    slots = first.shape[0]
    copies = [pltpu.make_async_copy(first.at[:, pl.ds(0, 1), pl.ds(TAIL, 128)], tags, tag_sem.at[0])]
    for c, second in enumerate(seconds):
        copies.append(
            pltpu.make_async_copy(second.at[pl.ds(0, 1), pl.ds(TAIL, 128)], more_tags.at[c], tag_sem.at[1 + c])
        )
    for copy in copies:
        copy.start()
    places = SIDE * SIDE

    @pl.loop(0, places)
    def _(p):
        present[p] = 0

    for copy in copies:
        copy.wait()

    def fetch(source, p):
        return pltpu.make_async_copy(source, tiles.at[p], tile_sem.at[p])

    def take(source, tag):
        place = tag.astype(I32)

        @pl.when(place >= 0)
        def _():
            present[place] = 1
            fetch(source, place).start()

    @pl.loop(0, slots)
    def _(i):
        take(first.at[i], tags[i, 0, TAG])

    for c, second in enumerate(seconds):
        take(second, more_tags[c, 0, TAG])

    @pl.loop(0, places)
    def _(p):
        @pl.when(present[p] == 0)
        def _():
            tiles[p] = jnp.zeros((8, FLAT), F32)

    @pl.loop(0, SIDE)
    def _(r):
        for c in range(SIDE):

            @pl.when(present[r * SIDE + c] != 0)
            def _():
                fetch(first.at[0], r * SIDE + c).wait()

        for y in range(TILE):
            for c in range(SIDE):
                lined[r * TILE + y, :, TILE * c : TILE * c + TILE] = tiles[
                    r * SIDE + c, :, TILE * y : TILE * y + TILE
                ]

    @pl.loop(0, CHUNKS)
    def _(g):
        block = jnp.swapaxes(lined[pl.ds(8 * g, 8)], 0, 1)
        for j in range(3):
            state[:, j, pl.ds(aligned(TOP + 8 * g), 8), :] = block[:, :, 128 * j : 128 * j + 128]

    west[...] = strip_columns(lambda f: state[f, 0, TOP : TOP + N + 2, :], 8, 0)
    east[...] = strip_columns(lambda f: state[f, 2, TOP : TOP + N + 2, :], 8, N - HALO - 256)
    for f in range(8):
        for j, width in BLOCKS:
            lanes = slice(128 * j, 128 * j + width)
            rows = slice(HALO * f, HALO * f + HALO)
            south[rows, lanes] = state[f, j, TOP : TOP + HALO, 0:width]
            north[rows, lanes] = state[f, j, TOP + N - HALO : TOP + N, 0:width]


def unpack_tiles(first, *seconds):
    strip = jax.ShapeDtypeStruct((24, N + 2), F32)
    extra = len(seconds)
    return pl.pallas_call(
        functools.partial(unpack_kernel, extra),
        out_shape=(jax.ShapeDtypeStruct((8, 3, ROWS, 128), F32),) + (strip,) * 4,
        in_specs=[ANY] * (1 + extra),
        out_specs=(VMEM,) * 5,
        scratch_shapes=[
            pltpu.SMEM((first.shape[0], 1, 128), F32),
            pltpu.SMEM((8, 1, 128), F32),
            pltpu.SMEM((SIDE * SIDE,), I32),
            pltpu.VMEM((SIDE * SIDE, 8, FLAT), F32),
            pltpu.VMEM((8 * CHUNKS, 8, LANES), F32),
            pltpu.SemaphoreType.DMA((9,)),
            pltpu.SemaphoreType.DMA((SIDE * SIDE,)),
        ],
        name="unpack_tiles",
    )(first, *seconds)


def forward_kernel(state, coef, west, east, south, north, out, first, second, final, sem, out_sem):
    copy = pltpu.make_async_copy(state, first, sem)
    copy.start()
    copy.wait()
    insert_halos(first, 0, 8, west, east, south, north)

    def load_coef(b):
        rows = pl.ds(b, 8)
        return lambda j: [coef[i, j, rows, :] for i in range(6)]

    def step(src, dst):
        @pl.loop(0, CHUNKS // 2 + 1)
        def _(r):
            for u in range(2):
                b = aligned(r * 16 + 8 * u + 8)
                rows = pl.ds(b, 8)

                def take(t, j, old, new):
                    dst[t * LEV, j, rows, :] = new[0] + coef[6 + t, j, rows, :]
                    for k in range(1, LEV):
                        dst[t * LEV + k, j, rows, :] = new[k]

                stencil(src, b, load_coef(b), take)

    step(first, second)
    step(second, first)

    def finish(i, count):
        b = aligned(TOP + 8 * i)

        def take(t, j, old, new):
            top = new[0] + coef[6 + t, j, pl.ds(b, 8), :]
            store_levels(final, t, j, [top] + new[1:], i, count)

        stencil(first, b, load_coef(b), take)

    cuts = (0, 96, 192, N)
    copies = []
    for part, (low, high) in enumerate(zip(cuts, cuts[1:])):
        pairs = high // 16 - low // 16

        @pl.loop(0, pairs)
        def _(i):
            finish(low // 8 + 2 * i, 8)
            finish(low // 8 + 2 * i + 1, 8)

        if high == N:
            finish(N // 8 - 1, 8)
            finish(N // 8, N % 8)
        rows = pl.ds(low, high - low)
        copies.append(pltpu.make_async_copy(final.at[:, rows], out.at[:, rows], out_sem.at[part]))
        copies[-1].start()
    for copy in copies:
        copy.wait()


def forward_window(state, coef, west, east, south, north):
    shape = (2, N, LEV, N)
    return pl.pallas_call(
        forward_kernel,
        out_shape=jax.ShapeDtypeStruct(shape, F32),
        in_specs=[ANY] + [VMEM] * 5,
        out_specs=ANY,
        scratch_shapes=[
            pltpu.VMEM((8, 3, ROWS, 128), F32),
            pltpu.VMEM((8, 3, ROWS, 128), F32),
            pltpu.VMEM(shape, F32),
            pltpu.SemaphoreType.DMA,
            pltpu.SemaphoreType.DMA((3,)),
        ],
        name="forward_window",
        compiler_params=pltpu.CompilerParams(vmem_limit_bytes=67043328),
    )(state, coef, west, east, south, north)


def control_kernel(gathered, control, clash):
    total = jnp.sum(gathered[...], axis=0)
    part = COARSE // 2
    for i in range(part):
        for h in range(2):
            for t in range(2):
                at = part * COARSE * h + COARSE * i
                lane = 64 * h + COARSE * t
                control[0, t : t + 1, at : at + COARSE] = total[i : i + 1, lane : lane + COARSE]
    clash[0] = jnp.max(total[15:16])


def control_rows(gathered):
    return pl.pallas_call(
        control_kernel,
        out_shape=(
            jax.ShapeDtypeStruct((1, 2, COARSE * COARSE), F32), jax.ShapeDtypeStruct((1,), F32)
        ),
        in_specs=[VMEM],
        out_specs=(VMEM, SMEM),
        name="control_rows",
    )(gathered)


def neighbours(low, high, axis, periodic):
    count = lax.axis_size(axis)
    up = [(i, i + 1) for i in range(count - 1)] + ([(count - 1, 0)] if periodic else [])
    down = [(b, a) for a, b in up]
    return lax.ppermute(high, axis, up), lax.ppermute(low, axis, down)


def xor_permute(x, axis, bits):
    return lax.ppermute(x, axis, [(i, i ^ bits) for i in range(lax.axis_size(axis))])


def per_device(
    stored_tiles, stored_ids, wet_tiles, control_map, zonal_diffusivity, meridional_diffusivity,
    zonal_flow, meridional_flow, vertical_mixing, forcing, final_adjoint,
):
    owners = lax.axis_size("lon")
    fields = (
        zonal_diffusivity, zonal_flow, meridional_diffusivity, meridional_flow, vertical_mixing,
        forcing.transpose(1, 0, 2), final_adjoint.transpose(0, 2, 1, 3),
    )
    low, high, bottom, top, first, own, cross = strips_and_tiles(
        stored_ids, stored_tiles, owners, wet_tiles, *fields
    )
    west, east = neighbours(low, high, "lon", True)
    first = lax.all_to_all(first, "lon", split_axis=0, concat_axis=0, tiled=True)
    cross = xor_permute(cross, "lon", 1)
    south, north = neighbours(*with_corners(bottom, top, west, east), "lat", False)
    *seconds, clash = merge_tiles(own, cross)
    seconds = [seconds[0]] + [xor_permute(x, "lon", 2 * c) for c, x in enumerate(seconds) if c > 0]
    initial, coef, keep, give = adjoint_window(
        wet_tiles, control_map, clash, *fields, west, east, south, north, owners
    )
    keep = keep + xor_permute(give, "lon", 1)
    for bit in (2, 1, 4):
        half = keep.shape[0] // 2
        keep = keep[:half] + xor_permute(keep[half:], "lat", bit)
    parity = [list(range(c, owners, 2)) for c in range(2)]
    gathered = lax.all_to_all(
        keep, "lon", split_axis=0, concat_axis=0, axis_index_groups=parity, tiled=True
    )
    control, clashes = control_rows(gathered)

    def halos(low, high, bottom, top):
        west, east = neighbours(low, high, "lon", True)
        to_south, to_north = with_corners(bottom, top, west, east)
        return (west, east) + neighbours(to_south, to_north, "lat", False)

    state, *strips = unpack_tiles(first, *seconds)
    strips = halos(*strips)
    final = forward_window(state, coef, *strips)

    def complete(carry):
        outgoing = pack_tiles(stored_ids, stored_tiles, carry[0], owners)
        arrived = lax.all_to_all(outgoing, "lon", split_axis=0, concat_axis=0, tiled=True)
        state, *strips = unpack_tiles(arrived.reshape(owners * PAIR, 8, FLAT))
        return forward_window(state, coef, *halos(*strips)), jnp.float32(0)

    final, _ = lax.while_loop(lambda carry: carry[1] > 0, complete, (final, clashes[0]))
    return final.transpose(0, 2, 1, 3), initial.transpose(0, 2, 1, 3), control


def solution(mesh):
    grid = P("lat", "lon")
    return jax.shard_map(
        per_device,
        mesh=mesh,
        in_specs=(
            P(("lat", "lon"), None, None), P(("lat", "lon")), grid, grid, grid, grid, grid, grid, grid,
            P(None, "lat", "lon"), P(None, None, "lat", "lon"),
        ),
        out_specs=(
            P(None, None, "lat", "lon"), P(None, None, "lat", "lon"), P(("lat", "lon"), None, None),
        ),
        check_vma=False,
    )
```

```python
import functools

import jax
import jax.numpy as jnp
from jax import lax
from jax.experimental import pallas as pl
from jax.experimental.pallas import tpu as pltpu
from jax.sharding import PartitionSpec as P


F32 = jnp.float32
I32 = jnp.int32
TILE = 90
SIDE = 3
COLUMNS = 48
HALO = 3
SLOTS = 27
PAIR = 2
LEV = 4
CELLS = TILE * TILE
N = TILE * SIDE
FLAT = 8192
TAIL = 8064
TAG = CELLS - TAIL
TOP = 16
ROWS = 304
LANES = 384
BLOCKS = ((0, 128), (1, 128), (2, N - 256))
CHUNKS = 34
COARSE = 30
VMEM = pl.BlockSpec(memory_space=pltpu.VMEM)
SMEM = pl.BlockSpec(memory_space=pltpu.SMEM)
ANY = pl.BlockSpec(memory_space=pl.ANY)


def aligned(x):
    return pl.multiple_of(x, 8)


def pack_kernel(ids, stored, after, out, held, tail, empty, count, route, in_sem, out_sem, tail_sem, empty_sem):
    owners = out.shape[0]

    def fetch(s):
        return pltpu.make_async_copy(stored.at[s], held.at[s], in_sem.at[s])

    def send(s, owner, rank):
        return pltpu.make_async_copy(
            held.at[s, :, pl.ds(0, TAIL)], out.at[owner, rank, :, pl.ds(0, TAIL)], out_sem.at[s]
        )

    def send_tail(s, owner, rank):
        return pltpu.make_async_copy(
            tail.at[s], out.at[owner, rank, :, pl.ds(TAIL, 128)], tail_sem.at[s]
        )

    def send_empty(owner, rank):
        return pltpu.make_async_copy(
            empty, out.at[owner, rank, :, pl.ds(TAIL, 128)], empty_sem.at[owner, rank]
        )

    @pl.loop(0, SLOTS)
    def _(s):
        @pl.when(ids[s] >= 0)
        def _():
            fetch(s).start()

    @pl.loop(0, owners)
    def _(o):
        count[o] = 0

    empty[...] = jnp.full((8, 128), -1.0, F32)
    lane = lax.broadcasted_iota(I32, (8, 128), 1)

    @pl.loop(0, SLOTS)
    def _(s):
        tile = ids[s]

        @pl.when(tile >= 0)
        def _():
            row = tile // COLUMNS
            column = tile - row * COLUMNS
            owner = column // SIDE
            rank = count[owner]
            count[owner] = rank + 1
            route[s] = owner * PAIR + rank
            place = row * SIDE + column - owner * SIDE
            fetch(s).wait()
            last = jnp.concatenate([held[s, :, TAIL:CELLS], jnp.zeros((8, 128 - TAG), F32)], axis=1)
            tail[s] = jnp.where(lane < TAG, last, place.astype(F32))
            send(s, owner, rank).start()
            send_tail(s, owner, rank).start()

    for rank in range(PAIR):

        @pl.loop(0, owners)
        def _(o):
            @pl.when(count[o] <= rank)
            def _():
                send_empty(o, rank).start()

    @pl.loop(0, SLOTS)
    def _(s):
        @pl.when(ids[s] >= 0)
        def _():
            owner = route[s] // PAIR
            rank = route[s] - owner * PAIR
            send(s, owner, rank).wait()
            send_tail(s, owner, rank).wait()

    for rank in range(PAIR):

        @pl.loop(0, owners)
        def _(o):
            @pl.when(count[o] <= rank)
            def _():
                send_empty(o, rank).wait()


def pack_tiles(ids, stored, after, owners):
    return pl.pallas_call(
        pack_kernel,
        out_shape=jax.ShapeDtypeStruct((owners, PAIR, 8, FLAT), F32),
        in_specs=[SMEM, ANY, ANY],
        out_specs=ANY,
        scratch_shapes=[
            pltpu.VMEM((SLOTS, 8, CELLS), F32),
            pltpu.VMEM((SLOTS, 8, 128), F32),
            pltpu.VMEM((8, 128), F32),
            pltpu.SMEM((owners,), I32),
            pltpu.SMEM((SLOTS,), I32),
            pltpu.SemaphoreType.DMA((SLOTS,)),
            pltpu.SemaphoreType.DMA((SLOTS,)),
            pltpu.SemaphoreType.DMA((SLOTS,)),
            pltpu.SemaphoreType.DMA((owners, PAIR)),
        ],
        name="pack_tiles",
    )(ids, stored, after)


def split_kernel(edges, ids, stored, first, own, cross, held, tail, empty, count, route, filled, in_sem, out_sem, tail_sem, empty_sem):
    owners = first.shape[0]
    chips = own.shape[0]
    me = lax.axis_index("lon")
    outs = [(first, owners), (own, chips), (cross, chips)]

    def fetch(s):
        return pltpu.make_async_copy(stored.at[s], held.at[s], in_sem.at[s])

    def each(s, act):
        for kind, (out, _) in enumerate(outs):

            @pl.when(route[s, 0] == kind)
            def _():
                to = out.at[route[s, 1]]
                act(pltpu.make_async_copy(held.at[s, :, pl.ds(0, TAIL)], to.at[:, pl.ds(0, TAIL)], out_sem.at[s]))
                act(pltpu.make_async_copy(tail.at[s], to.at[:, pl.ds(TAIL, 128)], tail_sem.at[s]))

    def each_empty(act):
        for kind, (out, size) in enumerate(outs):

            @pl.loop(0, size)
            def _(i):
                @pl.when(filled[kind, i] == 0)
                def _():
                    act(
                        pltpu.make_async_copy(
                            empty, out.at[i, :, pl.ds(TAIL, 128)], empty_sem.at[kind, i]
                        )
                    )

    @pl.loop(0, SLOTS)
    def _(s):
        @pl.when(ids[s] >= 0)
        def _():
            fetch(s).start()

    @pl.loop(0, owners)
    def _(o):
        count[o] = 0
        for kind in range(3):
            filled[kind, o] = 0

    edges()
    empty[...] = jnp.full((8, 128), -1.0, F32)
    lane = lax.broadcasted_iota(I32, (8, 128), 1)

    @pl.loop(0, SLOTS)
    def _(s):
        tile = ids[s]

        @pl.when(tile >= 0)
        def _():
            row = tile // COLUMNS
            column = tile - row * COLUMNS
            owner = column // SIDE
            rank = count[owner]
            count[owner] = rank + 1
            away = owner ^ me
            kind = jnp.where(rank == 0, 0, 1 + (away & 1))
            index = jnp.where(rank == 0, owner, away >> 1)
            route[s, 0] = kind
            route[s, 1] = index
            filled[kind, index] = 1
            place = row * SIDE + column - owner * SIDE
            fetch(s).wait()
            last = jnp.concatenate([held[s, :, TAIL:CELLS], jnp.zeros((8, 128 - TAG), F32)], axis=1)
            tail[s] = jnp.where(lane < TAG, last, place.astype(F32))
            each(s, lambda copy: copy.start())

    each_empty(lambda copy: copy.start())

    @pl.loop(0, SLOTS)
    def _(s):
        @pl.when(ids[s] >= 0)
        def _():
            each(s, lambda copy: copy.wait())

    each_empty(lambda copy: copy.wait())


def merge_kernel(own, cross, *refs):
    chips = own.shape[0]
    outs = refs[:chips]
    clash, held, empty, own_tags, cross_tags, sem, in_sem, out_sem = refs[chips:]
    copies = [
        pltpu.make_async_copy(x.at[:, pl.ds(0, 1), pl.ds(TAIL, 128)], tags, sem.at[i])
        for i, (x, tags) in enumerate(((own, own_tags), (cross, cross_tags)))
    ]
    for copy in copies:
        copy.start()
    empty[...] = jnp.full((8, 128), -1.0, F32)
    for copy in copies:
        copy.wait()
    total = jnp.int32(0)
    has = []
    for c in range(chips):
        mine = own_tags[c, 0, TAG] >= 0
        other = cross_tags[c, 0, TAG] >= 0
        total = total + jnp.where(mine & other, 1, 0)
        has.append((mine, other))
    clash[0] = total

    def filling(c, act):
        mine, other = has[c]

        @pl.when(mine)
        def _():
            act(pltpu.make_async_copy(own.at[c], held.at[c], in_sem.at[c]))

        @pl.when(other & ~mine)
        def _():
            act(pltpu.make_async_copy(cross.at[c], held.at[c], in_sem.at[c]))

    def leaving(c, act):
        mine, other = has[c]

        @pl.when(mine | other)
        def _():
            act(pltpu.make_async_copy(held.at[c], outs[c], out_sem.at[c]))

        @pl.when(~(mine | other))
        def _():
            act(pltpu.make_async_copy(empty, outs[c].at[:, pl.ds(TAIL, 128)], out_sem.at[c]))

    for c in range(chips):
        filling(c, lambda copy: copy.start())
    for c in range(chips):
        filling(c, lambda copy: copy.wait())
        leaving(c, lambda copy: copy.start())
    for c in range(chips):
        leaving(c, lambda copy: copy.wait())


def merge_tiles(own, cross):
    chips = own.shape[0]
    return pl.pallas_call(
        merge_kernel,
        out_shape=(jax.ShapeDtypeStruct((8, FLAT), F32),) * chips + (jax.ShapeDtypeStruct((1,), I32),),
        in_specs=[ANY, ANY],
        out_specs=(ANY,) * chips + (SMEM,),
        scratch_shapes=[
            pltpu.VMEM((chips, 8, FLAT), F32),
            pltpu.VMEM((8, 128), F32),
            pltpu.SMEM((chips, 1, 128), F32),
            pltpu.SMEM((chips, 1, 128), F32),
            pltpu.SemaphoreType.DMA((2,)),
            pltpu.SemaphoreType.DMA((chips,)),
            pltpu.SemaphoreType.DMA((chips,)),
        ],
        name="merge_tiles",
        compiler_params=pltpu.CompilerParams(vmem_limit_bytes=67043328),
    )(own, cross)


def strip_columns(load, count, first):
    lane = lax.broadcasted_iota(I32, (N + 2, 128), 1)
    strip = jnp.zeros((N + 2, 128), F32)
    for f in range(count):
        moved = pltpu.roll(load(f), (HALO * f - first) % 128, 1)
        strip = jnp.where((lane >= HALO * f) & (lane < HALO * f + HALO), moved, strip)
    return strip.T[0 : HALO * count]


def wet_field(wet, rows, row0):
    row = lax.broadcasted_iota(I32, (rows, LANES), 0) + row0
    lane = lax.broadcasted_iota(I32, (rows, LANES), 1)
    bands = []
    for r in range(SIDE):
        w = [wet[r, c].astype(F32) for c in range(SIDE)]
        bands.append(jnp.where(lane < TILE, w[0], jnp.where(lane < 2 * TILE, w[1], w[2])))
    return jnp.where(row < TILE, bands[0], jnp.where(row < 2 * TILE, bands[1], bands[2]))


def edges_kernel(wet, zd, zf, md, mf, vm, forcing, adjoint, west, east, south, north, held):
    views = [zd, zf, md, mf, vm]
    full = wet_field(wet, N + 2, 0)
    held[0, 0] = full[:, 0:128]
    held[1, 0] = full[:, 256:384]
    south[0:HALO, 0:N] = full[0:HALO, 0:N]
    north[0:HALO, 0:N] = full[N - HALO : N, 0:N]
    for f in range(1, 6):
        ref = views[f - 1]
        south[HALO * f : HALO * f + HALO, 0:N] = ref[0:HALO, :]
        north[HALO * f : HALO * f + HALO, 0:N] = ref[N - HALO : N, :]
        held[0, f, 0:N, :] = ref[:, 0:128]
        held[1, f, 0:N, 0 : N - 256] = ref[:, 256:N]
    for out, first in ((south, 0), (north, N - HALO)):
        for y in range(HALO):
            row = forcing[first + y]
            for f in range(2):
                out[HALO * (6 + f) + y, 0:N] = row[f]
            for t in range(2):
                row = adjoint[t, first + y]
                for k in range(LEV):
                    out[HALO * (8 + LEV * t + k) + y, 0:N] = row[k]

    def lines(at, start):
        for side, width in ((0, 128), (1, N - 256)):
            lanes = slice(256 * side, 256 * side + width)
            for base, ref, depth in ((6, forcing, 2), (8, adjoint.at[0], LEV), (8 + LEV, adjoint.at[1], LEV)):
                block = jnp.swapaxes(ref[pl.ds(start, 8), :, lanes], 0, 1)
                for k in range(depth):
                    held[side, base + k, at, 0:width] = block[k]

    @pl.loop(0, N // 8)
    def _(g):
        lines(pl.ds(aligned(8 * g), 8), 8 * g)

    lines(slice(N - 8, N), N - 8)

    def low(f):
        return held[0, f]

    def high(f):
        return held[1, f]

    west[...] = strip_columns(low, 16, 0)
    east[...] = strip_columns(high, 16, N - HALO - 256)


def head_kernel(ids, stored, *refs):
    inputs, strips, tiles = refs[:8], refs[8:12], refs[12:15]
    edge_scratch, scratch = refs[15], refs[16:]
    split_kernel(lambda: edges_kernel(*inputs, *strips, edge_scratch), ids, stored, *tiles, *scratch)


def strips_and_tiles(ids, stored, owners, *fields):
    chips = owners // 2
    strip = jax.ShapeDtypeStruct((48, N + 2), F32)
    return pl.pallas_call(
        head_kernel,
        out_shape=(strip,) * 4
        + tuple(jax.ShapeDtypeStruct((n, 8, FLAT), F32) for n in (owners, chips, chips)),
        in_specs=[SMEM, ANY, SMEM] + [VMEM] * 7,
        out_specs=(VMEM,) * 4 + (ANY,) * 3,
        scratch_shapes=[
            pltpu.VMEM((2, 16, N + 2, 128), F32),
            pltpu.VMEM((SLOTS, 8, CELLS), F32),
            pltpu.VMEM((SLOTS, 8, 128), F32),
            pltpu.VMEM((8, 128), F32),
            pltpu.SMEM((owners,), I32),
            pltpu.SMEM((SLOTS, 2), I32),
            pltpu.SMEM((3, owners), I32),
            pltpu.SemaphoreType.DMA((SLOTS,)),
            pltpu.SemaphoreType.DMA((SLOTS,)),
            pltpu.SemaphoreType.DMA((SLOTS,)),
            pltpu.SemaphoreType.DMA((3, owners)),
        ],
        name="strips_and_tiles",
        compiler_params=pltpu.CompilerParams(vmem_limit_bytes=67043328),
    )(ids, stored, *fields)


def corners_kernel(south, north, west, east, to_south, to_north):
    for rows, out, first in ((south, to_south, 0), (north, to_north, N - HALO)):
        out[:, 0:N] = rows[:, 0:N]
        out[:, N : N + HALO] = west[:, first : first + HALO]
        out[:, N + HALO : N + 2 * HALO] = east[:, first : first + HALO]


def with_corners(south, north, west, east):
    shape = jax.ShapeDtypeStruct((south.shape[0], LANES), F32)
    return pl.pallas_call(
        corners_kernel,
        out_shape=(shape, shape),
        in_specs=[VMEM] * 4,
        out_specs=(VMEM,) * 2,
        name="row_strips",
    )(south, north, west, east)


def insert_halos(ext, base, count, west, east, south, north):
    blank = jnp.zeros((128 - HALO * count, N + 2), F32)
    from_west = jnp.concatenate([west[...], blank], axis=0).T
    from_east = jnp.concatenate([east[...], blank], axis=0).T
    blank = jnp.zeros((128 - HALO * count, 128), F32)
    low = jnp.concatenate([south[:, 256:384], blank], axis=0).T
    high = jnp.concatenate([north[:, 256:384], blank], axis=0).T
    at = N - 256
    for f in range(count):
        s = slice(HALO * f, HALO * f + HALO)
        field = ext.at[base + f]
        field[2, TOP : TOP + N + 2, 128 - HALO : 128] = from_west[:, s]
        field[2, TOP : TOP + N + 2, at : at + HALO] = from_east[:, s]
        for first, rows, block in ((TOP - HALO, south, low), (TOP + N, north, high)):
            for j, width in BLOCKS:
                field[j, first : first + HALO, 0:width] = rows[s, 128 * j : 128 * j + width]
            field[2, first : first + HALO, 128 - HALO : 128] = block[at : at + HALO, s]
            field[2, first : first + HALO, at : at + HALO] = block[at + HALO : at + 2 * HALO, s]


def from_east(block):
    lane = lax.broadcasted_iota(I32, (8, 128), 1)
    return lambda j: pltpu.roll(jnp.where(lane == 0, block((j + 1) % 3), block(j)), 127, 1)


def from_west(block):
    lane = lax.broadcasted_iota(I32, (8, 128), 1)
    return lambda j: pltpu.roll(jnp.where(lane == 127, block((j + 2) % 3), block(j)), 1, 1)


def stencil(src, b, coef, take):
    rows = pl.ds(b, 8)
    for j in range(3):
        center, east, west, north, south, mix = coef(j)
        for t in range(2):
            fields = [src.at[t * LEV + k] for k in range(LEV)]
            level = [field[j, rows, :] for field in fields]
            flux = [mix * (level[k] - level[k + 1]) for k in range(LEV - 1)]
            result = []
            for k in range(LEV):
                block = lambda i, field=fields[k]: field[i, rows, :]
                new = center * level[k] + east * from_east(block)(j) + west * from_west(block)(j)
                up = fields[k][j, pl.ds(b + 1, 8), :]
                down = fields[k][j, pl.ds(b - 1, 8), :]
                new = new + (north * up + south * down)
                if k > 0:
                    new = new + flux[k - 1]
                if k < LEV - 1:
                    new = new - flux[k]
                result.append(new)
            take(t, j, level, result)


def store_levels(out, t, j, values, i, rows):
    width = BLOCKS[j][1]
    block = jnp.swapaxes(jnp.stack(values), 0, 1)
    out[t, pl.ds(8 * i, rows), :, 128 * j : 128 * j + width] = block[0:rows, :, 0:width]


def adjoint_kernel(
    wet, labels, clash, zd, zf, md, mf, vm, forcing, adjoint, west, east, south, north,
    initial, forward_coef, keep, give,
    ext, other, coef, surface, coarse, piece,
):
    views = [zd, zf, md, mf, vm]
    full = wet_field(wet, N + 2, 0)
    for j, width in BLOCKS:
        ext[0, j, TOP : TOP + N + 2, :] = full[:, 128 * j : 128 * j + 128]
        for f in range(1, 6):
            ext[f, j, TOP : TOP + N, 0:width] = views[f - 1][:, 128 * j : 128 * j + width]

    def lines(at, start):
        for base, ref, depth in ((6, forcing, 2), (8, adjoint.at[0], LEV), (8 + LEV, adjoint.at[1], LEV)):
            block = jnp.swapaxes(ref[pl.ds(start, 8)], 0, 1)
            for k in range(depth):
                for j, width in BLOCKS:
                    ext[base + k, j, at, 0:width] = block[k, :, 128 * j : 128 * j + width]

    @pl.loop(0, N // 8)
    def _(g):
        lines(pl.ds(aligned(TOP + 8 * g), 8), 8 * g)

    lines(slice(TOP + N - 8, TOP + N), N - 8)
    insert_halos(ext, 0, 16, west, east, south, north)

    @pl.loop(1, CHUNKS + 2)
    def _(r):
        b = aligned(r * 8)
        rows = pl.ds(b, 8)
        faces = []
        wets = [ext[0, j, rows, :] for j in range(3)]
        for j in range(3):
            w, z_d, z_f, m_d, m_f, v = [ext[f, j, rows, :] for f in range(6)]
            east_open = w * from_east(wets.__getitem__)(j)
            north_open = w * ext[0, j, pl.ds(b + 1, 8), :]
            de = z_d * east_open
            ue = 0.5 * z_f * east_open
            dn = m_d * north_open
            vn = 0.5 * m_f * north_open
            faces.append((de + ue, ue - de))
            coef[0, j, rows, :] = de + ue
            coef[2, j, rows, :] = dn + vn
            forward_coef[1, j, rows, :] = de - ue
            forward_coef[3, j, rows, :] = dn - vn
            forward_coef[5, j, rows, :] = v * w
            forward_coef[6, j, rows, :] = ext[6, j, rows, :] * w
            forward_coef[7, j, rows, :] = ext[7, j, rows, :] * w
        for j in range(3):
            ea_west = from_west(lambda i: faces[i][0])(j)
            eb_west = from_west(lambda i: faces[i][1])(j)
            na_south = coef[2, j, pl.ds(b - 1, 8), :]
            minus_nb_south = forward_coef[3, j, pl.ds(b - 1, 8), :]
            forward_coef[0, j, rows, :] = 1.0 + (
                (eb_west - faces[j][0]) - (minus_nb_south + coef[2, j, rows, :])
            )
            forward_coef[2, j, rows, :] = ea_west
            forward_coef[4, j, rows, :] = na_south
            coef[1, j, rows, :] = -eb_west
            coef[3, j, rows, :] = minus_nb_south

    def load_coef(b):
        rows = pl.ds(b, 8)
        return lambda j: (
            [forward_coef[0, j, rows, :]]
            + [coef[i, j, rows, :] for i in range(4)]
            + [forward_coef[5, j, rows, :]]
        )

    lam = ext.at[pl.ds(8, 8)]

    def step(src, dst, first):
        @pl.loop(0, CHUNKS // 2 + 1)
        def _(r):
            for u in range(2):
                b = aligned(r * 16 + 8 * u + 8)
                rows = pl.ds(b, 8)

                def take(t, j, old, new):
                    for k in range(LEV):
                        dst[t * LEV + k, j, rows, :] = new[k]
                    surface[t, j, rows, :] = old[0] if first else surface[t, j, rows, :] + old[0]

                stencil(src, b, load_coef(b), take)

    step(lam, other, True)
    step(other, lam, False)

    def finish(i, count):
        b = aligned(TOP + 8 * i)
        rows = pl.ds(b, 8)

        def take(t, j, old, new):
            w = ext[0, j, rows, :]
            store_levels(initial, t, j, [w * value for value in new], i, count)
            surface[t, j, rows, :] = w * (surface[t, j, rows, :] + old[0])

        stencil(lam, b, load_coef(b), take)

    @pl.loop(0, N // 16)
    def _(i):
        finish(2 * i, 8)
        finish(2 * i + 1, 8)

    finish(N // 8 - 1, 8)
    finish(N // 8, N % 8)

    BF = jnp.bfloat16

    def parts(x):
        hi = x.astype(BF)
        rest = x - hi.astype(F32)
        mid = rest.astype(BF)
        return hi, mid, (rest - mid.astype(F32)).astype(BF)

    def band(shape, out_axis):
        i = lax.broadcasted_iota(I32, shape, out_axis) * 3
        j = lax.broadcasted_iota(I32, shape, 1 - out_axis)
        return ((j >= i) & (j < i + 3) & (j < N)).astype(F32).astype(BF)

    by_row = band((96, N + 2), 0)
    by_lane = band((LANES, 128), 1)
    shape = (N + 2, 128)
    for t in range(2):
        full = jnp.zeros((96, 128), F32)
        for j, width in BLOCKS:
            inside = (lax.broadcasted_iota(I32, shape, 0) < N) & (
                lax.broadcasted_iota(I32, shape, 1) < width
            )
            cells = jnp.where(inside, surface[t, j, TOP : TOP + N + 2, :], 0.0)
            half = sum(jnp.dot(by_row, p, preferred_element_type=F32) for p in parts(cells))
            for p in parts(half):
                full += jnp.dot(p, by_lane[128 * j : 128 * j + 128], preferred_element_type=F32)
        coarse[t] = full / 9.0
    chips = keep.shape[0] // 8
    owners = 2 * chips
    here = lax.axis_index("lat")
    me = lax.axis_index("lon")
    last = lax.broadcasted_iota(I32, (16, 128), 0) == 15
    piece[...] = jnp.where(last, clash[0].astype(F32), 0.0)
    keep[...] = jnp.broadcast_to(piece[...], keep.shape)
    give[...] = jnp.broadcast_to(piece[...], give.shape)
    part = COARSE // 2
    for r in range(SIDE):
        for c in range(SIDE):
            for t in range(2):
                for h in range(2):
                    at = COARSE * r + part * h
                    lane = 64 * h + COARSE * t
                    piece[0:part, lane : lane + COARSE] = coarse[
                        t, at : at + part, COARSE * c : COARSE * c + COARSE
                    ]
            label = labels[r, c]
            row = label // owners
            away = row ^ here
            column = label - row * owners
            at = ((away & 2) * 2 + (away & 1) * 2 + (row >> 2)) * chips + (column >> 1)
            other = (column ^ me) & 1

            @pl.when(other == 0)
            def _():
                keep[at] = piece[...]

            @pl.when(other != 0)
            def _():
                give[at] = piece[...]


def adjoint_window(wet, labels, clash, zd, zf, md, mf, vm, forcing, adjoint, west, east, south, north, owners):
    return pl.pallas_call(
        adjoint_kernel,
        out_shape=(
            jax.ShapeDtypeStruct((2, N, LEV, N), F32),
            jax.ShapeDtypeStruct((8, 3, ROWS, 128), F32),
            jax.ShapeDtypeStruct((4 * owners, 16, 128), F32),
            jax.ShapeDtypeStruct((4 * owners, 16, 128), F32),
        ),
        in_specs=[SMEM] * 3 + [VMEM] * 11,
        out_specs=(VMEM,) * 4,
        scratch_shapes=[
            pltpu.VMEM((16, 3, ROWS, 128), F32),
            pltpu.VMEM((8, 3, ROWS, 128), F32),
            pltpu.VMEM((4, 3, ROWS, 128), F32),
            pltpu.VMEM((2, 3, ROWS, 128), F32),
            pltpu.VMEM((2, 96, 128), F32),
            pltpu.VMEM((16, 128), F32),
        ],
        name="adjoint_window",
    )(wet, labels, clash, zd, zf, md, mf, vm, forcing, adjoint, west, east, south, north)


def unpack_kernel(extra, first, *refs):
    seconds = refs[:extra]
    state, west, east, south, north, tags, more_tags, present, tiles, lined, tag_sem, tile_sem = refs[extra:]
    slots = first.shape[0]
    copies = [pltpu.make_async_copy(first.at[:, pl.ds(0, 1), pl.ds(TAIL, 128)], tags, tag_sem.at[0])]
    for c, second in enumerate(seconds):
        copies.append(
            pltpu.make_async_copy(second.at[pl.ds(0, 1), pl.ds(TAIL, 128)], more_tags.at[c], tag_sem.at[1 + c])
        )
    for copy in copies:
        copy.start()
    places = SIDE * SIDE

    @pl.loop(0, places)
    def _(p):
        present[p] = 0

    for copy in copies:
        copy.wait()

    def fetch(source, p):
        return pltpu.make_async_copy(source, tiles.at[p], tile_sem.at[p])

    def take(source, tag):
        place = tag.astype(I32)

        @pl.when(place >= 0)
        def _():
            present[place] = 1
            fetch(source, place).start()

    @pl.loop(0, slots)
    def _(i):
        take(first.at[i], tags[i, 0, TAG])

    for c, second in enumerate(seconds):
        take(second, more_tags[c, 0, TAG])

    @pl.loop(0, places)
    def _(p):
        @pl.when(present[p] == 0)
        def _():
            tiles[p] = jnp.zeros((8, FLAT), F32)

    @pl.loop(0, SIDE)
    def _(r):
        for c in range(SIDE):

            @pl.when(present[r * SIDE + c] != 0)
            def _():
                fetch(first.at[0], r * SIDE + c).wait()

        for y in range(TILE):
            for c in range(SIDE):
                lined[r * TILE + y, :, TILE * c : TILE * c + TILE] = tiles[
                    r * SIDE + c, :, TILE * y : TILE * y + TILE
                ]

    @pl.loop(0, CHUNKS)
    def _(g):
        block = jnp.swapaxes(lined[pl.ds(8 * g, 8)], 0, 1)
        for j in range(3):
            state[:, j, pl.ds(aligned(TOP + 8 * g), 8), :] = block[:, :, 128 * j : 128 * j + 128]

    west[...] = strip_columns(lambda f: state[f, 0, TOP : TOP + N + 2, :], 8, 0)
    east[...] = strip_columns(lambda f: state[f, 2, TOP : TOP + N + 2, :], 8, N - HALO - 256)
    for f in range(8):
        for j, width in BLOCKS:
            lanes = slice(128 * j, 128 * j + width)
            rows = slice(HALO * f, HALO * f + HALO)
            south[rows, lanes] = state[f, j, TOP : TOP + HALO, 0:width]
            north[rows, lanes] = state[f, j, TOP + N - HALO : TOP + N, 0:width]


def unpack_tiles(first, *seconds):
    strip = jax.ShapeDtypeStruct((24, N + 2), F32)
    extra = len(seconds)
    return pl.pallas_call(
        functools.partial(unpack_kernel, extra),
        out_shape=(jax.ShapeDtypeStruct((8, 3, ROWS, 128), F32),) + (strip,) * 4,
        in_specs=[ANY] * (1 + extra),
        out_specs=(VMEM,) * 5,
        scratch_shapes=[
            pltpu.SMEM((first.shape[0], 1, 128), F32),
            pltpu.SMEM((8, 1, 128), F32),
            pltpu.SMEM((SIDE * SIDE,), I32),
            pltpu.VMEM((SIDE * SIDE, 8, FLAT), F32),
            pltpu.VMEM((8 * CHUNKS, 8, LANES), F32),
            pltpu.SemaphoreType.DMA((9,)),
            pltpu.SemaphoreType.DMA((SIDE * SIDE,)),
        ],
        name="unpack_tiles",
        compiler_params=pltpu.CompilerParams(vmem_limit_bytes=67043328),
    )(first, *seconds)


def forward_kernel(state, factors, west, east, south, north, out, first, second, coef, final, sem, out_sem):
    copies = [
        pltpu.make_async_copy(state, first, sem.at[0]), pltpu.make_async_copy(factors, coef, sem.at[1])
    ]
    for copy in copies:
        copy.start()
    copies[0].wait()
    insert_halos(first, 0, 8, west, east, south, north)
    copies[1].wait()

    def load_coef(b):
        rows = pl.ds(b, 8)
        return lambda j: [coef[i, j, rows, :] for i in range(6)]

    def step(src, dst):
        @pl.loop(0, CHUNKS // 2 + 1)
        def _(r):
            for u in range(2):
                b = aligned(r * 16 + 8 * u + 8)
                rows = pl.ds(b, 8)

                def take(t, j, old, new):
                    dst[t * LEV, j, rows, :] = new[0] + coef[6 + t, j, rows, :]
                    for k in range(1, LEV):
                        dst[t * LEV + k, j, rows, :] = new[k]

                stencil(src, b, load_coef(b), take)

    step(first, second)
    step(second, first)

    def finish(i, count):
        b = aligned(TOP + 8 * i)

        def take(t, j, old, new):
            top = new[0] + coef[6 + t, j, pl.ds(b, 8), :]
            store_levels(final, t, j, [top] + new[1:], i, count)

        stencil(first, b, load_coef(b), take)

    cuts = (0, 96, 192, N)
    copies = []
    for part, (low, high) in enumerate(zip(cuts, cuts[1:])):
        pairs = high // 16 - low // 16

        @pl.loop(0, pairs)
        def _(i):
            finish(low // 8 + 2 * i, 8)
            finish(low // 8 + 2 * i + 1, 8)

        if high == N:
            finish(N // 8 - 1, 8)
            finish(N // 8, N % 8)
        rows = pl.ds(low, high - low)
        copies.append(pltpu.make_async_copy(final.at[:, rows], out.at[:, rows], out_sem.at[part]))
        copies[-1].start()
    for copy in copies:
        copy.wait()


def forward_window(state, coef, west, east, south, north):
    shape = (2, N, LEV, N)
    return pl.pallas_call(
        forward_kernel,
        out_shape=jax.ShapeDtypeStruct(shape, F32),
        in_specs=[ANY] * 2 + [VMEM] * 4,
        out_specs=ANY,
        scratch_shapes=[
            pltpu.VMEM((8, 3, ROWS, 128), F32),
            pltpu.VMEM((8, 3, ROWS, 128), F32),
            pltpu.VMEM((8, 3, ROWS, 128), F32),
            pltpu.VMEM(shape, F32),
            pltpu.SemaphoreType.DMA((2,)),
            pltpu.SemaphoreType.DMA((3,)),
        ],
        name="forward_window",
        compiler_params=pltpu.CompilerParams(vmem_limit_bytes=67043328),
    )(state, coef, west, east, south, north)


def control_kernel(gathered, control, clash):
    total = jnp.sum(gathered[...], axis=0)
    part = COARSE // 2
    for i in range(part):
        for h in range(2):
            for t in range(2):
                at = part * COARSE * h + COARSE * i
                lane = 64 * h + COARSE * t
                control[0, t : t + 1, at : at + COARSE] = total[i : i + 1, lane : lane + COARSE]
    clash[0] = jnp.max(total[15:16])


def control_rows(gathered):
    return pl.pallas_call(
        control_kernel,
        out_shape=(
            jax.ShapeDtypeStruct((1, 2, COARSE * COARSE), F32), jax.ShapeDtypeStruct((1,), F32)
        ),
        in_specs=[VMEM],
        out_specs=(VMEM, SMEM),
        name="control_rows",
    )(gathered)


def neighbours(low, high, axis, periodic):
    count = lax.axis_size(axis)
    up = [(i, i + 1) for i in range(count - 1)] + ([(count - 1, 0)] if periodic else [])
    down = [(b, a) for a, b in up]
    return lax.ppermute(high, axis, up), lax.ppermute(low, axis, down)


def xor_permute(x, axis, bits):
    return lax.ppermute(x, axis, [(i, i ^ bits) for i in range(lax.axis_size(axis))])


def per_device(
    stored_tiles, stored_ids, wet_tiles, control_map, zonal_diffusivity, meridional_diffusivity,
    zonal_flow, meridional_flow, vertical_mixing, forcing, final_adjoint,
):
    owners = lax.axis_size("lon")
    fields = (
        zonal_diffusivity, zonal_flow, meridional_diffusivity, meridional_flow, vertical_mixing,
        forcing.transpose(1, 0, 2), final_adjoint.transpose(0, 2, 1, 3),
    )
    low, high, bottom, top, first, own, cross = strips_and_tiles(
        stored_ids, stored_tiles, owners, wet_tiles, *fields
    )
    west, east = neighbours(low, high, "lon", True)
    first = lax.all_to_all(first, "lon", split_axis=0, concat_axis=0, tiled=True)
    cross = xor_permute(cross, "lon", 1)
    south, north = neighbours(*with_corners(bottom, top, west, east), "lat", False)
    *seconds, clash = merge_tiles(own, cross)
    seconds = [seconds[0]] + [xor_permute(x, "lon", 2 * c) for c, x in enumerate(seconds) if c > 0]
    initial, coef, keep, give = adjoint_window(
        wet_tiles, control_map, clash, *fields, west, east, south, north, owners
    )
    keep = keep + xor_permute(give, "lon", 1)
    for bit in (2, 1):
        half = keep.shape[0] // 2
        keep = keep[:half] + xor_permute(keep[half:], "lat", bit)
    groups = [
        [row * owners + column for row in (y, y + 4) for column in range(c, owners, 2)]
        for y in range(4)
        for c in range(2)
    ]
    gathered = lax.all_to_all(
        keep, ("lat", "lon"), split_axis=0, concat_axis=0, axis_index_groups=groups, tiled=True
    )
    control, clashes = control_rows(gathered)

    def halos(low, high, bottom, top):
        west, east = neighbours(low, high, "lon", True)
        to_south, to_north = with_corners(bottom, top, west, east)
        return (west, east) + neighbours(to_south, to_north, "lat", False)

    state, *strips = unpack_tiles(first, *seconds)
    strips = halos(*strips)
    final = forward_window(state, coef, *strips)

    def complete(carry):
        outgoing = pack_tiles(stored_ids, stored_tiles, carry[0], owners)
        arrived = lax.all_to_all(outgoing, "lon", split_axis=0, concat_axis=0, tiled=True)
        state, *strips = unpack_tiles(arrived.reshape(owners * PAIR, 8, FLAT))
        return forward_window(state, coef, *halos(*strips)), jnp.float32(0)

    final, _ = lax.while_loop(lambda carry: carry[1] > 0, complete, (final, clashes[0]))
    return final.transpose(0, 2, 1, 3), initial.transpose(0, 2, 1, 3), control


def solution(mesh):
    grid = P("lat", "lon")
    return jax.shard_map(
        per_device,
        mesh=mesh,
        in_specs=(
            P(("lat", "lon"), None, None), P(("lat", "lon")), grid, grid, grid, grid, grid, grid, grid,
            P(None, "lat", "lon"), P(None, None, "lat", "lon"),
        ),
        out_specs=(
            P(None, None, "lat", "lon"), P(None, None, "lat", "lon"), P(("lat", "lon"), None, None),
        ),
        check_vma=False,
    )
```

```python
import functools

import jax
import jax.numpy as jnp
from jax import lax
from jax.experimental import pallas as pl
from jax.experimental.pallas import tpu as pltpu
from jax.sharding import PartitionSpec as P


F32 = jnp.float32
I32 = jnp.int32
TILE = 90
SIDE = 3
COLUMNS = 48
HALO = 3
SLOTS = 27
PAIR = 2
LEV = 4
CELLS = TILE * TILE
N = TILE * SIDE
FLAT = 8192
TAIL = 8064
TAG = CELLS - TAIL
TOP = 16
ROWS = 304
LANES = 384
BLOCKS = ((0, 128), (1, 128), (2, N - 256))
CHUNKS = 34
COARSE = 30
VMEM = pl.BlockSpec(memory_space=pltpu.VMEM)
SMEM = pl.BlockSpec(memory_space=pltpu.SMEM)
ANY = pl.BlockSpec(memory_space=pl.ANY)


def aligned(x):
    return pl.multiple_of(x, 8)


def pack_kernel(ids, stored, after, out, held, tail, empty, count, route, in_sem, out_sem, tail_sem, empty_sem):
    owners = out.shape[0]

    def fetch(s):
        return pltpu.make_async_copy(stored.at[s], held.at[s], in_sem.at[s])

    def send(s, owner, rank):
        return pltpu.make_async_copy(
            held.at[s, :, pl.ds(0, TAIL)], out.at[owner, rank, :, pl.ds(0, TAIL)], out_sem.at[s]
        )

    def send_tail(s, owner, rank):
        return pltpu.make_async_copy(
            tail.at[s], out.at[owner, rank, :, pl.ds(TAIL, 128)], tail_sem.at[s]
        )

    def send_empty(owner, rank):
        return pltpu.make_async_copy(
            empty, out.at[owner, rank, :, pl.ds(TAIL, 128)], empty_sem.at[owner, rank]
        )

    @pl.loop(0, SLOTS)
    def _(s):
        @pl.when(ids[s] >= 0)
        def _():
            fetch(s).start()

    @pl.loop(0, owners)
    def _(o):
        count[o] = 0

    empty[...] = jnp.full((8, 128), -1.0, F32)
    lane = lax.broadcasted_iota(I32, (8, 128), 1)

    @pl.loop(0, SLOTS)
    def _(s):
        tile = ids[s]

        @pl.when(tile >= 0)
        def _():
            row = tile // COLUMNS
            column = tile - row * COLUMNS
            owner = column // SIDE
            rank = count[owner]
            count[owner] = rank + 1
            route[s] = owner * PAIR + rank
            place = row * SIDE + column - owner * SIDE
            fetch(s).wait()
            last = jnp.concatenate([held[s, :, TAIL:CELLS], jnp.zeros((8, 128 - TAG), F32)], axis=1)
            tail[s] = jnp.where(lane < TAG, last, place.astype(F32))
            send(s, owner, rank).start()
            send_tail(s, owner, rank).start()

    for rank in range(PAIR):

        @pl.loop(0, owners)
        def _(o):
            @pl.when(count[o] <= rank)
            def _():
                send_empty(o, rank).start()

    @pl.loop(0, SLOTS)
    def _(s):
        @pl.when(ids[s] >= 0)
        def _():
            owner = route[s] // PAIR
            rank = route[s] - owner * PAIR
            send(s, owner, rank).wait()
            send_tail(s, owner, rank).wait()

    for rank in range(PAIR):

        @pl.loop(0, owners)
        def _(o):
            @pl.when(count[o] <= rank)
            def _():
                send_empty(o, rank).wait()


def pack_tiles(ids, stored, after, owners):
    return pl.pallas_call(
        pack_kernel,
        out_shape=jax.ShapeDtypeStruct((owners, PAIR, 8, FLAT), F32),
        in_specs=[SMEM, ANY, ANY],
        out_specs=ANY,
        scratch_shapes=[
            pltpu.VMEM((SLOTS, 8, CELLS), F32),
            pltpu.VMEM((SLOTS, 8, 128), F32),
            pltpu.VMEM((8, 128), F32),
            pltpu.SMEM((owners,), I32),
            pltpu.SMEM((SLOTS,), I32),
            pltpu.SemaphoreType.DMA((SLOTS,)),
            pltpu.SemaphoreType.DMA((SLOTS,)),
            pltpu.SemaphoreType.DMA((SLOTS,)),
            pltpu.SemaphoreType.DMA((owners, PAIR)),
        ],
        name="pack_tiles",
    )(ids, stored, after)


def split_kernel(edges, ids, stored, first, own, cross, held, tail, empty, count, route, filled, in_sem, out_sem, tail_sem, empty_sem):
    owners = first.shape[0]
    chips = own.shape[0]
    me = lax.axis_index("lon")
    outs = [(first, owners), (own, chips), (cross, chips)]

    def fetch(s):
        return pltpu.make_async_copy(stored.at[s], held.at[s], in_sem.at[s])

    def each(s, act):
        for kind, (out, _) in enumerate(outs):

            @pl.when(route[s, 0] == kind)
            def _():
                to = out.at[route[s, 1]]
                act(pltpu.make_async_copy(held.at[s, :, pl.ds(0, TAIL)], to.at[:, pl.ds(0, TAIL)], out_sem.at[s]))
                act(pltpu.make_async_copy(tail.at[s], to.at[:, pl.ds(TAIL, 128)], tail_sem.at[s]))

    def each_empty(act):
        for kind, (out, size) in enumerate(outs):

            @pl.loop(0, size)
            def _(i):
                @pl.when(filled[kind, i] == 0)
                def _():
                    act(
                        pltpu.make_async_copy(
                            empty, out.at[i, :, pl.ds(TAIL, 128)], empty_sem.at[kind, i]
                        )
                    )

    @pl.loop(0, SLOTS)
    def _(s):
        @pl.when(ids[s] >= 0)
        def _():
            fetch(s).start()

    @pl.loop(0, owners)
    def _(o):
        count[o] = 0
        for kind in range(3):
            filled[kind, o] = 0

    edges()
    empty[...] = jnp.full((8, 128), -1.0, F32)
    lane = lax.broadcasted_iota(I32, (8, 128), 1)

    @pl.loop(0, SLOTS)
    def _(s):
        tile = ids[s]

        @pl.when(tile >= 0)
        def _():
            row = tile // COLUMNS
            column = tile - row * COLUMNS
            owner = column // SIDE
            rank = count[owner]
            count[owner] = rank + 1
            away = owner ^ me
            kind = jnp.where(rank == 0, 0, 1 + (away & 1))
            index = jnp.where(rank == 0, owner, away >> 1)
            route[s, 0] = kind
            route[s, 1] = index
            filled[kind, index] = 1
            place = row * SIDE + column - owner * SIDE
            fetch(s).wait()
            last = jnp.concatenate([held[s, :, TAIL:CELLS], jnp.zeros((8, 128 - TAG), F32)], axis=1)
            tail[s] = jnp.where(lane < TAG, last, place.astype(F32))
            each(s, lambda copy: copy.start())

    each_empty(lambda copy: copy.start())

    @pl.loop(0, SLOTS)
    def _(s):
        @pl.when(ids[s] >= 0)
        def _():
            each(s, lambda copy: copy.wait())

    each_empty(lambda copy: copy.wait())


def merge_kernel(own, cross, *refs):
    chips = own.shape[0]
    outs = refs[:chips]
    clash, held, empty, own_tags, cross_tags, sem, in_sem, out_sem = refs[chips:]
    copies = [
        pltpu.make_async_copy(x.at[:, pl.ds(0, 1), pl.ds(TAIL, 128)], tags, sem.at[i])
        for i, (x, tags) in enumerate(((own, own_tags), (cross, cross_tags)))
    ]
    for copy in copies:
        copy.start()
    empty[...] = jnp.full((8, 128), -1.0, F32)
    for copy in copies:
        copy.wait()
    total = jnp.int32(0)
    has = []
    for c in range(chips):
        mine = own_tags[c, 0, TAG] >= 0
        other = cross_tags[c, 0, TAG] >= 0
        total = total + jnp.where(mine & other, 1, 0)
        has.append((mine, other))
    clash[0] = total

    def filling(c, act):
        mine, other = has[c]

        @pl.when(mine)
        def _():
            act(pltpu.make_async_copy(own.at[c], held.at[c], in_sem.at[c]))

        @pl.when(other & ~mine)
        def _():
            act(pltpu.make_async_copy(cross.at[c], held.at[c], in_sem.at[c]))

    def leaving(c, act):
        mine, other = has[c]

        @pl.when(mine | other)
        def _():
            act(pltpu.make_async_copy(held.at[c], outs[c], out_sem.at[c]))

        @pl.when(~(mine | other))
        def _():
            act(pltpu.make_async_copy(empty, outs[c].at[:, pl.ds(TAIL, 128)], out_sem.at[c]))

    for c in range(chips):
        filling(c, lambda copy: copy.start())
    for c in range(chips):
        filling(c, lambda copy: copy.wait())
        leaving(c, lambda copy: copy.start())
    for c in range(chips):
        leaving(c, lambda copy: copy.wait())


def merge_tiles(own, cross):
    chips = own.shape[0]
    return pl.pallas_call(
        merge_kernel,
        out_shape=(jax.ShapeDtypeStruct((8, FLAT), F32),) * chips + (jax.ShapeDtypeStruct((1,), I32),),
        in_specs=[ANY, ANY],
        out_specs=(ANY,) * chips + (SMEM,),
        scratch_shapes=[
            pltpu.VMEM((chips, 8, FLAT), F32),
            pltpu.VMEM((8, 128), F32),
            pltpu.SMEM((chips, 1, 128), F32),
            pltpu.SMEM((chips, 1, 128), F32),
            pltpu.SemaphoreType.DMA((2,)),
            pltpu.SemaphoreType.DMA((chips,)),
            pltpu.SemaphoreType.DMA((chips,)),
        ],
        name="merge_tiles",
        compiler_params=pltpu.CompilerParams(vmem_limit_bytes=67043328),
    )(own, cross)


def strip_columns(load, count, first):
    lane = lax.broadcasted_iota(I32, (N + 2, 128), 1)
    strip = jnp.zeros((N + 2, 128), F32)
    for f in range(count):
        moved = pltpu.roll(load(f), (HALO * f - first) % 128, 1)
        strip = jnp.where((lane >= HALO * f) & (lane < HALO * f + HALO), moved, strip)
    return strip.T[0 : HALO * count]


def wet_field(wet, rows, row0):
    row = lax.broadcasted_iota(I32, (rows, LANES), 0) + row0
    lane = lax.broadcasted_iota(I32, (rows, LANES), 1)
    bands = []
    for r in range(SIDE):
        w = [wet[r, c].astype(F32) for c in range(SIDE)]
        bands.append(jnp.where(lane < TILE, w[0], jnp.where(lane < 2 * TILE, w[1], w[2])))
    return jnp.where(row < TILE, bands[0], jnp.where(row < 2 * TILE, bands[1], bands[2]))


def edges_kernel(wet, zd, zf, md, mf, vm, forcing, adjoint, west, east, south, north, held):
    views = [zd, zf, md, mf, vm]
    full = wet_field(wet, N + 2, 0)
    held[0, 0] = full[:, 0:128]
    held[1, 0] = full[:, 256:384]
    south[0:HALO, 0:N] = full[0:HALO, 0:N]
    north[0:HALO, 0:N] = full[N - HALO : N, 0:N]
    for f in range(1, 6):
        ref = views[f - 1]
        south[HALO * f : HALO * f + HALO, 0:N] = ref[0:HALO, :]
        north[HALO * f : HALO * f + HALO, 0:N] = ref[N - HALO : N, :]
        held[0, f, 0:N, :] = ref[:, 0:128]
        held[1, f, 0:N, 0 : N - 256] = ref[:, 256:N]
    for out, first in ((south, 0), (north, N - HALO)):
        for y in range(HALO):
            row = forcing[first + y]
            for f in range(2):
                out[HALO * (6 + f) + y, 0:N] = row[f]
            for t in range(2):
                row = adjoint[t, first + y]
                for k in range(LEV):
                    out[HALO * (8 + LEV * t + k) + y, 0:N] = row[k]

    def lines(at, start):
        for side, width in ((0, 128), (1, N - 256)):
            lanes = slice(256 * side, 256 * side + width)
            for base, ref, depth in ((6, forcing, 2), (8, adjoint.at[0], LEV), (8 + LEV, adjoint.at[1], LEV)):
                block = jnp.swapaxes(ref[pl.ds(start, 8), :, lanes], 0, 1)
                for k in range(depth):
                    held[side, base + k, at, 0:width] = block[k]

    @pl.loop(0, N // 8)
    def _(g):
        lines(pl.ds(aligned(8 * g), 8), 8 * g)

    lines(slice(N - 8, N), N - 8)

    def low(f):
        return held[0, f]

    def high(f):
        return held[1, f]

    west[...] = strip_columns(low, 16, 0)
    east[...] = strip_columns(high, 16, N - HALO - 256)


def head_kernel(ids, stored, *refs):
    inputs, strips, tiles = refs[:8], refs[8:12], refs[12:15]
    edge_scratch, scratch = refs[15], refs[16:]
    split_kernel(lambda: edges_kernel(*inputs, *strips, edge_scratch), ids, stored, *tiles, *scratch)


def strips_and_tiles(ids, stored, owners, *fields):
    chips = owners // 2
    strip = jax.ShapeDtypeStruct((48, N + 2), F32)
    return pl.pallas_call(
        head_kernel,
        out_shape=(strip,) * 4
        + tuple(jax.ShapeDtypeStruct((n, 8, FLAT), F32) for n in (owners, chips, chips)),
        in_specs=[SMEM, ANY, SMEM] + [VMEM] * 7,
        out_specs=(VMEM,) * 4 + (ANY,) * 3,
        scratch_shapes=[
            pltpu.VMEM((2, 16, N + 2, 128), F32),
            pltpu.VMEM((SLOTS, 8, CELLS), F32),
            pltpu.VMEM((SLOTS, 8, 128), F32),
            pltpu.VMEM((8, 128), F32),
            pltpu.SMEM((owners,), I32),
            pltpu.SMEM((SLOTS, 2), I32),
            pltpu.SMEM((3, owners), I32),
            pltpu.SemaphoreType.DMA((SLOTS,)),
            pltpu.SemaphoreType.DMA((SLOTS,)),
            pltpu.SemaphoreType.DMA((SLOTS,)),
            pltpu.SemaphoreType.DMA((3, owners)),
        ],
        name="strips_and_tiles",
        compiler_params=pltpu.CompilerParams(vmem_limit_bytes=67043328),
    )(ids, stored, *fields)


def corners_kernel(south, north, west, east, to_south, to_north):
    for rows, out, first in ((south, to_south, 0), (north, to_north, N - HALO)):
        out[:, 0:N] = rows[:, 0:N]
        out[:, N : N + HALO] = west[:, first : first + HALO]
        out[:, N + HALO : N + 2 * HALO] = east[:, first : first + HALO]


def paired_kernel(south, north, west, east, one, two):
    even = lax.axis_index("lat") & 1 == 0

    @pl.when(even)
    def _():
        corners_kernel(south, north, west, east, two, one)

    @pl.when(jnp.logical_not(even))
    def _():
        corners_kernel(south, north, west, east, one, two)


def with_corners(south, north, west, east, kernel=corners_kernel):
    shape = jax.ShapeDtypeStruct((south.shape[0], LANES), F32)
    return pl.pallas_call(
        kernel,
        out_shape=(shape, shape),
        in_specs=[VMEM] * 4,
        out_specs=(VMEM,) * 2,
        name="row_strips",
    )(south, north, west, east)


def insert_halos(ext, base, count, west, east, south, north):
    blank = jnp.zeros((128 - HALO * count, N + 2), F32)
    from_west = jnp.concatenate([west[...], blank], axis=0).T
    from_east = jnp.concatenate([east[...], blank], axis=0).T
    blank = jnp.zeros((128 - HALO * count, 128), F32)
    low = jnp.concatenate([south[:, 256:384], blank], axis=0).T
    high = jnp.concatenate([north[:, 256:384], blank], axis=0).T
    at = N - 256
    for f in range(count):
        s = slice(HALO * f, HALO * f + HALO)
        field = ext.at[base + f]
        field[2, TOP : TOP + N + 2, 128 - HALO : 128] = from_west[:, s]
        field[2, TOP : TOP + N + 2, at : at + HALO] = from_east[:, s]
        for first, rows, block in ((TOP - HALO, south, low), (TOP + N, north, high)):
            for j, width in BLOCKS:
                field[j, first : first + HALO, 0:width] = rows[s, 128 * j : 128 * j + width]
            field[2, first : first + HALO, 128 - HALO : 128] = block[at : at + HALO, s]
            field[2, first : first + HALO, at : at + HALO] = block[at + HALO : at + 2 * HALO, s]


def from_east(block):
    lane = lax.broadcasted_iota(I32, (8, 128), 1)
    return lambda j: pltpu.roll(jnp.where(lane == 0, block((j + 1) % 3), block(j)), 127, 1)


def from_west(block):
    lane = lax.broadcasted_iota(I32, (8, 128), 1)
    return lambda j: pltpu.roll(jnp.where(lane == 127, block((j + 2) % 3), block(j)), 1, 1)


def stencil(src, b, coef, take):
    rows = pl.ds(b, 8)
    for j in range(3):
        center, east, west, north, south, mix = coef(j)
        for t in range(2):
            fields = [src.at[t * LEV + k] for k in range(LEV)]
            level = [field[j, rows, :] for field in fields]
            flux = [mix * (level[k] - level[k + 1]) for k in range(LEV - 1)]
            result = []
            for k in range(LEV):
                block = lambda i, field=fields[k]: field[i, rows, :]
                new = center * level[k] + east * from_east(block)(j) + west * from_west(block)(j)
                up = fields[k][j, pl.ds(b + 1, 8), :]
                down = fields[k][j, pl.ds(b - 1, 8), :]
                new = new + (north * up + south * down)
                if k > 0:
                    new = new + flux[k - 1]
                if k < LEV - 1:
                    new = new - flux[k]
                result.append(new)
            take(t, j, level, result)


def store_levels(out, t, j, values, i, rows):
    width = BLOCKS[j][1]
    block = jnp.swapaxes(jnp.stack(values), 0, 1)
    out[t, pl.ds(8 * i, rows), :, 128 * j : 128 * j + width] = block[0:rows, :, 0:width]


def adjoint_kernel(
    wet, labels, clash, zd, zf, md, mf, vm, forcing, adjoint, west, east, south, north,
    initial, forward_coef, keep, give,
    ext, other, coef, surface, coarse, piece,
):
    views = [zd, zf, md, mf, vm]
    full = wet_field(wet, N + 2, 0)
    for j, width in BLOCKS:
        ext[0, j, TOP : TOP + N + 2, :] = full[:, 128 * j : 128 * j + 128]
        for f in range(1, 6):
            ext[f, j, TOP : TOP + N, 0:width] = views[f - 1][:, 128 * j : 128 * j + width]

    def lines(at, start):
        for base, ref, depth in ((6, forcing, 2), (8, adjoint.at[0], LEV), (8 + LEV, adjoint.at[1], LEV)):
            block = jnp.swapaxes(ref[pl.ds(start, 8)], 0, 1)
            for k in range(depth):
                for j, width in BLOCKS:
                    ext[base + k, j, at, 0:width] = block[k, :, 128 * j : 128 * j + width]

    @pl.loop(0, N // 8)
    def _(g):
        lines(pl.ds(aligned(TOP + 8 * g), 8), 8 * g)

    lines(slice(TOP + N - 8, TOP + N), N - 8)
    insert_halos(ext, 0, 16, west, east, south, north)

    @pl.loop(1, CHUNKS + 2)
    def _(r):
        b = aligned(r * 8)
        rows = pl.ds(b, 8)
        faces = []
        wets = [ext[0, j, rows, :] for j in range(3)]
        for j in range(3):
            w, z_d, z_f, m_d, m_f, v = [ext[f, j, rows, :] for f in range(6)]
            east_open = w * from_east(wets.__getitem__)(j)
            north_open = w * ext[0, j, pl.ds(b + 1, 8), :]
            de = z_d * east_open
            ue = 0.5 * z_f * east_open
            dn = m_d * north_open
            vn = 0.5 * m_f * north_open
            faces.append((de + ue, ue - de))
            coef[0, j, rows, :] = de + ue
            coef[2, j, rows, :] = dn + vn
            forward_coef[1, j, rows, :] = de - ue
            forward_coef[3, j, rows, :] = dn - vn
            forward_coef[5, j, rows, :] = v * w
            forward_coef[6, j, rows, :] = ext[6, j, rows, :] * w
            forward_coef[7, j, rows, :] = ext[7, j, rows, :] * w
        for j in range(3):
            ea_west = from_west(lambda i: faces[i][0])(j)
            eb_west = from_west(lambda i: faces[i][1])(j)
            na_south = coef[2, j, pl.ds(b - 1, 8), :]
            minus_nb_south = forward_coef[3, j, pl.ds(b - 1, 8), :]
            forward_coef[0, j, rows, :] = 1.0 + (
                (eb_west - faces[j][0]) - (minus_nb_south + coef[2, j, rows, :])
            )
            forward_coef[2, j, rows, :] = ea_west
            forward_coef[4, j, rows, :] = na_south
            coef[1, j, rows, :] = -eb_west
            coef[3, j, rows, :] = minus_nb_south

    def load_coef(b):
        rows = pl.ds(b, 8)
        return lambda j: (
            [forward_coef[0, j, rows, :]]
            + [coef[i, j, rows, :] for i in range(4)]
            + [forward_coef[5, j, rows, :]]
        )

    lam = ext.at[pl.ds(8, 8)]

    def step(src, dst, first):
        @pl.loop(0, CHUNKS // 2 + 1)
        def _(r):
            for u in range(2):
                b = aligned(r * 16 + 8 * u + 8)
                rows = pl.ds(b, 8)

                def take(t, j, old, new):
                    for k in range(LEV):
                        dst[t * LEV + k, j, rows, :] = new[k]
                    surface[t, j, rows, :] = old[0] if first else surface[t, j, rows, :] + old[0]

                stencil(src, b, load_coef(b), take)

    step(lam, other, True)
    step(other, lam, False)

    def finish(i, count):
        b = aligned(TOP + 8 * i)
        rows = pl.ds(b, 8)

        def take(t, j, old, new):
            w = ext[0, j, rows, :]
            store_levels(initial, t, j, [w * value for value in new], i, count)
            surface[t, j, rows, :] = w * (surface[t, j, rows, :] + old[0])

        stencil(lam, b, load_coef(b), take)

    @pl.loop(0, N // 16)
    def _(i):
        finish(2 * i, 8)
        finish(2 * i + 1, 8)

    finish(N // 8 - 1, 8)
    finish(N // 8, N % 8)

    BF = jnp.bfloat16

    def parts(x):
        hi = x.astype(BF)
        rest = x - hi.astype(F32)
        mid = rest.astype(BF)
        return hi, mid, (rest - mid.astype(F32)).astype(BF)

    def band(shape, out_axis):
        i = lax.broadcasted_iota(I32, shape, out_axis) * 3
        j = lax.broadcasted_iota(I32, shape, 1 - out_axis)
        return ((j >= i) & (j < i + 3) & (j < N)).astype(F32).astype(BF)

    by_row = band((96, N + 2), 0)
    by_lane = band((LANES, 128), 1)
    shape = (N + 2, 128)
    for t in range(2):
        full = jnp.zeros((96, 128), F32)
        for j, width in BLOCKS:
            inside = (lax.broadcasted_iota(I32, shape, 0) < N) & (
                lax.broadcasted_iota(I32, shape, 1) < width
            )
            cells = jnp.where(inside, surface[t, j, TOP : TOP + N + 2, :], 0.0)
            half = sum(jnp.dot(by_row, p, preferred_element_type=F32) for p in parts(cells))
            for p in parts(half):
                full += jnp.dot(p, by_lane[128 * j : 128 * j + 128], preferred_element_type=F32)
        coarse[t] = full / 9.0
    chips = keep.shape[0] // 8
    owners = 2 * chips
    here = lax.axis_index("lat")
    me = lax.axis_index("lon")
    last = lax.broadcasted_iota(I32, (16, 128), 0) == 15
    piece[...] = jnp.where(last, clash[0].astype(F32), 0.0)
    keep[...] = jnp.broadcast_to(piece[...], keep.shape)
    give[...] = jnp.broadcast_to(piece[...], give.shape)
    part = COARSE // 2
    for r in range(SIDE):
        for c in range(SIDE):
            for t in range(2):
                for h in range(2):
                    at = COARSE * r + part * h
                    lane = 64 * h + COARSE * t
                    piece[0:part, lane : lane + COARSE] = coarse[
                        t, at : at + part, COARSE * c : COARSE * c + COARSE
                    ]
            label = labels[r, c]
            row = label // owners
            away = row ^ here
            column = label - row * owners
            at = ((away & 2) * 2 + (away & 1) * 2 + (row >> 2)) * chips + (column >> 1)
            other = (column ^ me) & 1

            @pl.when(other == 0)
            def _():
                keep[at] = piece[...]

            @pl.when(other != 0)
            def _():
                give[at] = piece[...]


def adjoint_window(wet, labels, clash, zd, zf, md, mf, vm, forcing, adjoint, west, east, south, north, owners):
    return pl.pallas_call(
        adjoint_kernel,
        out_shape=(
            jax.ShapeDtypeStruct((2, N, LEV, N), F32),
            jax.ShapeDtypeStruct((8, 3, ROWS, 128), F32),
            jax.ShapeDtypeStruct((4 * owners, 16, 128), F32),
            jax.ShapeDtypeStruct((4 * owners, 16, 128), F32),
        ),
        in_specs=[SMEM] * 3 + [VMEM] * 11,
        out_specs=(VMEM,) * 4,
        scratch_shapes=[
            pltpu.VMEM((16, 3, ROWS, 128), F32),
            pltpu.VMEM((8, 3, ROWS, 128), F32),
            pltpu.VMEM((4, 3, ROWS, 128), F32),
            pltpu.VMEM((2, 3, ROWS, 128), F32),
            pltpu.VMEM((2, 96, 128), F32),
            pltpu.VMEM((16, 128), F32),
        ],
        name="adjoint_window",
    )(wet, labels, clash, zd, zf, md, mf, vm, forcing, adjoint, west, east, south, north)


def unpack_kernel(extra, first, *refs):
    seconds = refs[:extra]
    state, west, east, south, north, tags, more_tags, present, tiles, lined, tag_sem, tile_sem = refs[extra:]
    slots = first.shape[0]
    copies = [pltpu.make_async_copy(first.at[:, pl.ds(0, 1), pl.ds(TAIL, 128)], tags, tag_sem.at[0])]
    for c, second in enumerate(seconds):
        copies.append(
            pltpu.make_async_copy(second.at[pl.ds(0, 1), pl.ds(TAIL, 128)], more_tags.at[c], tag_sem.at[1 + c])
        )
    for copy in copies:
        copy.start()
    places = SIDE * SIDE

    @pl.loop(0, places)
    def _(p):
        present[p] = 0

    for copy in copies:
        copy.wait()

    def fetch(source, p):
        return pltpu.make_async_copy(source, tiles.at[p], tile_sem.at[p])

    def take(source, tag):
        place = tag.astype(I32)

        @pl.when(place >= 0)
        def _():
            present[place] = 1
            fetch(source, place).start()

    @pl.loop(0, slots)
    def _(i):
        take(first.at[i], tags[i, 0, TAG])

    for c, second in enumerate(seconds):
        take(second, more_tags[c, 0, TAG])

    @pl.loop(0, places)
    def _(p):
        @pl.when(present[p] == 0)
        def _():
            tiles[p] = jnp.zeros((8, FLAT), F32)

    @pl.loop(0, SIDE)
    def _(r):
        for c in range(SIDE):

            @pl.when(present[r * SIDE + c] != 0)
            def _():
                fetch(first.at[0], r * SIDE + c).wait()

        for y in range(TILE):
            for c in range(SIDE):
                lined[r * TILE + y, :, TILE * c : TILE * c + TILE] = tiles[
                    r * SIDE + c, :, TILE * y : TILE * y + TILE
                ]

    @pl.loop(0, CHUNKS)
    def _(g):
        block = jnp.swapaxes(lined[pl.ds(8 * g, 8)], 0, 1)
        for j in range(3):
            state[:, j, pl.ds(aligned(TOP + 8 * g), 8), :] = block[:, :, 128 * j : 128 * j + 128]

    west[...] = strip_columns(lambda f: state[f, 0, TOP : TOP + N + 2, :], 8, 0)
    east[...] = strip_columns(lambda f: state[f, 2, TOP : TOP + N + 2, :], 8, N - HALO - 256)
    for f in range(8):
        for j, width in BLOCKS:
            lanes = slice(128 * j, 128 * j + width)
            rows = slice(HALO * f, HALO * f + HALO)
            south[rows, lanes] = state[f, j, TOP : TOP + HALO, 0:width]
            north[rows, lanes] = state[f, j, TOP + N - HALO : TOP + N, 0:width]


def unpack_tiles(first, *seconds):
    strip = jax.ShapeDtypeStruct((24, N + 2), F32)
    extra = len(seconds)
    return pl.pallas_call(
        functools.partial(unpack_kernel, extra),
        out_shape=(jax.ShapeDtypeStruct((8, 3, ROWS, 128), F32),) + (strip,) * 4,
        in_specs=[ANY] * (1 + extra),
        out_specs=(VMEM,) * 5,
        scratch_shapes=[
            pltpu.SMEM((first.shape[0], 1, 128), F32),
            pltpu.SMEM((8, 1, 128), F32),
            pltpu.SMEM((SIDE * SIDE,), I32),
            pltpu.VMEM((SIDE * SIDE, 8, FLAT), F32),
            pltpu.VMEM((8 * CHUNKS, 8, LANES), F32),
            pltpu.SemaphoreType.DMA((9,)),
            pltpu.SemaphoreType.DMA((SIDE * SIDE,)),
        ],
        name="unpack_tiles",
        compiler_params=pltpu.CompilerParams(vmem_limit_bytes=67043328),
    )(first, *seconds)


def forward_kernel(state, factors, west, east, one, two, out, first, second, coef, final, south, north, sem, out_sem):
    even = lax.axis_index("lat") & 1 == 0
    south[...] = jnp.where(even, two[...], one[...])
    north[...] = jnp.where(even, one[...], two[...])
    copies = [
        pltpu.make_async_copy(state, first, sem.at[0]), pltpu.make_async_copy(factors, coef, sem.at[1])
    ]
    for copy in copies:
        copy.start()
    copies[0].wait()
    insert_halos(first, 0, 8, west, east, south, north)
    copies[1].wait()

    def load_coef(b):
        rows = pl.ds(b, 8)
        return lambda j: [coef[i, j, rows, :] for i in range(6)]

    def step(src, dst):
        @pl.loop(0, CHUNKS // 2 + 1)
        def _(r):
            for u in range(2):
                b = aligned(r * 16 + 8 * u + 8)
                rows = pl.ds(b, 8)

                def take(t, j, old, new):
                    dst[t * LEV, j, rows, :] = new[0] + coef[6 + t, j, rows, :]
                    for k in range(1, LEV):
                        dst[t * LEV + k, j, rows, :] = new[k]

                stencil(src, b, load_coef(b), take)

    step(first, second)
    step(second, first)

    def finish(i, count):
        b = aligned(TOP + 8 * i)

        def take(t, j, old, new):
            top = new[0] + coef[6 + t, j, pl.ds(b, 8), :]
            store_levels(final, t, j, [top] + new[1:], i, count)

        stencil(first, b, load_coef(b), take)

    cuts = (0, 96, 192, N)
    copies = []
    for part, (low, high) in enumerate(zip(cuts, cuts[1:])):
        pairs = high // 16 - low // 16

        @pl.loop(0, pairs)
        def _(i):
            finish(low // 8 + 2 * i, 8)
            finish(low // 8 + 2 * i + 1, 8)

        if high == N:
            finish(N // 8 - 1, 8)
            finish(N // 8, N % 8)
        rows = pl.ds(low, high - low)
        copies.append(pltpu.make_async_copy(final.at[:, rows], out.at[:, rows], out_sem.at[part]))
        copies[-1].start()
    for copy in copies:
        copy.wait()


def forward_window(state, coef, west, east, one, two):
    shape = (2, N, LEV, N)
    return pl.pallas_call(
        forward_kernel,
        out_shape=jax.ShapeDtypeStruct(shape, F32),
        in_specs=[ANY] * 2 + [VMEM] * 4,
        out_specs=ANY,
        scratch_shapes=[
            pltpu.VMEM((8, 3, ROWS, 128), F32),
            pltpu.VMEM((8, 3, ROWS, 128), F32),
            pltpu.VMEM((8, 3, ROWS, 128), F32),
            pltpu.VMEM(shape, F32),
            pltpu.VMEM((24, LANES), F32),
            pltpu.VMEM((24, LANES), F32),
            pltpu.SemaphoreType.DMA((2,)),
            pltpu.SemaphoreType.DMA((3,)),
        ],
        name="forward_window",
        compiler_params=pltpu.CompilerParams(vmem_limit_bytes=67043328),
    )(state, coef, west, east, one, two)


def control_kernel(gathered, control, clash):
    total = jnp.sum(gathered[...], axis=0)
    part = COARSE // 2
    for i in range(part):
        for h in range(2):
            for t in range(2):
                at = part * COARSE * h + COARSE * i
                lane = 64 * h + COARSE * t
                control[0, t : t + 1, at : at + COARSE] = total[i : i + 1, lane : lane + COARSE]
    clash[0] = jnp.max(total[15:16])


def control_rows(gathered):
    return pl.pallas_call(
        control_kernel,
        out_shape=(
            jax.ShapeDtypeStruct((1, 2, COARSE * COARSE), F32), jax.ShapeDtypeStruct((1,), F32)
        ),
        in_specs=[VMEM],
        out_specs=(VMEM, SMEM),
        name="control_rows",
    )(gathered)


def neighbours(low, high, axis, periodic):
    count = lax.axis_size(axis)
    up = [(i, i + 1) for i in range(count - 1)] + ([(count - 1, 0)] if periodic else [])
    down = [(b, a) for a, b in up]
    return lax.ppermute(high, axis, up), lax.ppermute(low, axis, down)


def xor_permute(x, axis, bits):
    return lax.ppermute(x, axis, [(i, i ^ bits) for i in range(lax.axis_size(axis))])


def per_device(
    stored_tiles, stored_ids, wet_tiles, control_map, zonal_diffusivity, meridional_diffusivity,
    zonal_flow, meridional_flow, vertical_mixing, forcing, final_adjoint,
):
    owners = lax.axis_size("lon")
    fields = (
        zonal_diffusivity, zonal_flow, meridional_diffusivity, meridional_flow, vertical_mixing,
        forcing.transpose(1, 0, 2), final_adjoint.transpose(0, 2, 1, 3),
    )
    low, high, bottom, top, first, own, cross = strips_and_tiles(
        stored_ids, stored_tiles, owners, wet_tiles, *fields
    )
    west, east = neighbours(low, high, "lon", True)
    first = lax.all_to_all(first, "lon", split_axis=0, concat_axis=0, tiled=True)
    cross = xor_permute(cross, "lon", 1)
    south, north = neighbours(*with_corners(bottom, top, west, east), "lat", False)
    *seconds, clash = merge_tiles(own, cross)
    seconds = [seconds[0]] + [xor_permute(x, "lon", 2 * c) for c, x in enumerate(seconds) if c > 0]
    initial, coef, keep, give = adjoint_window(
        wet_tiles, control_map, clash, *fields, west, east, south, north, owners
    )
    keep = keep + xor_permute(give, "lon", 1)
    for bit in (2, 1):
        half = keep.shape[0] // 2
        keep = keep[:half] + xor_permute(keep[half:], "lat", bit)
    groups = [
        [row * owners + column for row in (y, y + 4) for column in range(c, owners, 2)]
        for y in range(4)
        for c in range(2)
    ]
    gathered = lax.all_to_all(
        keep, ("lat", "lon"), split_axis=0, concat_axis=0, axis_index_groups=groups, tiled=True
    )
    control, clashes = control_rows(gathered)

    def halos(low, high, bottom, top):
        west, east = neighbours(low, high, "lon", True)
        one, two = with_corners(bottom, top, west, east, paired_kernel)
        bands = lax.axis_size("lat")
        pairs = [[(i, i + 1) for i in range(first, bands - 1, 2)] for first in range(2)]
        one, two = [
            lax.ppermute(x, "lat", pair + [(b, a) for a, b in pair]) for x, pair in zip((one, two), pairs)
        ]
        return west, east, one, two

    state, *strips = unpack_tiles(first, *seconds)
    strips = halos(*strips)
    final = forward_window(state, coef, *strips)

    def complete(carry):
        outgoing = pack_tiles(stored_ids, stored_tiles, carry[0], owners)
        arrived = lax.all_to_all(outgoing, "lon", split_axis=0, concat_axis=0, tiled=True)
        state, *strips = unpack_tiles(arrived.reshape(owners * PAIR, 8, FLAT))
        return forward_window(state, coef, *halos(*strips)), jnp.float32(0)

    final, _ = lax.while_loop(lambda carry: carry[1] > 0, complete, (final, clashes[0]))
    return final.transpose(0, 2, 1, 3), initial.transpose(0, 2, 1, 3), control


def solution(mesh):
    grid = P("lat", "lon")
    return jax.shard_map(
        per_device,
        mesh=mesh,
        in_specs=(
            P(("lat", "lon"), None, None), P(("lat", "lon")), grid, grid, grid, grid, grid, grid, grid,
            P(None, "lat", "lon"), P(None, None, "lat", "lon"),
        ),
        out_specs=(
            P(None, None, "lat", "lon"), P(None, None, "lat", "lon"), P(("lat", "lon"), None, None),
        ),
        check_vma=False,
    )
```

```python
import functools

import jax
import jax.numpy as jnp
from jax import lax
from jax.experimental import pallas as pl
from jax.experimental.pallas import tpu as pltpu
from jax.sharding import PartitionSpec as P


F32 = jnp.float32
I32 = jnp.int32
TILE = 90
SIDE = 3
COLUMNS = 48
HALO = 3
SLOTS = 27
PAIR = 2
LEV = 4
CELLS = TILE * TILE
N = TILE * SIDE
FLAT = 8192
TAIL = 8064
TAG = CELLS - TAIL
TOP = 16
ROWS = 304
LANES = 384
BLOCKS = ((0, 128), (1, 128), (2, N - 256))
CHUNKS = 34
COARSE = 30
VMEM = pl.BlockSpec(memory_space=pltpu.VMEM)
SMEM = pl.BlockSpec(memory_space=pltpu.SMEM)
ANY = pl.BlockSpec(memory_space=pl.ANY)


def aligned(x):
    return pl.multiple_of(x, 8)


def pack_kernel(ids, stored, after, out, held, tail, empty, count, route, in_sem, out_sem, tail_sem, empty_sem):
    owners = out.shape[0]

    def fetch(s):
        return pltpu.make_async_copy(stored.at[s], held.at[s], in_sem.at[s])

    def send(s, owner, rank):
        return pltpu.make_async_copy(
            held.at[s, :, pl.ds(0, TAIL)], out.at[owner, rank, :, pl.ds(0, TAIL)], out_sem.at[s]
        )

    def send_tail(s, owner, rank):
        return pltpu.make_async_copy(
            tail.at[s], out.at[owner, rank, :, pl.ds(TAIL, 128)], tail_sem.at[s]
        )

    def send_empty(owner, rank):
        return pltpu.make_async_copy(
            empty, out.at[owner, rank, :, pl.ds(TAIL, 128)], empty_sem.at[owner, rank]
        )

    @pl.loop(0, SLOTS)
    def _(s):
        @pl.when(ids[s] >= 0)
        def _():
            fetch(s).start()

    @pl.loop(0, owners)
    def _(o):
        count[o] = 0

    empty[...] = jnp.full((8, 128), -1.0, F32)
    lane = lax.broadcasted_iota(I32, (8, 128), 1)

    @pl.loop(0, SLOTS)
    def _(s):
        tile = ids[s]

        @pl.when(tile >= 0)
        def _():
            row = tile // COLUMNS
            column = tile - row * COLUMNS
            owner = column // SIDE
            rank = count[owner]
            count[owner] = rank + 1
            route[s] = owner * PAIR + rank
            place = row * SIDE + column - owner * SIDE
            fetch(s).wait()
            last = jnp.concatenate([held[s, :, TAIL:CELLS], jnp.zeros((8, 128 - TAG), F32)], axis=1)
            tail[s] = jnp.where(lane < TAG, last, place.astype(F32))
            send(s, owner, rank).start()
            send_tail(s, owner, rank).start()

    for rank in range(PAIR):

        @pl.loop(0, owners)
        def _(o):
            @pl.when(count[o] <= rank)
            def _():
                send_empty(o, rank).start()

    @pl.loop(0, SLOTS)
    def _(s):
        @pl.when(ids[s] >= 0)
        def _():
            owner = route[s] // PAIR
            rank = route[s] - owner * PAIR
            send(s, owner, rank).wait()
            send_tail(s, owner, rank).wait()

    for rank in range(PAIR):

        @pl.loop(0, owners)
        def _(o):
            @pl.when(count[o] <= rank)
            def _():
                send_empty(o, rank).wait()


def pack_tiles(ids, stored, after, owners):
    return pl.pallas_call(
        pack_kernel,
        out_shape=jax.ShapeDtypeStruct((owners, PAIR, 8, FLAT), F32),
        in_specs=[SMEM, ANY, ANY],
        out_specs=ANY,
        scratch_shapes=[
            pltpu.VMEM((SLOTS, 8, CELLS), F32),
            pltpu.VMEM((SLOTS, 8, 128), F32),
            pltpu.VMEM((8, 128), F32),
            pltpu.SMEM((owners,), I32),
            pltpu.SMEM((SLOTS,), I32),
            pltpu.SemaphoreType.DMA((SLOTS,)),
            pltpu.SemaphoreType.DMA((SLOTS,)),
            pltpu.SemaphoreType.DMA((SLOTS,)),
            pltpu.SemaphoreType.DMA((owners, PAIR)),
        ],
        name="pack_tiles",
    )(ids, stored, after)


def split_kernel(edges, ids, stored, first, own, cross, held, tail, empty, count, route, filled, in_sem, out_sem, tail_sem, empty_sem):
    owners = first.shape[0]
    chips = own.shape[0]
    me = lax.axis_index("lon")
    outs = [(first, owners), (own, chips), (cross, chips)]

    def fetch(s):
        return pltpu.make_async_copy(stored.at[s], held.at[s], in_sem.at[s])

    def each(s, act):
        for kind, (out, _) in enumerate(outs):

            @pl.when(route[s, 0] == kind)
            def _():
                to = out.at[route[s, 1]]
                act(pltpu.make_async_copy(held.at[s, :, pl.ds(0, TAIL)], to.at[:, pl.ds(0, TAIL)], out_sem.at[s]))
                act(pltpu.make_async_copy(tail.at[s], to.at[:, pl.ds(TAIL, 128)], tail_sem.at[s]))

    def each_empty(act):
        for kind, (out, size) in enumerate(outs):

            @pl.loop(0, size)
            def _(i):
                @pl.when(filled[kind, i] == 0)
                def _():
                    act(
                        pltpu.make_async_copy(
                            empty, out.at[i, :, pl.ds(TAIL, 128)], empty_sem.at[kind, i]
                        )
                    )

    @pl.loop(0, SLOTS)
    def _(s):
        @pl.when(ids[s] >= 0)
        def _():
            fetch(s).start()

    @pl.loop(0, owners)
    def _(o):
        count[o] = 0
        for kind in range(3):
            filled[kind, o] = 0

    edges()
    empty[...] = jnp.full((8, 128), -1.0, F32)
    lane = lax.broadcasted_iota(I32, (8, 128), 1)

    @pl.loop(0, SLOTS)
    def _(s):
        tile = ids[s]

        @pl.when(tile >= 0)
        def _():
            row = tile // COLUMNS
            column = tile - row * COLUMNS
            owner = column // SIDE
            rank = count[owner]
            count[owner] = rank + 1
            away = owner ^ me
            kind = jnp.where(rank == 0, 0, 1 + (away & 1))
            index = jnp.where(rank == 0, owner, away >> 1)
            route[s, 0] = kind
            route[s, 1] = index
            filled[kind, index] = 1
            place = row * SIDE + column - owner * SIDE
            fetch(s).wait()
            last = jnp.concatenate([held[s, :, TAIL:CELLS], jnp.zeros((8, 128 - TAG), F32)], axis=1)
            tail[s] = jnp.where(lane < TAG, last, place.astype(F32))
            each(s, lambda copy: copy.start())

    each_empty(lambda copy: copy.start())

    @pl.loop(0, SLOTS)
    def _(s):
        @pl.when(ids[s] >= 0)
        def _():
            each(s, lambda copy: copy.wait())

    each_empty(lambda copy: copy.wait())


def merge_kernel(own, cross, *refs):
    chips = own.shape[0]
    outs = refs[:chips]
    clash, held, empty, own_tags, cross_tags, sem, in_sem, out_sem = refs[chips:]
    copies = [
        pltpu.make_async_copy(x.at[:, pl.ds(0, 1), pl.ds(TAIL, 128)], tags, sem.at[i])
        for i, (x, tags) in enumerate(((own, own_tags), (cross, cross_tags)))
    ]
    for copy in copies:
        copy.start()
    empty[...] = jnp.full((8, 128), -1.0, F32)
    for copy in copies:
        copy.wait()
    total = jnp.int32(0)
    has = []
    for c in range(chips):
        mine = own_tags[c, 0, TAG] >= 0
        other = cross_tags[c, 0, TAG] >= 0
        total = total + jnp.where(mine & other, 1, 0)
        has.append((mine, other))
    clash[0] = total

    def filling(c, act):
        mine, other = has[c]

        @pl.when(mine)
        def _():
            act(pltpu.make_async_copy(own.at[c], held.at[c], in_sem.at[c]))

        @pl.when(other & ~mine)
        def _():
            act(pltpu.make_async_copy(cross.at[c], held.at[c], in_sem.at[c]))

    def leaving(c, act):
        mine, other = has[c]

        @pl.when(mine | other)
        def _():
            act(pltpu.make_async_copy(held.at[c], outs[c], out_sem.at[c]))

        @pl.when(~(mine | other))
        def _():
            act(pltpu.make_async_copy(empty, outs[c].at[:, pl.ds(TAIL, 128)], out_sem.at[c]))

    for c in range(chips):
        filling(c, lambda copy: copy.start())
    for c in range(chips):
        filling(c, lambda copy: copy.wait())
        leaving(c, lambda copy: copy.start())
    for c in range(chips):
        leaving(c, lambda copy: copy.wait())


def merge_tiles(own, cross):
    chips = own.shape[0]
    return pl.pallas_call(
        merge_kernel,
        out_shape=(jax.ShapeDtypeStruct((8, FLAT), F32),) * chips + (jax.ShapeDtypeStruct((1,), I32),),
        in_specs=[ANY, ANY],
        out_specs=(ANY,) * chips + (SMEM,),
        scratch_shapes=[
            pltpu.VMEM((chips, 8, FLAT), F32),
            pltpu.VMEM((8, 128), F32),
            pltpu.SMEM((chips, 1, 128), F32),
            pltpu.SMEM((chips, 1, 128), F32),
            pltpu.SemaphoreType.DMA((2,)),
            pltpu.SemaphoreType.DMA((chips,)),
            pltpu.SemaphoreType.DMA((chips,)),
        ],
        name="merge_tiles",
        compiler_params=pltpu.CompilerParams(vmem_limit_bytes=67043328),
    )(own, cross)


def strip_columns(load, count, first):
    lane = lax.broadcasted_iota(I32, (N + 2, 128), 1)
    strip = jnp.zeros((N + 2, 128), F32)
    for f in range(count):
        moved = pltpu.roll(load(f), (HALO * f - first) % 128, 1)
        strip = jnp.where((lane >= HALO * f) & (lane < HALO * f + HALO), moved, strip)
    return strip.T[0 : HALO * count]


def wet_field(wet, rows, row0):
    row = lax.broadcasted_iota(I32, (rows, LANES), 0) + row0
    lane = lax.broadcasted_iota(I32, (rows, LANES), 1)
    bands = []
    for r in range(SIDE):
        w = [wet[r, c].astype(F32) for c in range(SIDE)]
        bands.append(jnp.where(lane < TILE, w[0], jnp.where(lane < 2 * TILE, w[1], w[2])))
    return jnp.where(row < TILE, bands[0], jnp.where(row < 2 * TILE, bands[1], bands[2]))


def edges_kernel(wet, zd, zf, md, mf, vm, forcing, adjoint, west, east, south, north, held):
    views = [zd, zf, md, mf, vm]
    full = wet_field(wet, N + 2, 0)
    held[0, 0] = full[:, 0:128]
    held[1, 0] = full[:, 256:384]
    south[0:HALO, 0:N] = full[0:HALO, 0:N]
    north[0:HALO, 0:N] = full[N - HALO : N, 0:N]
    for f in range(1, 6):
        ref = views[f - 1]
        south[HALO * f : HALO * f + HALO, 0:N] = ref[0:HALO, :]
        north[HALO * f : HALO * f + HALO, 0:N] = ref[N - HALO : N, :]
        held[0, f, 0:N, :] = ref[:, 0:128]
        held[1, f, 0:N, 0 : N - 256] = ref[:, 256:N]
    for out, first in ((south, 0), (north, N - HALO)):
        for y in range(HALO):
            row = forcing[first + y]
            for f in range(2):
                out[HALO * (6 + f) + y, 0:N] = row[f]
            for t in range(2):
                row = adjoint[t, first + y]
                for k in range(LEV):
                    out[HALO * (8 + LEV * t + k) + y, 0:N] = row[k]

    def lines(at, start):
        for side, width in ((0, 128), (1, N - 256)):
            lanes = slice(256 * side, 256 * side + width)
            for base, ref, depth in ((6, forcing, 2), (8, adjoint.at[0], LEV), (8 + LEV, adjoint.at[1], LEV)):
                block = jnp.swapaxes(ref[pl.ds(start, 8), :, lanes], 0, 1)
                for k in range(depth):
                    held[side, base + k, at, 0:width] = block[k]

    @pl.loop(0, N // 8)
    def _(g):
        lines(pl.ds(aligned(8 * g), 8), 8 * g)

    lines(slice(N - 8, N), N - 8)

    def low(f):
        return held[0, f]

    def high(f):
        return held[1, f]

    west[...] = strip_columns(low, 16, 0)
    east[...] = strip_columns(high, 16, N - HALO - 256)


def head_kernel(ids, stored, *refs):
    inputs, strips, tiles = refs[:8], refs[8:12], refs[12:15]
    edge_scratch, scratch = refs[15], refs[16:]
    split_kernel(lambda: edges_kernel(*inputs, *strips, edge_scratch), ids, stored, *tiles, *scratch)


def strips_and_tiles(ids, stored, owners, *fields):
    chips = owners // 2
    strip = jax.ShapeDtypeStruct((48, N + 2), F32)
    return pl.pallas_call(
        head_kernel,
        out_shape=(strip,) * 4
        + tuple(jax.ShapeDtypeStruct((n, 8, FLAT), F32) for n in (owners, chips, chips)),
        in_specs=[SMEM, ANY, SMEM] + [VMEM] * 7,
        out_specs=(VMEM,) * 4 + (ANY,) * 3,
        scratch_shapes=[
            pltpu.VMEM((2, 16, N + 2, 128), F32),
            pltpu.VMEM((SLOTS, 8, CELLS), F32),
            pltpu.VMEM((SLOTS, 8, 128), F32),
            pltpu.VMEM((8, 128), F32),
            pltpu.SMEM((owners,), I32),
            pltpu.SMEM((SLOTS, 2), I32),
            pltpu.SMEM((3, owners), I32),
            pltpu.SemaphoreType.DMA((SLOTS,)),
            pltpu.SemaphoreType.DMA((SLOTS,)),
            pltpu.SemaphoreType.DMA((SLOTS,)),
            pltpu.SemaphoreType.DMA((3, owners)),
        ],
        name="strips_and_tiles",
        compiler_params=pltpu.CompilerParams(vmem_limit_bytes=67043328),
    )(ids, stored, *fields)


def corners_kernel(south, north, west, east, to_south, to_north):
    for rows, out, first in ((south, to_south, 0), (north, to_north, N - HALO)):
        out[:, 0:N] = rows[:, 0:N]
        out[:, N : N + HALO] = west[:, first : first + HALO]
        out[:, N + HALO : N + 2 * HALO] = east[:, first : first + HALO]


def paired_kernel(south, north, near, far, one, two):
    even = lax.axis_index("lon") & 1 == 0
    west = jnp.where(even, far[...], near[...])
    east = jnp.where(even, near[...], far[...])
    even = lax.axis_index("lat") & 1 == 0

    @pl.when(even)
    def _():
        corners_kernel(south, north, west, east, two, one)

    @pl.when(jnp.logical_not(even))
    def _():
        corners_kernel(south, north, west, east, one, two)


def with_corners(south, north, west, east, kernel=corners_kernel):
    shape = jax.ShapeDtypeStruct((south.shape[0], LANES), F32)
    return pl.pallas_call(
        kernel,
        out_shape=(shape, shape),
        in_specs=[VMEM] * 4,
        out_specs=(VMEM,) * 2,
        name="row_strips",
    )(south, north, west, east)


def insert_halos(ext, base, count, west, east, south, north):
    blank = jnp.zeros((128 - HALO * count, N + 2), F32)
    from_west = jnp.concatenate([west[...], blank], axis=0).T
    from_east = jnp.concatenate([east[...], blank], axis=0).T
    blank = jnp.zeros((128 - HALO * count, 128), F32)
    low = jnp.concatenate([south[:, 256:384], blank], axis=0).T
    high = jnp.concatenate([north[:, 256:384], blank], axis=0).T
    at = N - 256
    for f in range(count):
        s = slice(HALO * f, HALO * f + HALO)
        field = ext.at[base + f]
        field[2, TOP : TOP + N + 2, 128 - HALO : 128] = from_west[:, s]
        field[2, TOP : TOP + N + 2, at : at + HALO] = from_east[:, s]
        for first, rows, block in ((TOP - HALO, south, low), (TOP + N, north, high)):
            for j, width in BLOCKS:
                field[j, first : first + HALO, 0:width] = rows[s, 128 * j : 128 * j + width]
            field[2, first : first + HALO, 128 - HALO : 128] = block[at : at + HALO, s]
            field[2, first : first + HALO, at : at + HALO] = block[at + HALO : at + 2 * HALO, s]


def from_east(block):
    lane = lax.broadcasted_iota(I32, (8, 128), 1)
    return lambda j: pltpu.roll(jnp.where(lane == 0, block((j + 1) % 3), block(j)), 127, 1)


def from_west(block):
    lane = lax.broadcasted_iota(I32, (8, 128), 1)
    return lambda j: pltpu.roll(jnp.where(lane == 127, block((j + 2) % 3), block(j)), 1, 1)


def stencil(src, b, coef, take):
    rows = pl.ds(b, 8)
    for j in range(3):
        center, east, west, north, south, mix = coef(j)
        for t in range(2):
            fields = [src.at[t * LEV + k] for k in range(LEV)]
            level = [field[j, rows, :] for field in fields]
            flux = [mix * (level[k] - level[k + 1]) for k in range(LEV - 1)]
            result = []
            for k in range(LEV):
                block = lambda i, field=fields[k]: field[i, rows, :]
                new = center * level[k] + east * from_east(block)(j) + west * from_west(block)(j)
                up = fields[k][j, pl.ds(b + 1, 8), :]
                down = fields[k][j, pl.ds(b - 1, 8), :]
                new = new + (north * up + south * down)
                if k > 0:
                    new = new + flux[k - 1]
                if k < LEV - 1:
                    new = new - flux[k]
                result.append(new)
            take(t, j, level, result)


def store_levels(out, t, j, values, i, rows):
    width = BLOCKS[j][1]
    block = jnp.swapaxes(jnp.stack(values), 0, 1)
    out[t, pl.ds(8 * i, rows), :, 128 * j : 128 * j + width] = block[0:rows, :, 0:width]


def adjoint_kernel(
    wet, labels, clash, zd, zf, md, mf, vm, forcing, adjoint, west, east, south, north,
    initial, forward_coef, keep, give,
    ext, other, coef, surface, coarse, piece,
):
    views = [zd, zf, md, mf, vm]
    full = wet_field(wet, N + 2, 0)
    for j, width in BLOCKS:
        ext[0, j, TOP : TOP + N + 2, :] = full[:, 128 * j : 128 * j + 128]
        for f in range(1, 6):
            ext[f, j, TOP : TOP + N, 0:width] = views[f - 1][:, 128 * j : 128 * j + width]

    def lines(at, start):
        for base, ref, depth in ((6, forcing, 2), (8, adjoint.at[0], LEV), (8 + LEV, adjoint.at[1], LEV)):
            block = jnp.swapaxes(ref[pl.ds(start, 8)], 0, 1)
            for k in range(depth):
                for j, width in BLOCKS:
                    ext[base + k, j, at, 0:width] = block[k, :, 128 * j : 128 * j + width]

    @pl.loop(0, N // 8)
    def _(g):
        lines(pl.ds(aligned(TOP + 8 * g), 8), 8 * g)

    lines(slice(TOP + N - 8, TOP + N), N - 8)
    insert_halos(ext, 0, 16, west, east, south, north)

    @pl.loop(1, CHUNKS + 2)
    def _(r):
        b = aligned(r * 8)
        rows = pl.ds(b, 8)
        faces = []
        wets = [ext[0, j, rows, :] for j in range(3)]
        for j in range(3):
            w, z_d, z_f, m_d, m_f, v = [ext[f, j, rows, :] for f in range(6)]
            east_open = w * from_east(wets.__getitem__)(j)
            north_open = w * ext[0, j, pl.ds(b + 1, 8), :]
            de = z_d * east_open
            ue = 0.5 * z_f * east_open
            dn = m_d * north_open
            vn = 0.5 * m_f * north_open
            faces.append((de + ue, ue - de))
            coef[0, j, rows, :] = de + ue
            coef[2, j, rows, :] = dn + vn
            forward_coef[1, j, rows, :] = de - ue
            forward_coef[3, j, rows, :] = dn - vn
            forward_coef[5, j, rows, :] = v * w
            forward_coef[6, j, rows, :] = ext[6, j, rows, :] * w
            forward_coef[7, j, rows, :] = ext[7, j, rows, :] * w
        for j in range(3):
            ea_west = from_west(lambda i: faces[i][0])(j)
            eb_west = from_west(lambda i: faces[i][1])(j)
            na_south = coef[2, j, pl.ds(b - 1, 8), :]
            minus_nb_south = forward_coef[3, j, pl.ds(b - 1, 8), :]
            forward_coef[0, j, rows, :] = 1.0 + (
                (eb_west - faces[j][0]) - (minus_nb_south + coef[2, j, rows, :])
            )
            forward_coef[2, j, rows, :] = ea_west
            forward_coef[4, j, rows, :] = na_south
            coef[1, j, rows, :] = -eb_west
            coef[3, j, rows, :] = minus_nb_south

    def load_coef(b):
        rows = pl.ds(b, 8)
        return lambda j: (
            [forward_coef[0, j, rows, :]]
            + [coef[i, j, rows, :] for i in range(4)]
            + [forward_coef[5, j, rows, :]]
        )

    lam = ext.at[pl.ds(8, 8)]

    def step(src, dst, first):
        @pl.loop(0, CHUNKS // 2 + 1)
        def _(r):
            for u in range(2):
                b = aligned(r * 16 + 8 * u + 8)
                rows = pl.ds(b, 8)

                def take(t, j, old, new):
                    for k in range(LEV):
                        dst[t * LEV + k, j, rows, :] = new[k]
                    surface[t, j, rows, :] = old[0] if first else surface[t, j, rows, :] + old[0]

                stencil(src, b, load_coef(b), take)

    step(lam, other, True)
    step(other, lam, False)

    def finish(i, count):
        b = aligned(TOP + 8 * i)
        rows = pl.ds(b, 8)

        def take(t, j, old, new):
            w = ext[0, j, rows, :]
            store_levels(initial, t, j, [w * value for value in new], i, count)
            surface[t, j, rows, :] = w * (surface[t, j, rows, :] + old[0])

        stencil(lam, b, load_coef(b), take)

    @pl.loop(0, N // 16)
    def _(i):
        finish(2 * i, 8)
        finish(2 * i + 1, 8)

    finish(N // 8 - 1, 8)
    finish(N // 8, N % 8)

    BF = jnp.bfloat16

    def parts(x):
        hi = x.astype(BF)
        rest = x - hi.astype(F32)
        mid = rest.astype(BF)
        return hi, mid, (rest - mid.astype(F32)).astype(BF)

    def band(shape, out_axis):
        i = lax.broadcasted_iota(I32, shape, out_axis) * 3
        j = lax.broadcasted_iota(I32, shape, 1 - out_axis)
        return ((j >= i) & (j < i + 3) & (j < N)).astype(F32).astype(BF)

    by_row = band((96, N + 2), 0)
    by_lane = band((LANES, 128), 1)
    shape = (N + 2, 128)
    for t in range(2):
        full = jnp.zeros((96, 128), F32)
        for j, width in BLOCKS:
            inside = (lax.broadcasted_iota(I32, shape, 0) < N) & (
                lax.broadcasted_iota(I32, shape, 1) < width
            )
            cells = jnp.where(inside, surface[t, j, TOP : TOP + N + 2, :], 0.0)
            half = sum(jnp.dot(by_row, p, preferred_element_type=F32) for p in parts(cells))
            for p in parts(half):
                full += jnp.dot(p, by_lane[128 * j : 128 * j + 128], preferred_element_type=F32)
        coarse[t] = full / 9.0
    chips = keep.shape[0] // 8
    owners = 2 * chips
    here = lax.axis_index("lat")
    me = lax.axis_index("lon")
    last = lax.broadcasted_iota(I32, (16, 128), 0) == 15
    piece[...] = jnp.where(last, clash[0].astype(F32), 0.0)
    keep[...] = jnp.broadcast_to(piece[...], keep.shape)
    give[...] = jnp.broadcast_to(piece[...], give.shape)
    part = COARSE // 2
    for r in range(SIDE):
        for c in range(SIDE):
            for t in range(2):
                for h in range(2):
                    at = COARSE * r + part * h
                    lane = 64 * h + COARSE * t
                    piece[0:part, lane : lane + COARSE] = coarse[
                        t, at : at + part, COARSE * c : COARSE * c + COARSE
                    ]
            label = labels[r, c]
            row = label // owners
            away = row ^ here
            column = label - row * owners
            at = ((away & 2) * 2 + (away & 1) * 2 + (row >> 2)) * chips + (column >> 1)
            other = (column ^ me) & 1

            @pl.when(other == 0)
            def _():
                keep[at] = piece[...]

            @pl.when(other != 0)
            def _():
                give[at] = piece[...]


def adjoint_window(wet, labels, clash, zd, zf, md, mf, vm, forcing, adjoint, west, east, south, north, owners):
    return pl.pallas_call(
        adjoint_kernel,
        out_shape=(
            jax.ShapeDtypeStruct((2, N, LEV, N), F32),
            jax.ShapeDtypeStruct((8, 3, ROWS, 128), F32),
            jax.ShapeDtypeStruct((4 * owners, 16, 128), F32),
            jax.ShapeDtypeStruct((4 * owners, 16, 128), F32),
        ),
        in_specs=[SMEM] * 3 + [VMEM] * 11,
        out_specs=(VMEM,) * 4,
        scratch_shapes=[
            pltpu.VMEM((16, 3, ROWS, 128), F32),
            pltpu.VMEM((8, 3, ROWS, 128), F32),
            pltpu.VMEM((4, 3, ROWS, 128), F32),
            pltpu.VMEM((2, 3, ROWS, 128), F32),
            pltpu.VMEM((2, 96, 128), F32),
            pltpu.VMEM((16, 128), F32),
        ],
        name="adjoint_window",
    )(wet, labels, clash, zd, zf, md, mf, vm, forcing, adjoint, west, east, south, north)


def unpack_kernel(extra, first, *refs):
    seconds = refs[:extra]
    state, west, east, south, north, tags, more_tags, present, tiles, lined, tag_sem, tile_sem = refs[extra:]
    slots = first.shape[0]
    copies = [pltpu.make_async_copy(first.at[:, pl.ds(0, 1), pl.ds(TAIL, 128)], tags, tag_sem.at[0])]
    for c, second in enumerate(seconds):
        copies.append(
            pltpu.make_async_copy(second.at[pl.ds(0, 1), pl.ds(TAIL, 128)], more_tags.at[c], tag_sem.at[1 + c])
        )
    for copy in copies:
        copy.start()
    places = SIDE * SIDE

    @pl.loop(0, places)
    def _(p):
        present[p] = 0

    for copy in copies:
        copy.wait()

    def fetch(source, p):
        return pltpu.make_async_copy(source, tiles.at[p], tile_sem.at[p])

    def take(source, tag):
        place = tag.astype(I32)

        @pl.when(place >= 0)
        def _():
            present[place] = 1
            fetch(source, place).start()

    @pl.loop(0, slots)
    def _(i):
        take(first.at[i], tags[i, 0, TAG])

    for c, second in enumerate(seconds):
        take(second, more_tags[c, 0, TAG])

    @pl.loop(0, places)
    def _(p):
        @pl.when(present[p] == 0)
        def _():
            tiles[p] = jnp.zeros((8, FLAT), F32)

    @pl.loop(0, SIDE)
    def _(r):
        for c in range(SIDE):

            @pl.when(present[r * SIDE + c] != 0)
            def _():
                fetch(first.at[0], r * SIDE + c).wait()

        for y in range(TILE):
            for c in range(SIDE):
                lined[r * TILE + y, :, TILE * c : TILE * c + TILE] = tiles[
                    r * SIDE + c, :, TILE * y : TILE * y + TILE
                ]

    @pl.loop(0, CHUNKS)
    def _(g):
        block = jnp.swapaxes(lined[pl.ds(8 * g, 8)], 0, 1)
        for j in range(3):
            state[:, j, pl.ds(aligned(TOP + 8 * g), 8), :] = block[:, :, 128 * j : 128 * j + 128]

    even = lax.axis_index("lon") & 1 == 0
    low = strip_columns(lambda f: state[f, 0, TOP : TOP + N + 2, :], 8, 0)
    high = strip_columns(lambda f: state[f, 2, TOP : TOP + N + 2, :], 8, N - HALO - 256)
    west[...] = jnp.where(even, high, low)
    east[...] = jnp.where(even, low, high)
    for f in range(8):
        for j, width in BLOCKS:
            lanes = slice(128 * j, 128 * j + width)
            rows = slice(HALO * f, HALO * f + HALO)
            south[rows, lanes] = state[f, j, TOP : TOP + HALO, 0:width]
            north[rows, lanes] = state[f, j, TOP + N - HALO : TOP + N, 0:width]


def unpack_tiles(first, *seconds):
    strip = jax.ShapeDtypeStruct((24, N + 2), F32)
    extra = len(seconds)
    return pl.pallas_call(
        functools.partial(unpack_kernel, extra),
        out_shape=(jax.ShapeDtypeStruct((8, 3, ROWS, 128), F32),) + (strip,) * 4,
        in_specs=[ANY] * (1 + extra),
        out_specs=(VMEM,) * 5,
        scratch_shapes=[
            pltpu.SMEM((first.shape[0], 1, 128), F32),
            pltpu.SMEM((8, 1, 128), F32),
            pltpu.SMEM((SIDE * SIDE,), I32),
            pltpu.VMEM((SIDE * SIDE, 8, FLAT), F32),
            pltpu.VMEM((8 * CHUNKS, 8, LANES), F32),
            pltpu.SemaphoreType.DMA((9,)),
            pltpu.SemaphoreType.DMA((SIDE * SIDE,)),
        ],
        name="unpack_tiles",
        compiler_params=pltpu.CompilerParams(vmem_limit_bytes=67043328),
    )(first, *seconds)


def forward_kernel(
    state, factors, near, far, one, two, out, first, second, coef, final, south, north, west, east, sem, out_sem
):
    even = lax.axis_index("lon") & 1 == 0
    west[...] = jnp.where(even, far[...], near[...])
    east[...] = jnp.where(even, near[...], far[...])
    even = lax.axis_index("lat") & 1 == 0
    south[...] = jnp.where(even, two[...], one[...])
    north[...] = jnp.where(even, one[...], two[...])
    copies = [
        pltpu.make_async_copy(state, first, sem.at[0]), pltpu.make_async_copy(factors, coef, sem.at[1])
    ]
    for copy in copies:
        copy.start()
    copies[0].wait()
    insert_halos(first, 0, 8, west, east, south, north)
    copies[1].wait()

    def load_coef(b):
        rows = pl.ds(b, 8)
        return lambda j: [coef[i, j, rows, :] for i in range(6)]

    def step(src, dst):
        @pl.loop(0, CHUNKS // 2 + 1)
        def _(r):
            for u in range(2):
                b = aligned(r * 16 + 8 * u + 8)
                rows = pl.ds(b, 8)

                def take(t, j, old, new):
                    dst[t * LEV, j, rows, :] = new[0] + coef[6 + t, j, rows, :]
                    for k in range(1, LEV):
                        dst[t * LEV + k, j, rows, :] = new[k]

                stencil(src, b, load_coef(b), take)

    step(first, second)
    step(second, first)

    def finish(i, count):
        b = aligned(TOP + 8 * i)

        def take(t, j, old, new):
            top = new[0] + coef[6 + t, j, pl.ds(b, 8), :]
            store_levels(final, t, j, [top] + new[1:], i, count)

        stencil(first, b, load_coef(b), take)

    cuts = (0, 96, 192, N)
    copies = []
    for part, (low, high) in enumerate(zip(cuts, cuts[1:])):
        pairs = high // 16 - low // 16

        @pl.loop(0, pairs)
        def _(i):
            finish(low // 8 + 2 * i, 8)
            finish(low // 8 + 2 * i + 1, 8)

        if high == N:
            finish(N // 8 - 1, 8)
            finish(N // 8, N % 8)
        rows = pl.ds(low, high - low)
        copies.append(pltpu.make_async_copy(final.at[:, rows], out.at[:, rows], out_sem.at[part]))
        copies[-1].start()
    for copy in copies:
        copy.wait()


def forward_window(state, coef, west, east, one, two):
    shape = (2, N, LEV, N)
    return pl.pallas_call(
        forward_kernel,
        out_shape=jax.ShapeDtypeStruct(shape, F32),
        in_specs=[ANY] * 2 + [VMEM] * 4,
        out_specs=ANY,
        scratch_shapes=[
            pltpu.VMEM((8, 3, ROWS, 128), F32),
            pltpu.VMEM((8, 3, ROWS, 128), F32),
            pltpu.VMEM((8, 3, ROWS, 128), F32),
            pltpu.VMEM(shape, F32),
            pltpu.VMEM((24, LANES), F32),
            pltpu.VMEM((24, LANES), F32),
            pltpu.VMEM((24, N + 2), F32),
            pltpu.VMEM((24, N + 2), F32),
            pltpu.SemaphoreType.DMA((2,)),
            pltpu.SemaphoreType.DMA((3,)),
        ],
        name="forward_window",
        compiler_params=pltpu.CompilerParams(vmem_limit_bytes=67043328),
    )(state, coef, west, east, one, two)


def control_kernel(gathered, control, clash):
    total = jnp.sum(gathered[...], axis=0)
    part = COARSE // 2
    for i in range(part):
        for h in range(2):
            for t in range(2):
                at = part * COARSE * h + COARSE * i
                lane = 64 * h + COARSE * t
                control[0, t : t + 1, at : at + COARSE] = total[i : i + 1, lane : lane + COARSE]
    clash[0] = jnp.max(total[15:16])


def control_rows(gathered):
    return pl.pallas_call(
        control_kernel,
        out_shape=(
            jax.ShapeDtypeStruct((1, 2, COARSE * COARSE), F32), jax.ShapeDtypeStruct((1,), F32)
        ),
        in_specs=[VMEM],
        out_specs=(VMEM, SMEM),
        name="control_rows",
    )(gathered)


def neighbours(low, high, axis, periodic):
    count = lax.axis_size(axis)
    up = [(i, i + 1) for i in range(count - 1)] + ([(count - 1, 0)] if periodic else [])
    down = [(b, a) for a, b in up]
    return lax.ppermute(high, axis, up), lax.ppermute(low, axis, down)


def xor_permute(x, axis, bits):
    return lax.ppermute(x, axis, [(i, i ^ bits) for i in range(lax.axis_size(axis))])


def per_device(
    stored_tiles, stored_ids, wet_tiles, control_map, zonal_diffusivity, meridional_diffusivity,
    zonal_flow, meridional_flow, vertical_mixing, forcing, final_adjoint,
):
    owners = lax.axis_size("lon")
    fields = (
        zonal_diffusivity, zonal_flow, meridional_diffusivity, meridional_flow, vertical_mixing,
        forcing.transpose(1, 0, 2), final_adjoint.transpose(0, 2, 1, 3),
    )
    low, high, bottom, top, first, own, cross = strips_and_tiles(
        stored_ids, stored_tiles, owners, wet_tiles, *fields
    )
    west, east = neighbours(low, high, "lon", True)
    first = lax.all_to_all(first, "lon", split_axis=0, concat_axis=0, tiled=True)
    cross = xor_permute(cross, "lon", 1)
    south, north = neighbours(*with_corners(bottom, top, west, east), "lat", False)
    *seconds, clash = merge_tiles(own, cross)
    seconds = [seconds[0]] + [xor_permute(x, "lon", 2 * c) for c, x in enumerate(seconds) if c > 0]
    initial, coef, keep, give = adjoint_window(wet_tiles, control_map, clash, *fields, west, east, south, north, owners)
    keep = keep + xor_permute(give, "lon", 1)
    for bit in (2, 1):
        half = keep.shape[0] // 2
        keep = keep[:half] + xor_permute(keep[half:], "lat", bit)
    groups = [
        [row * owners + column for row in (y, y + 4) for column in range(c, owners, 2)]
        for y in range(4)
        for c in range(2)
    ]
    gathered = lax.all_to_all(keep, ("lat", "lon"), split_axis=0, concat_axis=0, axis_index_groups=groups, tiled=True)
    control, clashes = control_rows(gathered)

    def halos(low, high, bottom, top):
        owners = lax.axis_size("lon")
        pairs = [[(i, (i + 1) % owners) for i in range(first, owners, 2)] for first in range(2)]
        west, east = [
            lax.ppermute(x, "lon", pair + [(b, a) for a, b in pair]) for x, pair in zip((low, high), pairs)
        ]
        one, two = with_corners(bottom, top, west, east, paired_kernel)
        bands = lax.axis_size("lat")
        pairs = [[(i, i + 1) for i in range(first, bands - 1, 2)] for first in range(2)]
        one, two = [
            lax.ppermute(x, "lat", pair + [(b, a) for a, b in pair]) for x, pair in zip((one, two), pairs)
        ]
        return west, east, one, two

    state, *strips = unpack_tiles(first, *seconds)
    strips = halos(*strips)
    final = forward_window(state, coef, *strips)

    def complete(carry):
        outgoing = pack_tiles(stored_ids, stored_tiles, carry[0], owners)
        arrived = lax.all_to_all(outgoing, "lon", split_axis=0, concat_axis=0, tiled=True)
        state, *strips = unpack_tiles(arrived.reshape(owners * PAIR, 8, FLAT))
        return forward_window(state, coef, *halos(*strips)), jnp.float32(0)

    final, _ = lax.while_loop(lambda carry: carry[1] > 0, complete, (final, clashes[0]))
    return final.transpose(0, 2, 1, 3), initial.transpose(0, 2, 1, 3), control


def solution(mesh):
    grid = P("lat", "lon")
    return jax.shard_map(
        per_device,
        mesh=mesh,
        in_specs=(
            P(("lat", "lon"), None, None), P(("lat", "lon")), grid, grid, grid, grid, grid, grid, grid,
            P(None, "lat", "lon"), P(None, None, "lat", "lon"),
        ),
        out_specs=(
            P(None, None, "lat", "lon"), P(None, None, "lat", "lon"), P(("lat", "lon"), None, None),
        ),
        check_vma=False,
    )
```
